128 devices in a mesh: tm: 4 (over z), cell: 32 (over x, y, core).
Axes of the slice: x: 4, y: 4, z: 4, core: 2. Of those that a mesh axis runs over, the one named last changes fastest.
Arguments:
- cheb_coef: float32 [4, 3, 17, 12288], P('tm', None, None, 'cell'), may hold values from -18 to 18
- obj_cell: int32 [4, 12288, 1], P('tm', 'cell'), may hold values from 0 to 31; in each aligned block of 384 rows (0 to 383, 384 to 767, ..., all dimensions but the last counted through in order) at most 24 rows name the same one
Outputs:
- min_dist_sq: float32 [4, 24576], P('tm', 'cell')
The draws below stay inside these ranges and needn't reach their ends.
Inputs may be any that keep to these rules, and one draw needn't show every extreme that they name: `obj_cell`: in each subwindow, of the 384 objects of one device (aligned blocks along the objects), at most 24 lie in one cell, and some cell holds exactly 24 of them.
All inputs are finite; a program needn't handle non-finite values.
Results may differ from the reference program's by a relative error of at most 0.0003.
Values sent between devices are 32-bit elements; how exact they have to be, the bound alone decides.
No kernel may reach another device: no remote copies, remote signals or barrier semaphores. Data moves between devices by JAX's collectives and lax.ppermute only.
A program may use at most 128 MiB of HBM per device.

```python
import math
from functools import reduce
import jax
import jax.numpy as jnp
import numpy as np
from jax import lax

DEG1 = 17
SAMP = 64
RIM = 8
OBJ_DEV = 384
OBJECTS = 12288
CAP = 24
SLOTS = 768
N_TM = 4
N_CELL = 32


def level_of(rng, shape, pieces, low, top_value):
    gain, own = 1.0, jax.random.fold_in(rng, 6)
    for position, shards_of in pieces:
        draws = jnp.exp(jax.random.uniform(jax.random.fold_in(own, position), (shards_of,), jnp.float32, low / len(pieces), top_value / len(pieces)))
        gain = gain * jnp.repeat(draws, shape[position] // shards_of).reshape([-1 if axis == position else 1 for axis in range(len(shape))])
    return gain


def shared_out(rng, own, number, rows, number_of, top, limit, lean):
    sequence = jax.random.permutation(rng, number_of)
    packed, usual = load_shares(number_of, rows * top, limit, lean, True), load_shares(number_of, rows * top, limit, lean, False)
    places = jnp.arange(number_of)

    def named(sizes, turn):
        used = int((sizes > 0).sum())
        fixed = max(1, used // 4)
        moved = fixed + (places - fixed + turn * (used - fixed)) % max(1, number_of - fixed)
        return jnp.zeros((number_of,), jnp.int32).at[sequence[jnp.where(places < fixed, places, moved)]].set(jnp.asarray(sizes, jnp.int32))

    sizes = jnp.where(number % 4 == 0, named(packed, number // 4), named(usual, number - number // 4 - 1))
    mixed = jax.random.permutation(jax.random.fold_in(own, 3), number_of)
    source_of, receiver = mixed[0:number_of // 2 * 2:2], mixed[1:number_of // 2 * 2:2]
    room = jnp.minimum(sizes[source_of] - 1, limit - sizes[receiver]) // 2
    room = jnp.where((source_of == sequence[0]) | (receiver == sequence[0]) | (sizes[receiver] == 0), 0, jnp.maximum(room, 0))
    moved = jax.random.randint(jax.random.fold_in(own, 4), (number_of // 2,), 0, 1 << 20) % (room + 1)
    sizes = sizes.at[source_of].add(-moved).at[receiver].add(moved)
    items = jnp.searchsorted(jnp.cumsum(sizes), jnp.arange(rows * top), side="right").astype(jnp.int32)
    table = items.reshape(top, rows).T
    table = table[jax.random.permutation(jax.random.fold_in(own, 1), rows)]
    turn = jax.random.randint(jax.random.fold_in(own, 2), (rows, 1), 0, top)
    return jnp.take_along_axis(table, (jnp.arange(top)[None, :] + turn) % top, axis=1)


def load_shares(count, total, bound, slope, full):
    weights = [(1 << 20) // math.isqrt(grade ** slope) + 1 for grade in range(1, count + 1)]
    largest = bound if full else min(bound, max(-(-total // count), total * weights[0] // sum(weights)))
    least = 1 if total - largest >= count - 1 else 0
    given, surplus = [largest] + [least] * (count - 1), total - largest - least * (count - 1)
    while surplus > 0:
        movable = [i for i in range(1, count) if given[i] < largest] or [i for i in range(1, count) if given[i] < bound]
        mass, left = sum([weights[i] for i in movable]), surplus
        for i in movable:
            more = min(bound - given[i], max(1, left * weights[i] // mass), surplus)
            given[i] = given[i] + more
            surplus = surplus - more
    return np.array(given)


def bell_draw(rng, extent, width, limit, shards=(), held_as=jnp.bfloat16):
    array = jax.random.normal(rng, extent, jnp.float32) * width
    if len(shards) > 0:
        array = level_of(rng, extent, shards, -0.22, 0.18) * array
    return jnp.clip(array, min=-limit, max=limit).astype(held_as)


def setup_inputs(seed: int = 0) -> dict:
    key_of = jax.random.split(jax.random.key(seed), 3)
    cheb_coef = bell_draw(key_of[0], (N_TM, 3, DEG1, OBJECTS), 3.0, 18.0, ((0, 4), (3, 32)), jnp.float32)
    obj_cell_keys = jax.random.split(jax.random.fold_in(key_of[1], 1), N_TM * OBJECTS // OBJ_DEV)
    obj_cell_turns = jax.random.permutation(jax.random.fold_in(key_of[1], 3), N_TM * OBJECTS // OBJ_DEV)
    obj_cell = jax.vmap(lambda own, number: shared_out(jax.random.fold_in(key_of[1], 2), own, number, OBJ_DEV, N_CELL, 1, CAP, 2))(obj_cell_keys, obj_cell_turns).reshape((N_TM, OBJECTS, 1))
    return dict(cheb_coef=cheb_coef, obj_cell=obj_cell)


clip_level = 25.0


def cheb_table(count, degree_plus):
    sample_nodes = (2.0 * jnp.arange(count, dtype=jnp.float32) + 1.0) / count - 1.0
    columns = [jnp.ones_like(sample_nodes), sample_nodes]
    for order in range(2, degree_plus):
        columns.append(2.0 * sample_nodes * columns[-1] - columns[-2])
    return jnp.stack(columns[:degree_plus], axis=1)


def synthesize(coef_three, table):
    return jnp.einsum("sk,ckn->csn", table, coef_three, precision=lax.Precision.HIGHEST)


def slot_ranks(cell_ids):
    positions = jnp.arange(cell_ids.shape[0], dtype=jnp.int32)
    same_cell = cell_ids[:, None] == cell_ids[None, :]
    earlier = positions[None, :] < positions[:, None]
    return jnp.sum((same_cell & earlier).astype(jnp.int32), axis=1).astype(jnp.int32)


def screen(left_pos, left_alive, right_pos, right_alive, skip_self):
    total_rows = left_pos.shape[2]
    total_cols = right_pos.shape[2]
    block_rows = min(256, total_rows)

    def one_block(block_num):
        start = block_num * block_rows
        left_block = lax.dynamic_slice_in_dim(left_pos, start, block_rows, 2)
        left_live = lax.dynamic_slice_in_dim(left_alive, start, block_rows, 0)
        row_ids = start + jnp.arange(block_rows, dtype=jnp.int32)
        row_parts = []
        col_parts = []
        for col_start in range(0, total_cols, block_rows):
            right_block = right_pos[:, :, col_start:col_start + block_rows]
            dist_sq = jnp.min(jnp.sum(jnp.square(left_block[:, :, :, None] - right_block[:, :, None, :]), axis=0), axis=0)
            usable = left_live[:, None] & right_alive[None, col_start:col_start + block_rows]
            if skip_self:
                col_ids = col_start + jnp.arange(block_rows, dtype=jnp.int32)
                usable = usable & (row_ids[:, None] != col_ids[None, :])
            dist_sq = jnp.where(usable, dist_sq, clip_level)
            row_parts.append(jnp.min(dist_sq, axis=1))
            col_parts.append(jnp.min(dist_sq, axis=0))
        return reduce(jnp.minimum, row_parts), jnp.concatenate(col_parts)

    row_mins, col_mins = lax.map(one_block, jnp.arange(total_rows // block_rows, dtype=jnp.int32))
    return row_mins.reshape(total_rows), jnp.min(col_mins, axis=0)


def reference(cheb_coef, obj_cell):
    table = cheb_table(SAMP, DEG1)
    outputs = []
    earlier_samples = None
    for window in range(N_TM):
        samples = synthesize(cheb_coef[window], table)
        if window == 0:
            rim_part = samples[:, :RIM]
        else:
            rim_part = earlier_samples[:, SAMP - RIM:]
        earlier_samples = samples
        extended = jnp.concatenate([rim_part, samples], axis=1)
        cell_ids = obj_cell[window, :, 0].reshape(N_CELL, OBJ_DEV).astype(jnp.int32)
        ranks = jax.vmap(slot_ranks)(cell_ids)
        sources = jnp.arange(N_CELL, dtype=jnp.int32)[:, None]
        targets = (cell_ids * SLOTS + sources * CAP + ranks).reshape(-1).astype(jnp.int32)
        placed = jnp.zeros((3, SAMP + RIM, N_CELL * SLOTS), jnp.float32).at[:, :, targets].set(extended)
        alive = jnp.zeros((N_CELL * SLOTS,), jnp.int32).at[targets].set(1) > 0
        per_cell = placed.reshape(3, SAMP + RIM, N_CELL, SLOTS).transpose(2, 0, 1, 3)
        alive_cells = alive.reshape(N_CELL, SLOTS)

        def per_owner(owner):
            follower = (owner + 1) % N_CELL
            self_rows, unused = screen(per_cell[owner], alive_cells[owner], per_cell[owner], alive_cells[owner], True)
            cross_rows, cross_cols = screen(per_cell[owner], alive_cells[owner], per_cell[follower], alive_cells[follower], False)
            return self_rows, cross_rows, cross_cols

        self_rows, cross_rows, cross_cols = lax.map(per_owner, jnp.arange(N_CELL, dtype=jnp.int32))
        prev_rows = jnp.roll(cross_cols, 1, axis=0)
        result = jnp.minimum(jnp.minimum(self_rows, cross_rows), prev_rows)
        outputs.append(jnp.minimum(result, clip_level).reshape(-1))
    return jnp.stack(outputs)
```

```python
import functools

import jax
import jax.numpy as jnp
import ml_dtypes
import numpy as np
from jax import lax
from jax.experimental import pallas as pl
from jax.experimental.pallas import tpu as pltpu
from jax.sharding import PartitionSpec as P

DEG1 = 17
SAMP = 64
RIM = 8
CAP = 24
EXT = SAMP + RIM
CLIP = 25.0
FAR = 1.0e9

LANES = 128
RIM_AT = 72
FLAG_AT = 96

PIECES = 32
GROUP = LANES // PIECES
CHUNK = 24
SRC = 256
COLS = 256
UNROLL = 3


def cheb_table():
    nodes = ((2.0 * np.arange(SAMP, dtype=np.float32) + 1.0) / SAMP - 1.0).astype(np.float32)
    columns = [np.ones_like(nodes), nodes]
    for _ in range(2, DEG1):
        columns.append((2.0 * nodes * columns[-1] - columns[-2]).astype(np.float32))
    return np.stack(columns, axis=1)


def rim_tables():
    table = cheb_table()
    return np.stack([table[:RIM], table[SAMP - RIM :]])


def synth_matrix():
    table = cheb_table()
    weights = np.zeros((3 * EXT, LANES), np.float32)
    for c in range(3):
        for s in range(RIM):
            weights[c * EXT + s, RIM_AT + RIM * c + s] = 1.0
        weights[c * EXT + RIM : (c + 1) * EXT, 24 * c : 24 * c + DEG1] = table
    return weights


def selection(left):
    hi, mid, norm, one = 0, 3, 6, 9
    uses = []
    for c in range(3):
        for l, r in ((hi, hi), (hi, mid), (mid, hi), (mid, mid)):
            uses.append((l + c, 1.0) if left else (r + c, -2.0))
    for p in range(3):
        uses.append((norm + p, 1.0) if left else (one, 1.0))
    for p in range(3):
        uses.append((one, 1.0) if left else (norm + p, 1.0))
    matrix = np.zeros((CHUNK * PIECES, SRC), np.float32)
    for t in range(CHUNK):
        for k, (kind, value) in enumerate(uses):
            matrix[t * PIECES + k, kind * CHUNK + (0 if kind == one else t)] = value
    return matrix.astype(ml_dtypes.bfloat16)


def as_piece(value):
    return value.astype(jnp.bfloat16).astype(jnp.float32)


def front_kernel(first_ref, own_ref, prev_ref, cell_ref, table_ref, out_ref, rows_ref):
    count = own_ref.shape[2]
    first = first_ref[0] == 0
    rows_ref[...] = jnp.zeros_like(rows_ref)
    table = jnp.where(first, table_ref[0], table_ref[1])
    for c in range(3):
        own = own_ref[c]
        rows_ref[24 * c : 24 * c + DEG1, :] = own
        source = jnp.where(first, own, prev_ref[c])
        rows_ref[RIM_AT + RIM * c : RIM_AT + RIM * (c + 1), :] = jnp.dot(
            table, source, precision=lax.Precision.HIGHEST, preferred_element_type=jnp.float32
        )
    rows_ref[FLAG_AT : FLAG_AT + 1, :] = jnp.ones((1, count), jnp.float32)
    cell = cell_ref[...].astype(jnp.float32)
    column = jnp.transpose(jnp.broadcast_to(cell, (LANES, count)))
    column = jnp.concatenate([column] * (count // LANES), axis=1)
    before = lax.broadcasted_iota(jnp.int32, (count, count), 0) < lax.broadcasted_iota(jnp.int32, (count, count), 1)
    same = (column == jnp.broadcast_to(cell, (count, count))) & before
    rank = jnp.sum(jnp.where(same, 1.0, 0.0), axis=0, keepdims=True)
    slot = (cell * CAP + rank).astype(jnp.int32)
    slots = out_ref.shape[0]
    chosen = lax.broadcasted_iota(jnp.int32, (slots, count), 0) == jnp.broadcast_to(slot, (slots, count))
    chosen = jnp.where(chosen, 1.0, 0.0).astype(jnp.bfloat16)
    data = jnp.transpose(rows_ref[...])
    total = None
    for _ in range(3):
        piece = data.astype(jnp.bfloat16)
        data = data - piece.astype(jnp.float32)
        term = jnp.dot(chosen, piece, preferred_element_type=jnp.float32)
        total = term if total is None else total + term
    out_ref[...] = total


def operands(packed_ref, synth_ref, right_sel_ref, right_ref, left_sel_ref=None, left_ref=None):
    count = packed_ref.shape[0]
    packed = jnp.transpose(packed_ref[...])
    flag = packed[FLAG_AT : FLAG_AT + 1, :] > 0.5
    track = jnp.dot(synth_ref[...], packed, precision=lax.Precision.HIGHEST, preferred_element_type=jnp.float32)
    axes = [track[c * EXT : (c + 1) * EXT] for c in range(3)]
    hi = [as_piece(a) for a in axes]
    mid = [as_piece(a - h) for a, h in zip(axes, hi)]
    held = [h + m for h, m in zip(hi, mid)]
    norm = held[0] * held[0] + held[1] * held[1] + held[2] * held[2]
    norm = jnp.where(jnp.broadcast_to(flag, norm.shape), norm, FAR)
    norms = []
    for _ in range(3):
        piece = as_piece(norm)
        norm = norm - piece
        norms.append(piece)
    ones = jnp.ones((8, count), jnp.float32)
    zeros = jnp.zeros((SRC - 9 * CHUNK - 8, count), jnp.float32)
    for n in range(EXT // CHUNK):
        rows = slice(n * CHUNK, (n + 1) * CHUNK)
        source = jnp.concatenate([a[rows] for a in hi + mid + norms] + [ones, zeros], axis=0)
        right = jnp.dot(right_sel_ref[...], source.astype(jnp.bfloat16), preferred_element_type=jnp.float32)
        right = right.astype(jnp.bfloat16)
        for t in range(CHUNK):
            right_ref[n * CHUNK + t] = right[t * PIECES : (t + 1) * PIECES]
        if left_ref is not None:
            flipped = jnp.transpose(source).astype(jnp.bfloat16)
            for g in range(CHUNK // GROUP):
                block = jnp.dot(
                    flipped, left_sel_ref[:, g * LANES : (g + 1) * LANES], preferred_element_type=jnp.float32
                )
                left_ref[n * (CHUNK // GROUP) + g] = block.astype(jnp.bfloat16)


def tile_min(left_ref, right_ref, acc_ref, rows, col_start):
    groups = left_ref.shape[0]
    acc_ref[0:rows, :] = jnp.full((rows, COLS), CLIP, jnp.float32)

    def step(it, carry):
        best = acc_ref[0:rows, :]
        for u in range(UNROLL):
            g = it * UNROLL + u
            left = left_ref[g, 0:rows, :]
            for j in range(GROUP):
                block = right_ref[g * GROUP + j, :, pl.ds(col_start, COLS)]
                parts = [block]
                if j > 0:
                    parts = [jnp.zeros((PIECES * j, COLS), jnp.bfloat16)] + parts
                if j < GROUP - 1:
                    parts = parts + [jnp.zeros((PIECES * (GROUP - 1 - j), COLS), jnp.bfloat16)]
                weights = jnp.concatenate(parts, axis=0)
                best = jnp.minimum(best, jnp.dot(left, weights, preferred_element_type=jnp.float32))
        acc_ref[0:rows, :] = best
        return carry

    lax.fori_loop(0, groups // UNROLL, step, 0)


def fold(acc_ref, row_ref, rows):
    acc = acc_ref[0:rows, :]
    half = jnp.minimum(acc[:, :LANES], acc[:, LANES:])
    row_ref[0:rows, :] = jnp.minimum(row_ref[0:rows, :], half)
    return jnp.min(acc, axis=0, keepdims=True)


def self_kernel(packed_ref, synth_ref, left_sel_ref, right_sel_ref, out_ref, left_ref, right_ref, acc_ref, row_ref):
    count = packed_ref.shape[0]
    operands(packed_ref, synth_ref, right_sel_ref, right_ref, left_sel_ref, left_ref)
    row_ref[...] = jnp.full_like(row_ref, CLIP)
    parts = []
    for n in range(count // COLS):
        rows = (n + 1) * COLS
        tile_min(left_ref, right_ref, acc_ref, rows, n * COLS)
        near = acc_ref[rows - COLS : rows, :]
        same = lax.broadcasted_iota(jnp.int32, (COLS, COLS), 0) == lax.broadcasted_iota(jnp.int32, (COLS, COLS), 1)
        acc_ref[rows - COLS : rows, :] = jnp.where(same, CLIP, near)
        parts.append(fold(acc_ref, row_ref, rows))
    by_row = jnp.min(jnp.transpose(row_ref[...]), axis=0, keepdims=True)
    out_ref[...] = jnp.minimum(jnp.concatenate(parts, axis=1), by_row)


def cross_kernel(left_ref, packed_ref, synth_ref, right_sel_ref, row_out_ref, col_out_ref, right_ref, acc_ref, row_ref):
    count = packed_ref.shape[0]
    operands(packed_ref, synth_ref, right_sel_ref, right_ref)
    row_ref[...] = jnp.full_like(row_ref, CLIP)

    def column(n, carry):
        start = pl.multiple_of(n * COLS, COLS)
        tile_min(left_ref, right_ref, acc_ref, count, start)
        col_out_ref[:, pl.ds(start, COLS)] = fold(acc_ref, row_ref, count)
        return carry

    lax.fori_loop(0, count // COLS, column, 0)
    row_out_ref[...] = jnp.min(jnp.transpose(row_ref[...]), axis=0, keepdims=True)


VMEM = pl.BlockSpec(memory_space=pltpu.VMEM)
SMEM = pl.BlockSpec(memory_space=pltpu.SMEM)
PARAMS = pltpu.CompilerParams(vmem_limit_bytes=44 << 20)


def body(cheb_coef, obj_cell):
    own = cheb_coef[0]
    objects = own.shape[2]
    cells = lax.axis_size("cell")
    slots = cells * CAP
    windows = lax.axis_size("tm")
    window = lax.axis_index("tm").astype(jnp.int32).reshape(1)
    prev = lax.ppermute(own, "tm", [(i, i + 1) for i in range(windows - 1)])
    row = jax.ShapeDtypeStruct((1, slots), jnp.float32)
    send = pl.pallas_call(
        front_kernel,
        out_shape=jax.ShapeDtypeStruct((slots, LANES), jnp.float32),
        in_specs=[SMEM, VMEM, VMEM, VMEM, VMEM],
        out_specs=VMEM,
        scratch_shapes=[pltpu.VMEM((LANES, objects), jnp.float32)],
        name="front",
    )(window, own, prev, obj_cell.reshape(1, objects), jnp.asarray(rim_tables()))
    packed = lax.all_to_all(send, "cell", split_axis=0, concat_axis=0, tiled=True)
    following = lax.ppermute(packed, "cell", [((i + 1) % cells, i) for i in range(cells)])
    synth = jnp.asarray(synth_matrix())
    left_sel = jnp.asarray(np.ascontiguousarray(selection(True).T))
    right_sel = jnp.asarray(selection(False))
    left_shape = jax.ShapeDtypeStruct((EXT // GROUP, slots, LANES), jnp.bfloat16)
    right_scratch = pltpu.VMEM((EXT, PIECES, slots), jnp.bfloat16)
    scratch = [right_scratch, pltpu.VMEM((slots, COLS), jnp.float32), pltpu.VMEM((slots, LANES), jnp.float32)]
    cost = pl.CostEstimate(flops=40_000_000_000, bytes_accessed=8_000_000, transcendentals=0)
    own_min, left = pl.pallas_call(
        self_kernel,
        out_shape=(row, left_shape),
        in_specs=[VMEM] * 4,
        out_specs=(VMEM, VMEM),
        scratch_shapes=scratch,
        compiler_params=PARAMS,
        cost_estimate=cost,
        name="self_screen",
    )(packed, synth, left_sel, right_sel)
    row_min, col_min = pl.pallas_call(
        cross_kernel,
        out_shape=(row, row),
        in_specs=[VMEM] * 4,
        out_specs=(VMEM, VMEM),
        scratch_shapes=scratch,
        compiler_params=PARAMS,
        cost_estimate=cost,
        name="cross_screen",
    )(left, following, synth, right_sel)
    back_min = lax.ppermute(col_min, "cell", [(i, (i + 1) % cells) for i in range(cells)])
    result = jnp.minimum(jnp.minimum(own_min, row_min), back_min)
    return jnp.clip(result, 0.0, CLIP)


def solution(mesh):
    in_specs = (P("tm", None, None, "cell"), P("tm", "cell", None))
    return jax.shard_map(body, mesh=mesh, in_specs=in_specs, out_specs=P("tm", "cell"), check_vma=False)
```

```python
import functools

import jax
import jax.numpy as jnp
import ml_dtypes
import numpy as np
from jax import lax
from jax.experimental import pallas as pl
from jax.experimental.pallas import tpu as pltpu
from jax.sharding import PartitionSpec as P

DEG1 = 17
SAMP = 64
RIM = 8
CAP = 24
EXT = SAMP + RIM
CLIP = 25.0
FAR = 1.0e9

LANES = 128
RIM_AT = 72
FLAG_AT = 96

PIECES = 32
GROUP = LANES // PIECES
CHUNK = 24
PARTS = 2
NORMS = 3
KINDS = 3 * PARTS + NORMS
SRC = 256
COLS = 256
UNROLL = 3
BF16 = jnp.bfloat16


def cheb_table():
    nodes = ((2.0 * np.arange(SAMP, dtype=np.float32) + 1.0) / SAMP - 1.0).astype(np.float32)
    columns = [np.ones_like(nodes), nodes]
    for _ in range(2, DEG1):
        columns.append((2.0 * nodes * columns[-1] - columns[-2]).astype(np.float32))
    return np.stack(columns, axis=1)


def rim_tables():
    table = cheb_table()
    return np.stack([table[:RIM], table[SAMP - RIM :]])


def synth_matrix():
    table = cheb_table()
    weights = np.zeros((3 * EXT, LANES), np.float32)
    for c in range(3):
        for s in range(RIM):
            weights[c * EXT + s, RIM_AT + RIM * c + s] = 1.0
        weights[c * EXT + RIM : (c + 1) * EXT, 24 * c : 24 * c + DEG1] = table
    return weights


def selection(left):
    one = KINDS
    uses = []
    for i in range(PARTS):
        for j in range(PARTS):
            for c in range(3):
                uses.append((3 * i + c, 1.0) if left else (3 * j + c, -1.0))
    for n in range(NORMS):
        uses.append((3 * PARTS + n, 1.0) if left else (one, 1.0))
    for n in range(NORMS):
        uses.append((one, 1.0) if left else (3 * PARTS + n, 1.0))
    matrix = np.zeros((CHUNK * PIECES, SRC), np.float32)
    for t in range(CHUNK):
        for k, (kind, value) in enumerate(uses):
            matrix[t * PIECES + k, kind * CHUNK + (0 if kind == one else t)] = value
    return matrix.astype(ml_dtypes.bfloat16)


def split(value, count):
    pieces = []
    for _ in range(count):
        piece = value.astype(BF16).astype(jnp.float32)
        value = value - piece
        pieces.append(piece)
    return pieces, value


def place_kernel(cell_ref, out_ref):
    slots, count = out_ref.shape
    cell = cell_ref[...].astype(jnp.float32)
    column = jnp.transpose(jnp.broadcast_to(cell, (LANES, count)))
    column = jnp.concatenate([column] * (count // LANES), axis=1)
    before = lax.broadcasted_iota(jnp.int32, (count, count), 0) < lax.broadcasted_iota(jnp.int32, (count, count), 1)
    same = (column == jnp.broadcast_to(cell, (count, count))) & before
    rank = jnp.sum(jnp.where(same, 1.0, 0.0), axis=0, keepdims=True)
    slot = (cell * CAP + rank).astype(jnp.int32)
    chosen = lax.broadcasted_iota(jnp.int32, (slots, count), 0) == jnp.broadcast_to(slot, (slots, count))
    out_ref[...] = jnp.where(chosen, 1.0, 0.0).astype(BF16)


def front_kernel(first_ref, own_ref, prev_ref, chosen_ref, table_ref, out_ref, rows_ref):
    count = chosen_ref.shape[1]
    blocks = count // LANES
    first = first_ref[0] == 0
    rows_ref[...] = jnp.zeros_like(rows_ref)
    table = jnp.where(first, table_ref[0], table_ref[1])
    for c in range(3):
        for n in range(blocks):
            lanes = slice(n * LANES, (n + 1) * LANES)
            rows = pl.ds(c * DEG1 * blocks + n, DEG1, stride=blocks)
            own = own_ref[rows, :]
            rows_ref[24 * c : 24 * c + DEG1, lanes] = own
            source = jnp.where(first, own, prev_ref[rows, :])
            rows_ref[RIM_AT + RIM * c : RIM_AT + RIM * (c + 1), lanes] = jnp.dot(
                table, source, precision=lax.Precision.HIGHEST, preferred_element_type=jnp.float32
            )
    rows_ref[FLAG_AT : FLAG_AT + 1, :] = jnp.ones((1, count), jnp.float32)
    data = jnp.transpose(rows_ref[...])
    total = None
    for _ in range(3):
        piece = data.astype(BF16)
        data = data - piece.astype(jnp.float32)
        term = jnp.dot(chosen_ref[...], piece, preferred_element_type=jnp.float32)
        total = term if total is None else total + term
    out_ref[...] = total


def fetched(sources, targets, sem):
    copies = [pltpu.make_async_copy(s, t, sem.at[i]) for i, (s, t) in enumerate(zip(sources, targets))]
    for copy in copies:
        copy.start()
    return copies


def operands(packed_ref, synth_ref, right_sel_ref, right_ref, copies, left_sel_ref=None, left_ref=None):
    count = packed_ref.shape[0]
    packed = jnp.transpose(packed_ref[...])
    flag = packed[FLAG_AT : FLAG_AT + 1, :] > 0.5
    for copy in copies:
        copy.wait()
    track = jnp.dot(synth_ref[...], packed, precision=lax.Precision.HIGHEST, preferred_element_type=jnp.float32)
    parts = [[], [], []]
    norm = None
    for c in range(3):
        axis = track[c * EXT : (c + 1) * EXT]
        parts[c], rest = split(axis, PARTS)
        held = axis - rest
        norm = held * held if norm is None else norm + held * held
    norm = jnp.where(jnp.broadcast_to(flag, norm.shape), 0.5 * norm, FAR)
    kinds = [parts[c][i] for i in range(PARTS) for c in range(3)] + split(norm, NORMS)[0]
    ones = jnp.ones((8, count), jnp.float32)
    zeros = jnp.zeros((SRC - KINDS * CHUNK - 8, count), jnp.float32)
    for n in range(EXT // CHUNK):
        rows = slice(n * CHUNK, (n + 1) * CHUNK)
        source = jnp.concatenate([k[rows] for k in kinds] + [ones, zeros], axis=0)
        right = jnp.dot(right_sel_ref[...], source.astype(BF16), preferred_element_type=jnp.float32).astype(BF16)
        for t in range(CHUNK):
            right_ref[n * CHUNK + t] = right[t * PIECES : (t + 1) * PIECES]
        if left_ref is not None:
            flipped = jnp.transpose(source).astype(BF16)
            for g in range(CHUNK // GROUP):
                block = jnp.dot(
                    flipped, left_sel_ref[:, g * LANES : (g + 1) * LANES], preferred_element_type=jnp.float32
                )
                left_ref[n * (CHUNK // GROUP) + g] = block.astype(BF16)


def tile_min(left_ref, right_ref, acc_ref, rows, col_start):
    groups = left_ref.shape[0]
    acc_ref[0:rows, :] = jnp.full((rows, COLS), CLIP, jnp.float32)

    def step(it, carry):
        best = acc_ref[0:rows, :]
        for u in range(UNROLL):
            g = it * UNROLL + u
            left = left_ref[g, 0:rows, :]
            for j in range(GROUP):
                block = right_ref[g * GROUP + j, :, pl.ds(col_start, COLS)]
                parts = [block]
                if j > 0:
                    parts = [jnp.zeros((PIECES * j, COLS), BF16)] + parts
                if j < GROUP - 1:
                    parts = parts + [jnp.zeros((PIECES * (GROUP - 1 - j), COLS), BF16)]
                weights = jnp.concatenate(parts, axis=0)
                best = jnp.minimum(best, jnp.dot(left, weights, preferred_element_type=jnp.float32))
        acc_ref[0:rows, :] = best
        return carry

    lax.fori_loop(0, groups // UNROLL, step, 0)


def fold(acc_ref, row_ref, rows):
    acc = acc_ref[0:rows, :]
    half = jnp.minimum(acc[:, :LANES], acc[:, LANES:])
    row_ref[0:rows, :] = jnp.minimum(row_ref[0:rows, :], half)
    return jnp.min(acc, axis=0, keepdims=True)


def finished(half):
    return jnp.clip(2.0 * half, 0.0, CLIP)


def prepare_kernel(
    packed_ref, synth_hbm, left_sel_hbm, right_sel_hbm, left_ref, right_ref, synth_ref, left_sel_ref, right_sel_ref, sem
):
    copies = fetched((synth_hbm, left_sel_hbm, right_sel_hbm), (synth_ref, left_sel_ref, right_sel_ref), sem)
    operands(packed_ref, synth_ref, right_sel_ref, right_ref, copies, left_sel_ref, left_ref)


def self_kernel(left_ref, right_ref, cross_ref, out_ref, acc_ref, row_ref):
    count = left_ref.shape[1]
    row_ref[...] = jnp.full_like(row_ref, CLIP)
    parts = []
    for n in range(count // COLS):
        rows = (n + 1) * COLS
        tile_min(left_ref, right_ref, acc_ref, rows, n * COLS)
        near = acc_ref[rows - COLS : rows, :]
        same = lax.broadcasted_iota(jnp.int32, (COLS, COLS), 0) == lax.broadcasted_iota(jnp.int32, (COLS, COLS), 1)
        acc_ref[rows - COLS : rows, :] = jnp.where(same, CLIP, near)
        parts.append(fold(acc_ref, row_ref, rows))
    by_row = jnp.min(jnp.transpose(row_ref[...]), axis=0, keepdims=True)
    best = jnp.minimum(jnp.concatenate(parts, axis=1), by_row)
    out_ref[...] = jnp.minimum(finished(best), cross_ref[...])


def cross_kernel(
    left_ref, packed_ref, synth_hbm, right_sel_hbm, row_out_ref, col_out_ref, right_ref, acc_ref, row_ref, synth_ref,
    right_sel_ref, sem
):
    count = packed_ref.shape[0]
    copies = fetched((synth_hbm, right_sel_hbm), (synth_ref, right_sel_ref), sem)
    operands(packed_ref, synth_ref, right_sel_ref, right_ref, copies)
    row_ref[...] = jnp.full_like(row_ref, CLIP)

    def column(n, carry):
        start = pl.multiple_of(n * COLS, COLS)
        tile_min(left_ref, right_ref, acc_ref, count, start)
        col_out_ref[:, pl.ds(start, COLS)] = finished(fold(acc_ref, row_ref, count))
        return carry

    lax.fori_loop(0, count // COLS, column, 0)
    row_out_ref[...] = finished(jnp.min(jnp.transpose(row_ref[...]), axis=0, keepdims=True))


VMEM = pl.BlockSpec(memory_space=pltpu.VMEM)
SMEM = pl.BlockSpec(memory_space=pltpu.SMEM)
ANY = pl.BlockSpec(memory_space=pl.ANY)


def call(kernel, name, out_shape, in_specs, scratch, vmem, flops):
    return pl.pallas_call(
        kernel,
        out_shape=out_shape,
        in_specs=in_specs,
        out_specs=jax.tree.map(lambda _: VMEM, out_shape),
        scratch_shapes=scratch,
        compiler_params=pltpu.CompilerParams(vmem_limit_bytes=vmem << 20),
        cost_estimate=pl.CostEstimate(flops=flops, bytes_accessed=4_000_000, transcendentals=0),
        name=name,
    )


def body(cheb_coef, obj_cell):
    objects = cheb_coef.shape[3]
    own = cheb_coef.reshape(-1, LANES)
    cells = lax.axis_size("cell")
    slots = cells * CAP
    windows = lax.axis_size("tm")
    window = lax.axis_index("tm").astype(jnp.int32).reshape(1)
    prev = lax.ppermute(own, "tm", [(i, i + 1) for i in range(windows - 1)])
    row = jax.ShapeDtypeStruct((1, slots), jnp.float32)
    chosen = call(
        place_kernel, "place", jax.ShapeDtypeStruct((slots, objects), BF16), [VMEM], [], 8, 2_000_000_000
    )(obj_cell.reshape(1, objects))
    send = call(
        front_kernel,
        "front",
        jax.ShapeDtypeStruct((slots, LANES), jnp.float32),
        [SMEM, VMEM, VMEM, VMEM, VMEM],
        [pltpu.VMEM((LANES, objects), jnp.float32)],
        8,
        2_000_000_000,
    )(window, own, prev, chosen, jnp.asarray(rim_tables()))
    packed = lax.all_to_all(send, "cell", split_axis=0, concat_axis=0, tiled=True)
    following = lax.ppermute(packed, "cell", [((i + 1) % cells, i) for i in range(cells)])
    synth = jnp.asarray(synth_matrix())
    left_sel = jnp.asarray(np.ascontiguousarray(selection(True).T))
    right_sel = jnp.asarray(selection(False))
    left_shape = jax.ShapeDtypeStruct((EXT // GROUP, slots, LANES), BF16)
    right_shape = jax.ShapeDtypeStruct((EXT, PIECES, slots), BF16)
    synth_scratch = pltpu.VMEM(synth.shape, jnp.float32)
    left_sel_scratch = pltpu.VMEM(left_sel.shape, BF16)
    right_sel_scratch = pltpu.VMEM(right_sel.shape, BF16)
    minima = [pltpu.VMEM((slots, COLS), jnp.float32), pltpu.VMEM((slots, LANES), jnp.float32)]
    left, right = call(
        prepare_kernel,
        "prepare",
        (left_shape, right_shape),
        [VMEM, ANY, ANY, ANY],
        [synth_scratch, left_sel_scratch, right_sel_scratch, pltpu.SemaphoreType.DMA((3,))],
        24,
        6_000_000_000,
    )(packed, synth, left_sel, right_sel)
    row_min, col_min = call(
        cross_kernel,
        "cross_screen",
        (row, row),
        [VMEM, VMEM, ANY, ANY],
        [pltpu.VMEM(right_shape.shape, BF16)]
        + minima
        + [synth_scratch, right_sel_scratch, pltpu.SemaphoreType.DMA((2,))],
        32,
        20_000_000_000,
    )(left, following, synth, right_sel)
    back_min = lax.ppermute(col_min, "cell", [(i, (i + 1) % cells) for i in range(cells)])
    own_min = call(self_kernel, "self_screen", row, [VMEM] * 3, minima, 24, 15_000_000_000)(left, right, row_min)
    return jnp.minimum(own_min, back_min)


def solution(mesh):
    in_specs = (P("tm", None, None, "cell"), P("tm", "cell", None))
    return jax.shard_map(body, mesh=mesh, in_specs=in_specs, out_specs=P("tm", "cell"), check_vma=False)
```

```python
import functools

import jax
import jax.numpy as jnp
import ml_dtypes
import numpy as np
from jax import lax
from jax.experimental import pallas as pl
from jax.experimental.pallas import tpu as pltpu
from jax.sharding import PartitionSpec as P

DEG1 = 17
SAMP = 64
RIM = 8
CAP = 24
EXT = SAMP + RIM
CLIP = 25.0
FAR = 1.0e9

LANES = 128
FLAG_AT = 17
RIM_AT = 72
COUNT_AT = 96

PIECES = 32
GROUP = LANES // PIECES
CHUNK = 8
UNITS = EXT // CHUNK
PARTS = 2
NORMS = 3
KINDS = 3 * PARTS + NORMS
SRC = 128
ROWS = 128
COLS = 256
BF16 = jnp.bfloat16


def cheb_table():
    nodes = ((2.0 * np.arange(SAMP, dtype=np.float32) + 1.0) / SAMP - 1.0).astype(np.float32)
    columns = [np.ones_like(nodes), nodes]
    for _ in range(2, DEG1):
        columns.append((2.0 * nodes * columns[-1] - columns[-2]).astype(np.float32))
    return np.stack(columns, axis=1)


def rim_tables():
    table = cheb_table()
    return np.stack([table[:RIM], table[SAMP - RIM :]])


def synth_matrix():
    table = cheb_table()
    weights = np.zeros((3 * EXT, LANES), np.float32)
    for c in range(3):
        for s in range(RIM):
            weights[c * EXT + s, RIM_AT + RIM * c + s] = 1.0
        weights[c * EXT + RIM : (c + 1) * EXT, 24 * c : 24 * c + DEG1] = table
    return weights


def selection(left):
    one = KINDS
    uses = []
    for i in range(PARTS):
        for j in range(PARTS):
            for c in range(3):
                uses.append((3 * i + c, 1.0) if left else (3 * j + c, -1.0))
    for n in range(NORMS):
        uses.append((3 * PARTS + n, 1.0) if left else (one, 1.0))
    for n in range(NORMS):
        uses.append((one, 1.0) if left else (3 * PARTS + n, 1.0))
    matrix = np.zeros((CHUNK * PIECES, SRC), np.float32)
    for t in range(CHUNK):
        for k, (kind, value) in enumerate(uses):
            matrix[t * PIECES + k, kind * CHUNK + (0 if kind == one else t)] = value
    return matrix.astype(ml_dtypes.bfloat16)


def split(value, count):
    pieces = []
    for _ in range(count):
        piece = value.astype(BF16).astype(jnp.float32)
        value = value - piece
        pieces.append(piece)
    return pieces, value


def place_kernel(cell_ref, out_ref, count_ref):
    slots, count = out_ref.shape
    cell = cell_ref[...].astype(jnp.float32)
    column = jnp.transpose(jnp.broadcast_to(cell, (LANES, count)))
    lane = lax.broadcasted_iota(jnp.int32, (count, LANES), 1).astype(jnp.float32)
    named = jnp.where(column == lane - COUNT_AT, 1.0, 0.0)
    count_ref[...] = jnp.sum(named, axis=0, keepdims=True)
    column = jnp.concatenate([column] * (count // LANES), axis=1)
    before = lax.broadcasted_iota(jnp.int32, (count, count), 0) < lax.broadcasted_iota(jnp.int32, (count, count), 1)
    same = (column == jnp.broadcast_to(cell, (count, count))) & before
    rank = jnp.sum(jnp.where(same, 1.0, 0.0), axis=0, keepdims=True)
    slot = (cell * CAP + rank).astype(jnp.int32)
    chosen = lax.broadcasted_iota(jnp.int32, (slots, count), 0) == jnp.broadcast_to(slot, (slots, count))
    out_ref[...] = jnp.where(chosen, 1.0, 0.0).astype(BF16)


def placed(chosen, data):
    total = None
    for _ in range(3):
        piece = data.astype(BF16)
        data = data - piece.astype(jnp.float32)
        term = jnp.dot(chosen, piece, preferred_element_type=jnp.float32)
        total = term if total is None else total + term
    return total


def front_kernel(first_ref, own_ref, prev_ref, chosen_ref, count_ref, table_ref, out_ref, rows_ref):
    count = chosen_ref.shape[1]
    blocks = count // LANES
    first = first_ref[0] == 0
    rows_ref[...] = jnp.zeros_like(rows_ref)
    table = jnp.where(first, table_ref[0], table_ref[1])
    for c in range(3):
        for n in range(blocks):
            lanes = slice(n * LANES, (n + 1) * LANES)
            rows = pl.ds(c * DEG1 * blocks + n, DEG1, stride=blocks)
            own = own_ref[rows, :]
            rows_ref[24 * c : 24 * c + DEG1, lanes] = own
            source = jnp.where(first, own, prev_ref[rows, :])
            rows_ref[RIM_AT + RIM * c : RIM_AT + RIM * (c + 1), lanes] = jnp.dot(
                table, source, precision=lax.Precision.HIGHEST, preferred_element_type=jnp.float32
            )
    rows_ref[FLAG_AT : FLAG_AT + 1, :] = jnp.ones((1, count), jnp.float32)
    out_ref[...] = placed(chosen_ref[...], jnp.transpose(rows_ref[...])) + count_ref[...]


def plan(counts):
    rows = jnp.maximum(jnp.ceil(counts / ROWS), 1.0) * ROWS
    tiles = jnp.maximum(jnp.ceil(counts / COLS), 1.0)
    fixed, per_row = 11.0, 0.139
    alone = tiles * fixed + per_row * (
        jnp.minimum(rows, COLS)
        + jnp.where(tiles > 1.5, jnp.minimum(rows, 2 * COLS), 0.0)
        + jnp.where(tiles > 2.5, rows, 0.0)
    )
    after = lambda value: pltpu.roll(value, LANES - 1, 1)
    ahead = lambda value: pltpu.roll(value, 1, 1)
    here = after(tiles) * (fixed + per_row * rows)
    there = tiles * (fixed + per_row * after(rows))
    share = jnp.full_like(counts, 0.5)
    for _ in range(6):
        load = alone + share * here + ahead((1.0 - share) * there)
        share = jnp.clip(share + 0.8 * (after(load) - load) / (here + there), 0.0, 1.0)
    return jnp.floor(share * UNITS + 0.5)


def compact_kernel(packed_ref, live_ref, chosen_ref, plan_ref):
    packed = packed_ref[...]
    slots = packed.shape[0]
    flag = jnp.transpose(packed)[FLAG_AT : FLAG_AT + 1, :]
    first = lax.broadcasted_iota(jnp.int32, (slots, slots), 0)
    second = lax.broadcasted_iota(jnp.int32, (slots, slots), 1)
    before = jnp.where(first < second, 1.0, 0.0).astype(BF16)
    flags = jnp.broadcast_to(flag, (16, slots)).astype(BF16)
    place = jnp.dot(flags, before, preferred_element_type=jnp.float32)[0:1]
    place = jnp.where(flag > 0.5, place, -1.0).astype(jnp.int32)
    chosen = jnp.where(first == jnp.broadcast_to(place, (slots, slots)), 1.0, 0.0).astype(BF16)
    chosen_ref[...] = chosen
    live_ref[...] = placed(chosen, packed)
    lane = lax.broadcasted_iota(jnp.int32, (1, LANES), 1)
    counts = jnp.sum(packed, axis=0, keepdims=True) * (1.0 / CAP)
    counts = jnp.floor(jnp.where(lane >= COUNT_AT, counts, 0.0) + 0.5)
    cells = LANES - COUNT_AT
    counts = counts + pltpu.roll(counts, cells, 1)
    counts = counts + pltpu.roll(counts, 2 * cells, 1)
    plan_ref[0:1, :] = counts
    plan_ref[1:2, :] = plan(counts)


def fetched(sources, targets, sem):
    copies = [pltpu.make_async_copy(s, t, sem.at[i]) for i, (s, t) in enumerate(zip(sources, targets))]
    for copy in copies:
        copy.start()
    return copies


def tracks(live_ref, synth_ref, track_ref, flag_ref, copies):
    live = jnp.transpose(live_ref[...])
    flag_ref[...] = jnp.broadcast_to(live[FLAG_AT : FLAG_AT + 1, :], flag_ref.shape)
    for copy in copies:
        copy.wait()
    track = jnp.dot(synth_ref[...], live, precision=lax.Precision.HIGHEST, preferred_element_type=jnp.float32)
    track_ref[...] = track.reshape(track_ref.shape)


def source_of(track_ref, flag_ref, unit):
    count = track_ref.shape[3]
    parts, norm = [], None
    for c in range(3):
        axis = track_ref[c, unit]
        pieces, rest = split(axis, PARTS)
        parts.append(pieces)
        held = axis - rest
        norm = held * held if norm is None else norm + held * held
    norm = jnp.where(flag_ref[...] > 0.5, 0.5 * norm, FAR)
    kinds = [parts[c][i] for i in range(PARTS) for c in range(3)] + split(norm, NORMS)[0]
    ones = jnp.ones((CHUNK, count), jnp.float32)
    zeros = jnp.zeros((SRC - (KINDS + 1) * CHUNK, count), jnp.float32)
    return jnp.concatenate(kinds + [ones, zeros], axis=0)


def put_right(source, right_sel_ref, right_ref, unit):
    right = jnp.dot(right_sel_ref[...], source.astype(BF16), preferred_element_type=jnp.float32)
    right_ref[pl.ds(unit * CHUNK, CHUNK)] = right.astype(BF16).reshape(CHUNK, PIECES, right.shape[1])


def put_left(source, left_sel_ref, left_ref, unit):
    left = jnp.dot(jnp.transpose(source).astype(BF16), left_sel_ref[...], preferred_element_type=jnp.float32)
    left = left.astype(BF16)
    for g in range(CHUNK // GROUP):
        left_ref[unit * (CHUNK // GROUP) + g] = left[:, g * LANES : (g + 1) * LANES]


def sweep(left_ref, right_ref, acc_ref, row_tiles, col_start, first, last):
    acc_ref[...] = jnp.full_like(acc_ref, CLIP)
    for n in range(1, acc_ref.shape[0] // ROWS + 1):

        @pl.when(row_tiles == n)
        def _(rows=n * ROWS):
            def step(unit, carry):
                best = acc_ref[0:rows, :]
                for h in range(CHUNK // GROUP):
                    g = unit * (CHUNK // GROUP) + h
                    left = left_ref[g, 0:rows, :]
                    for j in range(GROUP):
                        parts = [right_ref[g * GROUP + j, :, pl.ds(col_start, COLS)]]
                        if j > 0:
                            parts = [jnp.zeros((PIECES * j, COLS), BF16)] + parts
                        if j < GROUP - 1:
                            parts = parts + [jnp.zeros((PIECES * (GROUP - 1 - j), COLS), BF16)]
                        weights = jnp.concatenate(parts, axis=0)
                        best = jnp.minimum(best, jnp.dot(left, weights, preferred_element_type=jnp.float32))
                acc_ref[0:rows, :] = best
                return carry

            lax.fori_loop(first, last, step, 0)


def fold(acc_ref, row_ref):
    acc = acc_ref[...]
    row_ref[...] = jnp.minimum(row_ref[...], jnp.minimum(acc[:, :LANES], acc[:, LANES:]))
    return jnp.min(acc, axis=0, keepdims=True)


def by_row(row_ref):
    return finished(jnp.min(jnp.transpose(row_ref[...]), axis=0, keepdims=True))


def finished(half):
    return jnp.clip(2.0 * half, 0.0, CLIP)


def planned(plan_ref, row, cell, cells):
    lane = lax.broadcasted_iota(jnp.int32, (1, LANES), 1)
    value = jnp.sum(jnp.where(lane == lax.rem(cell, cells), plan_ref[row : row + 1, :], 0.0))
    return value.astype(jnp.int32)


def tiles_of(count, size):
    return jnp.maximum((count + (size - 1)) // size, 1)


def prepare_kernel(
    live_ref, synth_hbm, left_sel_hbm, right_sel_hbm, left_ref, right_ref,
    synth_ref, left_sel_ref, right_sel_ref, track_ref, flag_ref, sem,
):
    copies = fetched((synth_hbm, left_sel_hbm, right_sel_hbm), (synth_ref, left_sel_ref, right_sel_ref), sem)
    tracks(live_ref, synth_ref, track_ref, flag_ref, copies)
    for unit in range(UNITS):
        source = source_of(track_ref, flag_ref, unit)
        put_right(source, right_sel_ref, right_ref, unit)
        put_left(source, left_sel_ref, left_ref, unit)


def cross_kernel(
    ahead, cells, cell_ref, plan_ref, left_ref, live_ref, synth_hbm, right_sel_hbm, row_out_ref, col_out_ref,
    right_ref, acc_ref, row_ref, synth_ref, right_sel_ref, track_ref, flag_ref, sem,
):
    copies = fetched((synth_hbm, right_sel_hbm), (synth_ref, right_sel_ref), sem)
    cell = cell_ref[0]
    other = cell + 1 if ahead else cell + (cells - 1)
    bound = planned(plan_ref, 1, cell if ahead else other, cells)
    first, last = (0, bound) if ahead else (bound, UNITS)
    row_tiles = tiles_of(planned(plan_ref, 0, cell, cells), ROWS)
    col_tiles = tiles_of(planned(plan_ref, 0, other, cells), COLS)
    tracks(live_ref, synth_ref, track_ref, flag_ref, copies)

    def unit_step(unit, carry):
        put_right(source_of(track_ref, flag_ref, unit), right_sel_ref, right_ref, unit)
        return carry

    lax.fori_loop(first, last, unit_step, 0)
    row_ref[...] = jnp.full_like(row_ref, CLIP)
    col_out_ref[...] = jnp.full_like(col_out_ref, CLIP)

    def column(n, carry):
        start = pl.multiple_of(n * COLS, COLS)
        sweep(left_ref, right_ref, acc_ref, row_tiles, start, first, last)
        col_out_ref[:, pl.ds(start, COLS)] = finished(fold(acc_ref, row_ref))
        return carry

    lax.fori_loop(0, col_tiles, column, 0)
    row_out_ref[...] = by_row(row_ref)


def self_kernel(cells, cell_ref, plan_ref, left_ref, right_ref, next_ref, prev_ref, out_ref, acc_ref, row_ref, col_ref):
    count = planned(plan_ref, 0, cell_ref[0], cells)
    row_tiles = tiles_of(count, ROWS)
    row_ref[...] = jnp.full_like(row_ref, CLIP)
    col_ref[...] = jnp.full_like(col_ref, CLIP)
    same = lax.broadcasted_iota(jnp.int32, (COLS, COLS), 0) == lax.broadcasted_iota(jnp.int32, (COLS, COLS), 1)

    def column(n, carry):
        start = pl.multiple_of(n * COLS, COLS)
        sweep(left_ref, right_ref, acc_ref, jnp.minimum(row_tiles, (n + 1) * (COLS // ROWS)), start, 0, UNITS)
        acc_ref[pl.ds(start, COLS), :] = jnp.where(same, CLIP, acc_ref[pl.ds(start, COLS), :])
        col_ref[:, pl.ds(start, COLS)] = finished(fold(acc_ref, row_ref))
        return carry

    lax.fori_loop(0, tiles_of(count, COLS), column, 0)
    best = jnp.minimum(by_row(row_ref), col_ref[...])
    out_ref[...] = jnp.minimum(best, jnp.minimum(next_ref[...], prev_ref[...]))


def restore_kernel(own_ref, next_ref, prev_ref, chosen_ref, out_ref):
    count = own_ref.shape[1]
    best = jnp.minimum(own_ref[...], jnp.minimum(next_ref[...], prev_ref[...]))
    pieces = split(best, 3)[0]
    ones, zeros = jnp.ones((1, count), jnp.float32), jnp.zeros((12, count), jnp.float32)
    rows = jnp.concatenate(pieces + [ones, zeros], axis=0).astype(BF16)
    found = jnp.dot(rows, chosen_ref[...], preferred_element_type=jnp.float32)
    value = found[0:1] + found[1:2] + found[2:3]
    out_ref[...] = jnp.where(found[3:4] > 0.5, value, CLIP)


VMEM = pl.BlockSpec(memory_space=pltpu.VMEM)
SMEM = pl.BlockSpec(memory_space=pltpu.SMEM)
ANY = pl.BlockSpec(memory_space=pl.ANY)


def call(kernel, name, out_shape, in_specs, scratch, vmem, flops):
    return pl.pallas_call(
        kernel,
        out_shape=out_shape,
        in_specs=in_specs,
        out_specs=jax.tree.map(lambda _: VMEM, out_shape),
        scratch_shapes=scratch,
        compiler_params=pltpu.CompilerParams(vmem_limit_bytes=vmem << 20),
        cost_estimate=pl.CostEstimate(flops=flops, bytes_accessed=4_000_000, transcendentals=0),
        name=name,
    )


def body(cheb_coef, obj_cell):
    objects = cheb_coef.shape[3]
    own = cheb_coef.reshape(-1, LANES)
    cells = lax.axis_size("cell")
    slots = cells * CAP
    windows = lax.axis_size("tm")
    window = lax.axis_index("tm").astype(jnp.int32).reshape(1)
    prev = lax.ppermute(own, "tm", [(i, i + 1) for i in range(windows - 1)])
    row = jax.ShapeDtypeStruct((1, slots), jnp.float32)
    cell = lax.axis_index("cell").astype(jnp.int32).reshape(1)
    wide = jax.ShapeDtypeStruct((slots, LANES), jnp.float32)
    chosen, counts = call(
        place_kernel,
        "place",
        (jax.ShapeDtypeStruct((slots, objects), BF16), jax.ShapeDtypeStruct((1, LANES), jnp.float32)),
        [VMEM],
        [],
        8,
        2_000_000_000,
    )(obj_cell.reshape(1, objects))
    send = call(
        front_kernel,
        "front",
        wide,
        [SMEM] + [VMEM] * 5,
        [pltpu.VMEM((LANES, objects), jnp.float32)],
        8,
        2_000_000_000,
    )(window, own, prev, chosen, counts, jnp.asarray(rim_tables()))
    packed = lax.all_to_all(send, "cell", split_axis=0, concat_axis=0, tiled=True)
    live, chosen, shares = call(
        compact_kernel,
        "compact",
        (wide, jax.ShapeDtypeStruct((slots, slots), BF16), jax.ShapeDtypeStruct((8, LANES), jnp.float32)),
        [VMEM],
        [],
        16,
        2_000_000_000,
    )(packed)
    forward = [(i, (i + 1) % cells) for i in range(cells)]
    backward = [((i + 1) % cells, i) for i in range(cells)]
    next_live = lax.ppermute(live, "cell", backward)
    prev_live = lax.ppermute(live, "cell", forward)
    synth = jnp.asarray(synth_matrix())
    left_sel = jnp.asarray(np.ascontiguousarray(selection(True).T))
    right_sel = jnp.asarray(selection(False))
    left_shape = jax.ShapeDtypeStruct((EXT // GROUP, slots, LANES), BF16)
    right_shape = jax.ShapeDtypeStruct((EXT, PIECES, slots), BF16)
    synth_scratch = pltpu.VMEM(synth.shape, jnp.float32)
    left_sel_scratch = pltpu.VMEM(left_sel.shape, BF16)
    right_sel_scratch = pltpu.VMEM(right_sel.shape, BF16)
    track_scratch = [pltpu.VMEM((3, UNITS, CHUNK, slots), jnp.float32), pltpu.VMEM((CHUNK, slots), jnp.float32)]
    minima = [pltpu.VMEM((slots, COLS), jnp.float32), pltpu.VMEM((slots, LANES), jnp.float32)]
    left, right = call(
        prepare_kernel,
        "prepare",
        (left_shape, right_shape),
        [VMEM, ANY, ANY, ANY],
        [synth_scratch, left_sel_scratch, right_sel_scratch] + track_scratch + [pltpu.SemaphoreType.DMA((3,))],
        24,
        6_000_000_000,
    )(live, synth, left_sel, right_sel)

    def cross(ahead, other):
        return call(
            functools.partial(cross_kernel, ahead, cells),
            "cross_next" if ahead else "cross_prev",
            (row, row),
            [SMEM, VMEM, VMEM, VMEM, ANY, ANY],
            [pltpu.VMEM(right_shape.shape, BF16)]
            + minima
            + [synth_scratch, right_sel_scratch]
            + track_scratch
            + [pltpu.SemaphoreType.DMA((2,))],
            32,
            12_000_000_000,
        )(cell, shares, left, other, synth, right_sel)

    next_row, next_col = cross(True, next_live)
    from_prev = lax.ppermute(next_col, "cell", forward)
    prev_row, prev_col = cross(False, prev_live)
    from_next = lax.ppermute(prev_col, "cell", backward)
    own_min = call(
        functools.partial(self_kernel, cells),
        "self_screen",
        row,
        [SMEM] + [VMEM] * 5,
        minima + [pltpu.VMEM((1, slots), jnp.float32)],
        24,
        15_000_000_000,
    )(cell, shares, left, right, next_row, prev_row)
    return call(restore_kernel, "restore", row, [VMEM] * 4, [], 8, 100_000_000)(own_min, from_prev, from_next, chosen)


def solution(mesh):
    in_specs = (P("tm", None, None, "cell"), P("tm", "cell", None))
    return jax.shard_map(body, mesh=mesh, in_specs=in_specs, out_specs=P("tm", "cell"), check_vma=False)
```

```python
import functools

import jax
import jax.numpy as jnp
import ml_dtypes
import numpy as np
from jax import lax
from jax.experimental import pallas as pl
from jax.experimental.pallas import tpu as pltpu
from jax.sharding import PartitionSpec as P

DEG1 = 17
SAMP = 64
RIM = 8
CAP = 24
EXT = SAMP + RIM
CLIP = 25.0
FAR = 1.0e9

LANES = 128
FLAG_AT = 3 * DEG1
RIM_AT = FLAG_AT + 1
RECORD = RIM_AT + 3 * RIM
PACK = 16
LATE = CAP - PACK
COUNT_AT = RECORD + 3 * RIM
HALF = 16

PIECES = 32
GROUP = LANES // PIECES
CHUNK = 8
UNITS = EXT // CHUNK
PARTS = 2
NORMS = 3
KINDS = 3 * PARTS + NORMS
SRC = 128
ROWS = 128
COLS = 256
BF16 = jnp.bfloat16


def cheb_table():
    nodes = ((2.0 * np.arange(SAMP, dtype=np.float32) + 1.0) / SAMP - 1.0).astype(np.float32)
    columns = [np.ones_like(nodes), nodes]
    for _ in range(2, DEG1):
        columns.append((2.0 * nodes * columns[-1] - columns[-2]).astype(np.float32))
    return np.stack(columns, axis=1)


def rim_tables():
    table = cheb_table()
    return np.stack([table[:RIM], table[SAMP - RIM :]])


def synth_matrix():
    table = cheb_table()
    weights = np.zeros((3 * EXT, LANES), np.float32)
    for c in range(3):
        for s in range(RIM):
            weights[c * EXT + s, RIM_AT + RIM * c + s] = 1.0
        weights[c * EXT + RIM : (c + 1) * EXT, DEG1 * c : DEG1 * (c + 1)] = table
    return weights


def selection(left):
    one = KINDS
    uses = []
    for i in range(PARTS):
        for j in range(PARTS):
            for c in range(3):
                uses.append((3 * i + c, 1.0) if left else (3 * j + c, -1.0))
    for n in range(NORMS):
        uses.append((3 * PARTS + n, 1.0) if left else (one, 1.0))
    for n in range(NORMS):
        uses.append((one, 1.0) if left else (3 * PARTS + n, 1.0))
    matrix = np.zeros((CHUNK * PIECES, SRC), np.float32)
    for t in range(CHUNK):
        for k, (kind, value) in enumerate(uses):
            matrix[t * PIECES + k, kind * CHUNK + (0 if kind == one else t)] = value
    return matrix.astype(ml_dtypes.bfloat16)


def split(value, count):
    pieces = []
    for _ in range(count):
        piece = value.astype(BF16).astype(jnp.float32)
        value = value - piece
        pieces.append(piece)
    return pieces, value


def one_hot(row_ids, names):
    return jnp.where(row_ids == jnp.broadcast_to(names, row_ids.shape), 1.0, 0.0).astype(BF16)


def place_kernel(cell_ref, out_ref, count_ref):
    rows = out_ref.shape[0]
    count = cell_ref.shape[1]
    cell = cell_ref[...].astype(jnp.float32)
    column = jnp.transpose(jnp.broadcast_to(cell, (LANES, count)))
    lane = lax.broadcasted_iota(jnp.int32, (count, LANES), 1)
    for n in range(2):
        name = jnp.where((lane >= COUNT_AT) & (lane < COUNT_AT + HALF), lane - COUNT_AT + n * HALF, -1)
        named = jnp.where(column == name.astype(jnp.float32), 1.0, 0.0)
        count_ref[n : n + 1, :] = jnp.sum(named, axis=0, keepdims=True)
    column = jnp.concatenate([column] * (count // LANES), axis=1)
    before = lax.broadcasted_iota(jnp.int32, (count, count), 0) < lax.broadcasted_iota(jnp.int32, (count, count), 1)
    same = (column == jnp.broadcast_to(cell, (count, count))) & before
    rank = jnp.sum(jnp.where(same, 1.0, 0.0), axis=0, keepdims=True)
    early = jnp.where(rank < PACK, cell * PACK + rank, -1.0).astype(jnp.int32)
    late = jnp.where(rank < PACK, -1.0, cell * PACK + rank - PACK).astype(jnp.int32)
    ids = lax.broadcasted_iota(jnp.int32, (rows, count), 0)
    out_ref[:, 0:count] = one_hot(ids, early)
    out_ref[:, count : 2 * count] = one_hot(ids, late)
    out_ref[:, 2 * count : 3 * count] = one_hot(ids, jnp.where(late < 0, -1, late + LATE))


def placed(chosen, data):
    pieces = []
    for _ in range(3):
        piece = data.astype(BF16)
        data = data - piece.astype(jnp.float32)
        pieces.append(piece)
    found = jnp.dot(chosen, jnp.concatenate(pieces, axis=1), preferred_element_type=jnp.float32)
    return found[:, :LANES] + found[:, LANES : 2 * LANES] + found[:, 2 * LANES :]


def front_kernel(first_ref, own_ref, prev_ref, chosen_ref, count_ref, table_ref, out_ref, rows_ref):
    count = own_ref.shape[2]
    first = first_ref[0] == 0
    rows_ref[...] = jnp.zeros_like(rows_ref)
    table = jnp.where(first, table_ref[0], table_ref[1])
    for c in range(3):
        rows = slice(c * DEG1, (c + 1) * DEG1)
        own = own_ref[rows, 0, :]
        rows_ref[rows, :] = own
        source = jnp.where(first, own, prev_ref[rows, 0, :])
        rows_ref[RIM_AT + RIM * c : RIM_AT + RIM * (c + 1), :] = jnp.dot(
            table, source, precision=lax.Precision.HIGHEST, preferred_element_type=jnp.float32
        )
    rows_ref[FLAG_AT : FLAG_AT + 1, :] = jnp.ones((1, count), jnp.float32)
    data = jnp.transpose(rows_ref[...])
    lane = lax.broadcasted_iota(jnp.int32, data.shape, 1)
    late = jnp.where(lane >= RECORD, pltpu.roll(data, RECORD, 1), 0.0)
    rim = jnp.where((lane >= RECORD) & (lane < COUNT_AT), pltpu.roll(data, RECORD - RIM_AT, 1), 0.0)
    found = placed(chosen_ref[...], jnp.concatenate([data, late, rim], axis=0))
    row = lax.rem(lax.broadcasted_iota(jnp.int32, found.shape, 0), PACK)
    counts = jnp.where(lax.rem(row, 2) == 0, count_ref[0:1, :], count_ref[1:2, :])
    out_ref[...] = found + jnp.where(row >= LATE, counts, 0.0)


def plan(counts):
    rows = jnp.maximum(jnp.ceil(counts / ROWS), 1.0) * ROWS
    tiles = jnp.maximum(jnp.ceil(counts / COLS), 1.0)
    fixed, per_row = 11.0, 0.139
    alone = tiles * fixed + per_row * (
        jnp.minimum(rows, COLS)
        + jnp.where(tiles > 1.5, jnp.minimum(rows, 2 * COLS), 0.0)
        + jnp.where(tiles > 2.5, rows, 0.0)
    )
    after = lambda value: pltpu.roll(value, LANES - 1, 1)
    ahead = lambda value: pltpu.roll(value, 1, 1)
    here = after(tiles) * (fixed + per_row * rows)
    there = tiles * (fixed + per_row * after(rows))
    share = jnp.full_like(counts, 0.5)
    for _ in range(6):
        load = alone + share * here + ahead((1.0 - share) * there)
        share = jnp.clip(share + 0.8 * (after(load) - load) / (here + there), 0.0, 1.0)
    return jnp.floor(share * UNITS + 0.5)


def records(packed):
    tiles = packed.reshape(packed.shape[0] // PACK, 2, LATE, LANES)
    blocks = tiles.shape[0]
    flat = (blocks * LATE, LANES)
    low, high = tiles[:, 0].reshape(flat), tiles[:, 1].reshape(flat)
    lane = lax.broadcasted_iota(jnp.int32, flat, 1)
    late = jnp.where(
        lane < RIM_AT,
        pltpu.roll(low, LANES - RECORD, 1),
        jnp.where(lane < RECORD, pltpu.roll(high, LANES - (RECORD - RIM_AT), 1), 0.0),
    )
    each = [v.reshape(blocks, 1, LATE, LANES) for v in (low, high, late)]
    return jnp.concatenate(each, axis=1).reshape(blocks * CAP, LANES), high


def cell_counts(high):
    row = lax.rem(lax.broadcasted_iota(jnp.int32, high.shape, 0), 2)
    lane = lax.broadcasted_iota(jnp.int32, high.shape, 1)
    held = jnp.where((lane >= COUNT_AT) & (lane < COUNT_AT + HALF), high, 0.0)
    total = None
    for n in range(2):
        part = jnp.sum(jnp.where(row == n, held, 0.0), axis=0, keepdims=True) * (2.0 / LATE)
        part = pltpu.roll(part, (n * HALF - COUNT_AT) % LANES, 1)
        total = part if total is None else total + part
    total = total + pltpu.roll(total, 2 * HALF, 1)
    return total + pltpu.roll(total, 4 * HALF, 1)


def compact_kernel(packed_ref, live_ref, chosen_ref, plan_ref):
    data, high = records(packed_ref[...])
    slots = data.shape[0]
    flag = jnp.transpose(data)[FLAG_AT : FLAG_AT + 1, :]
    first = lax.broadcasted_iota(jnp.int32, (slots, slots), 0)
    second = lax.broadcasted_iota(jnp.int32, (slots, slots), 1)
    before = jnp.where(first < second, 1.0, 0.0).astype(BF16)
    flags = jnp.broadcast_to(flag, (16, slots)).astype(BF16)
    place = jnp.dot(flags, before, preferred_element_type=jnp.float32)[0:1]
    place = jnp.where(flag > 0.5, place, -1.0).astype(jnp.int32)
    chosen = one_hot(first, place)
    chosen_ref[...] = chosen
    live_ref[...] = placed(chosen, data)
    counts = cell_counts(high)
    plan_ref[0:1, :] = counts
    plan_ref[1:2, :] = plan(counts)


def fetched(sources, targets, sem):
    copies = [pltpu.make_async_copy(s, t, sem.at[i]) for i, (s, t) in enumerate(zip(sources, targets))]
    for copy in copies:
        copy.start()
    return copies


def tracks(live_ref, synth_ref, track_ref, flag_ref, copies):
    live = jnp.transpose(live_ref[...])
    flag_ref[...] = jnp.broadcast_to(live[FLAG_AT : FLAG_AT + 1, :], flag_ref.shape)
    for copy in copies:
        copy.wait()
    track = jnp.dot(synth_ref[...], live, precision=lax.Precision.HIGHEST, preferred_element_type=jnp.float32)
    track_ref[...] = track.reshape(track_ref.shape)


def source_of(track_ref, flag_ref, unit):
    count = track_ref.shape[3]
    parts, norm = [], None
    for c in range(3):
        axis = track_ref[c, unit]
        pieces, rest = split(axis, PARTS)
        parts.append(pieces)
        held = axis - rest
        norm = held * held if norm is None else norm + held * held
    norm = jnp.where(flag_ref[...] > 0.5, 0.5 * norm, FAR)
    kinds = [parts[c][i] for i in range(PARTS) for c in range(3)] + split(norm, NORMS)[0]
    ones = jnp.ones((CHUNK, count), jnp.float32)
    zeros = jnp.zeros((SRC - (KINDS + 1) * CHUNK, count), jnp.float32)
    return jnp.concatenate(kinds + [ones, zeros], axis=0)


def put_right(source, right_sel_ref, right_ref, unit):
    right = jnp.dot(right_sel_ref[...], source.astype(BF16), preferred_element_type=jnp.float32)
    right_ref[pl.ds(unit * CHUNK, CHUNK)] = right.astype(BF16).reshape(CHUNK, PIECES, right.shape[1])


def put_left(source, left_sel_ref, left_ref, unit):
    left = jnp.dot(jnp.transpose(source).astype(BF16), left_sel_ref[...], preferred_element_type=jnp.float32)
    left = left.astype(BF16)
    for g in range(CHUNK // GROUP):
        left_ref[unit * (CHUNK // GROUP) + g] = left[:, g * LANES : (g + 1) * LANES]


def sweep(left_ref, right_ref, acc_ref, row_tiles, col_start, first, last):
    acc_ref[...] = jnp.full_like(acc_ref, CLIP)
    for n in range(1, acc_ref.shape[0] // ROWS + 1):

        @pl.when(row_tiles == n)
        def _(rows=n * ROWS):
            def step(unit, carry):
                best = acc_ref[0:rows, :]
                for h in range(CHUNK // GROUP):
                    g = unit * (CHUNK // GROUP) + h
                    left = left_ref[g, 0:rows, :]
                    for j in range(GROUP):
                        parts = [right_ref[g * GROUP + j, :, pl.ds(col_start, COLS)]]
                        if j > 0:
                            parts = [jnp.zeros((PIECES * j, COLS), BF16)] + parts
                        if j < GROUP - 1:
                            parts = parts + [jnp.zeros((PIECES * (GROUP - 1 - j), COLS), BF16)]
                        weights = jnp.concatenate(parts, axis=0)
                        best = jnp.minimum(best, jnp.dot(left, weights, preferred_element_type=jnp.float32))
                acc_ref[0:rows, :] = best
                return carry

            lax.fori_loop(first, last, step, 0)


def fold(acc_ref, row_ref):
    acc = acc_ref[...]
    row_ref[...] = jnp.minimum(row_ref[...], jnp.minimum(acc[:, :LANES], acc[:, LANES:]))
    return jnp.min(acc, axis=0, keepdims=True)


def by_row(row_ref):
    return finished(jnp.min(jnp.transpose(row_ref[...]), axis=0, keepdims=True))


def finished(half):
    return jnp.clip(2.0 * half, 0.0, CLIP)


def planned(plan_ref, row, cell, cells):
    lane = lax.broadcasted_iota(jnp.int32, (1, LANES), 1)
    value = jnp.sum(jnp.where(lane == lax.rem(cell, cells), plan_ref[row : row + 1, :], 0.0))
    return value.astype(jnp.int32)


def tiles_of(count, size):
    return jnp.maximum((count + (size - 1)) // size, 1)


def prepare_kernel(
    live_ref, synth_hbm, left_sel_hbm, right_sel_hbm, left_ref, right_ref,
    synth_ref, left_sel_ref, right_sel_ref, track_ref, flag_ref, sem,
):
    copies = fetched((synth_hbm, left_sel_hbm, right_sel_hbm), (synth_ref, left_sel_ref, right_sel_ref), sem)
    tracks(live_ref, synth_ref, track_ref, flag_ref, copies)
    for unit in range(UNITS):
        source = source_of(track_ref, flag_ref, unit)
        put_right(source, right_sel_ref, right_ref, unit)
        put_left(source, left_sel_ref, left_ref, unit)


def cross_kernel(
    ahead, cells, cell_ref, plan_ref, left_ref, live_ref, base_ref, synth_hbm, right_sel_hbm, row_out_ref, col_out_ref,
    right_ref, acc_ref, row_ref, synth_ref, right_sel_ref, track_ref, flag_ref, sem,
):
    copies = fetched((synth_hbm, right_sel_hbm), (synth_ref, right_sel_ref), sem)
    cell = cell_ref[0]
    other = cell + 1 if ahead else cell + (cells - 1)
    bound = planned(plan_ref, 1, cell if ahead else other, cells)
    first, last = (0, bound) if ahead else (bound, UNITS)
    row_tiles = tiles_of(planned(plan_ref, 0, cell, cells), ROWS)
    col_tiles = tiles_of(planned(plan_ref, 0, other, cells), COLS)

    for copy in copies:
        copy.wait()

    @pl.when(first < last)
    def _():
        tracks(live_ref, synth_ref, track_ref, flag_ref, ())

        def unit_step(unit, carry):
            put_right(source_of(track_ref, flag_ref, unit), right_sel_ref, right_ref, unit)
            return carry

        lax.fori_loop(first, last, unit_step, 0)

    row_ref[...] = jnp.full_like(row_ref, CLIP)
    col_out_ref[...] = jnp.full_like(col_out_ref, CLIP)

    def column(n, carry):
        start = pl.multiple_of(n * COLS, COLS)
        sweep(left_ref, right_ref, acc_ref, row_tiles, start, first, last)
        col_out_ref[:, pl.ds(start, COLS)] = finished(fold(acc_ref, row_ref))
        return carry

    lax.fori_loop(0, jnp.where(first < last, col_tiles, 0), column, 0)
    row_out_ref[...] = jnp.minimum(by_row(row_ref), base_ref[...])


def self_kernel(cells, cell_ref, plan_ref, left_ref, right_ref, out_ref, acc_ref, row_ref, col_ref):
    count = planned(plan_ref, 0, cell_ref[0], cells)
    row_tiles = tiles_of(count, ROWS)
    row_ref[...] = jnp.full_like(row_ref, CLIP)
    col_ref[...] = jnp.full_like(col_ref, CLIP)
    same = lax.broadcasted_iota(jnp.int32, (COLS, COLS), 0) == lax.broadcasted_iota(jnp.int32, (COLS, COLS), 1)

    def column(n, carry):
        start = pl.multiple_of(n * COLS, COLS)
        sweep(left_ref, right_ref, acc_ref, jnp.minimum(row_tiles, (n + 1) * (COLS // ROWS)), start, 0, UNITS)
        acc_ref[pl.ds(start, COLS), :] = jnp.where(same, CLIP, acc_ref[pl.ds(start, COLS), :])
        col_ref[:, pl.ds(start, COLS)] = finished(fold(acc_ref, row_ref))
        return carry

    lax.fori_loop(0, tiles_of(count, COLS), column, 0)
    out_ref[...] = jnp.minimum(by_row(row_ref), col_ref[...])


def restore_kernel(*refs):
    *minima, chosen_ref, out_ref = refs
    count = out_ref.shape[1]
    best = functools.reduce(jnp.minimum, [ref[...] for ref in minima])
    pieces = split(best, 3)[0]
    ones, zeros = jnp.ones((1, count), jnp.float32), jnp.zeros((12, count), jnp.float32)
    rows = jnp.concatenate(pieces + [ones, zeros], axis=0).astype(BF16)
    found = jnp.dot(rows, chosen_ref[...], preferred_element_type=jnp.float32)
    value = found[0:1] + found[1:2] + found[2:3]
    out_ref[...] = jnp.where(found[3:4] > 0.5, value, CLIP)


VMEM = pl.BlockSpec(memory_space=pltpu.VMEM)
SMEM = pl.BlockSpec(memory_space=pltpu.SMEM)
ANY = pl.BlockSpec(memory_space=pl.ANY)


def call(kernel, name, out_shape, in_specs, scratch, vmem, flops):
    return pl.pallas_call(
        kernel,
        out_shape=out_shape,
        in_specs=in_specs,
        out_specs=jax.tree.map(lambda _: VMEM, out_shape),
        scratch_shapes=scratch,
        compiler_params=pltpu.CompilerParams(vmem_limit_bytes=vmem << 20),
        cost_estimate=pl.CostEstimate(flops=flops, bytes_accessed=4_000_000, transcendentals=0),
        name=name,
    )


def body(cheb_coef, obj_cell):
    objects = cheb_coef.shape[3]
    own = cheb_coef.reshape(3 * DEG1, 1, objects)
    cells = lax.axis_size("cell")
    slots = cells * CAP
    windows = lax.axis_size("tm")
    window = lax.axis_index("tm").astype(jnp.int32).reshape(1)
    prev = lax.ppermute(own, "tm", [(i, i + 1) for i in range(windows - 1)])
    row = jax.ShapeDtypeStruct((1, slots), jnp.float32)
    cell = lax.axis_index("cell").astype(jnp.int32).reshape(1)
    wide = jax.ShapeDtypeStruct((slots, LANES), jnp.float32)
    chosen, counts = call(
        place_kernel,
        "place",
        (jax.ShapeDtypeStruct((cells * PACK, 3 * objects), BF16), jax.ShapeDtypeStruct((8, LANES), jnp.float32)),
        [VMEM],
        [],
        8,
        2_000_000_000,
    )(obj_cell.reshape(1, objects))
    send = call(
        front_kernel,
        "front",
        jax.ShapeDtypeStruct((cells * PACK, LANES), jnp.float32),
        [SMEM] + [VMEM] * 5,
        [pltpu.VMEM((LANES, objects), jnp.float32)],
        8,
        2_000_000_000,
    )(window, own, prev, chosen, counts, jnp.asarray(rim_tables()))
    packed = lax.all_to_all(send, "cell", split_axis=0, concat_axis=0, tiled=True)
    live, chosen, shares = call(
        compact_kernel,
        "compact",
        (wide, jax.ShapeDtypeStruct((slots, slots), BF16), jax.ShapeDtypeStruct((8, LANES), jnp.float32)),
        [VMEM],
        [],
        16,
        2_000_000_000,
    )(packed)
    forward = [(i, (i + 1) % cells) for i in range(cells)]
    backward = [((i + 1) % cells, i) for i in range(cells)]
    next_live = lax.ppermute(live, "cell", backward)
    prev_live = lax.ppermute(live, "cell", forward)
    synth = jnp.asarray(synth_matrix())
    left_sel = jnp.asarray(np.ascontiguousarray(selection(True).T))
    right_sel = jnp.asarray(selection(False))
    left_shape = jax.ShapeDtypeStruct((EXT // GROUP, slots, LANES), BF16)
    right_shape = jax.ShapeDtypeStruct((EXT, PIECES, slots), BF16)
    synth_scratch = pltpu.VMEM(synth.shape, jnp.float32)
    left_sel_scratch = pltpu.VMEM(left_sel.shape, BF16)
    right_sel_scratch = pltpu.VMEM(right_sel.shape, BF16)
    track_scratch = [pltpu.VMEM((3, UNITS, CHUNK, slots), jnp.float32), pltpu.VMEM((CHUNK, slots), jnp.float32)]
    minima = [pltpu.VMEM((slots, COLS), jnp.float32), pltpu.VMEM((slots, LANES), jnp.float32)]
    left, right = call(
        prepare_kernel,
        "prepare",
        (left_shape, right_shape),
        [VMEM, ANY, ANY, ANY],
        [synth_scratch, left_sel_scratch, right_sel_scratch] + track_scratch + [pltpu.SemaphoreType.DMA((3,))],
        24,
        6_000_000_000,
    )(live, synth, left_sel, right_sel)

    def cross(ahead, other, base):
        return call(
            functools.partial(cross_kernel, ahead, cells),
            "cross_next" if ahead else "cross_prev",
            (row, row),
            [SMEM] + [VMEM] * 4 + [ANY, ANY],
            [pltpu.VMEM(right_shape.shape, BF16)]
            + minima
            + [synth_scratch, right_sel_scratch]
            + track_scratch
            + [pltpu.SemaphoreType.DMA((2,))],
            32,
            12_000_000_000,
        )(cell, shares, left, other, base, synth, right_sel)

    own_min = call(
        functools.partial(self_kernel, cells),
        "self_screen",
        row,
        [SMEM] + [VMEM] * 3,
        minima + [pltpu.VMEM((1, slots), jnp.float32)],
        24,
        15_000_000_000,
    )(cell, shares, left, right)
    best, next_col = cross(True, next_live, own_min)
    best, prev_col = cross(False, prev_live, best)
    best, next_col, prev_col = lax.optimization_barrier((best, next_col, prev_col))
    from_prev = lax.ppermute(next_col, "cell", forward)
    from_next = lax.ppermute(prev_col, "cell", backward)
    return call(restore_kernel, "restore", row, [VMEM] * 4, [], 8, 100_000_000)(best, from_prev, from_next, chosen)


def solution(mesh):
    in_specs = (P("tm", None, None, "cell"), P("tm", "cell", None))
    return jax.shard_map(body, mesh=mesh, in_specs=in_specs, out_specs=P("tm", "cell"), check_vma=False)
```

```python
import functools

import jax
import jax.numpy as jnp
import ml_dtypes
import numpy as np
from jax import lax
from jax.experimental import pallas as pl
from jax.experimental.pallas import tpu as pltpu
from jax.sharding import PartitionSpec as P

DEG1 = 17
SAMP = 64
RIM = 8
CAP = 24
EXT = SAMP + RIM
CLIP = 25.0
FAR = 1.0e9

LANES = 128
FLAG_AT = 3 * DEG1
RIM_AT = FLAG_AT + 1
RECORD = RIM_AT + 3 * RIM
PACK = 16
LATE = CAP - PACK
COUNT_AT = RECORD + 3 * RIM
HALF = 16

PIECES = 32
GROUP = LANES // PIECES
CHUNK = 8
UNITS = EXT // CHUNK
PARTS = 2
NORMS = 3
KINDS = 3 * PARTS + NORMS
SRC = 128
ROWS = 128
COLS = 256
BF16 = jnp.bfloat16


def cheb_table():
    nodes = ((2.0 * np.arange(SAMP, dtype=np.float32) + 1.0) / SAMP - 1.0).astype(np.float32)
    columns = [np.ones_like(nodes), nodes]
    for _ in range(2, DEG1):
        columns.append((2.0 * nodes * columns[-1] - columns[-2]).astype(np.float32))
    return np.stack(columns, axis=1)


def rim_tables():
    table = cheb_table()
    return np.stack([table[:RIM], table[SAMP - RIM :]])


def synth_matrix():
    table = cheb_table()
    weights = np.zeros((3 * EXT, LANES), np.float32)
    for c in range(3):
        for s in range(RIM):
            weights[c * EXT + s, RIM_AT + RIM * c + s] = 1.0
        weights[c * EXT + RIM : (c + 1) * EXT, DEG1 * c : DEG1 * (c + 1)] = table
    return weights


def selection(left):
    one = KINDS
    uses = []
    for i in range(PARTS):
        for j in range(PARTS):
            for c in range(3):
                uses.append((3 * i + c, 1.0) if left else (3 * j + c, -1.0))
    for n in range(NORMS):
        uses.append((3 * PARTS + n, 1.0) if left else (one, 1.0))
    for n in range(NORMS):
        uses.append((one, 1.0) if left else (3 * PARTS + n, 1.0))
    matrix = np.zeros((CHUNK * PIECES, SRC), np.float32)
    for t in range(CHUNK):
        for k, (kind, value) in enumerate(uses):
            matrix[t * PIECES + k, kind * CHUNK + (0 if kind == one else t)] = value
    return matrix.astype(ml_dtypes.bfloat16)


def split(value, count):
    pieces = []
    for _ in range(count):
        piece = value.astype(BF16).astype(jnp.float32)
        value = value - piece
        pieces.append(piece)
    return pieces, value


def one_hot(row_ids, names):
    return jnp.where(row_ids == jnp.broadcast_to(names, row_ids.shape), 1.0, 0.0).astype(BF16)


def place_kernel(cell_ref, out_ref, count_ref):
    rows = out_ref.shape[0]
    count = cell_ref.shape[1]
    cell = cell_ref[...].astype(jnp.float32)
    column = jnp.transpose(jnp.broadcast_to(cell, (LANES, count)))
    lane = lax.broadcasted_iota(jnp.int32, (count, LANES), 1)
    for n in range(2):
        name = jnp.where((lane >= COUNT_AT) & (lane < COUNT_AT + HALF), lane - COUNT_AT + n * HALF, -1)
        named = jnp.where(column == name.astype(jnp.float32), 1.0, 0.0)
        count_ref[n : n + 1, :] = jnp.sum(named, axis=0, keepdims=True)
    column = jnp.concatenate([column] * (count // LANES), axis=1)
    before = lax.broadcasted_iota(jnp.int32, (count, count), 0) < lax.broadcasted_iota(jnp.int32, (count, count), 1)
    same = (column == jnp.broadcast_to(cell, (count, count))) & before
    rank = jnp.sum(jnp.where(same, 1.0, 0.0), axis=0, keepdims=True)
    early = jnp.where(rank < PACK, cell * PACK + rank, -1.0).astype(jnp.int32)
    late = jnp.where(rank < PACK, -1.0, cell * PACK + rank - PACK).astype(jnp.int32)
    ids = lax.broadcasted_iota(jnp.int32, (rows, count), 0)
    out_ref[:, 0:count] = one_hot(ids, early)
    out_ref[:, count : 2 * count] = one_hot(ids, late)
    out_ref[:, 2 * count : 3 * count] = one_hot(ids, jnp.where(late < 0, -1, late + LATE))


def placed(chosen, data):
    pieces = []
    for _ in range(3):
        piece = data.astype(BF16)
        data = data - piece.astype(jnp.float32)
        pieces.append(piece)
    found = jnp.dot(chosen, jnp.concatenate(pieces, axis=1), preferred_element_type=jnp.float32)
    return found[:, :LANES] + found[:, LANES : 2 * LANES] + found[:, 2 * LANES :]


def front_kernel(first_ref, own_ref, prev_ref, chosen_ref, count_ref, table_ref, out_ref, rows_ref):
    count = own_ref.shape[2]
    first = first_ref[0] == 0
    rows_ref[...] = jnp.zeros_like(rows_ref)
    table = jnp.where(first, table_ref[0], table_ref[1])
    for c in range(3):
        rows = slice(c * DEG1, (c + 1) * DEG1)
        own = own_ref[rows, 0, :]
        rows_ref[rows, :] = own
        source = jnp.where(first, own, prev_ref[rows, 0, :])
        rows_ref[RIM_AT + RIM * c : RIM_AT + RIM * (c + 1), :] = jnp.dot(
            table, source, precision=lax.Precision.HIGHEST, preferred_element_type=jnp.float32
        )
    rows_ref[FLAG_AT : FLAG_AT + 1, :] = jnp.ones((1, count), jnp.float32)
    data = jnp.transpose(rows_ref[...])
    lane = lax.broadcasted_iota(jnp.int32, data.shape, 1)
    late = jnp.where(lane >= RECORD, pltpu.roll(data, RECORD, 1), 0.0)
    rim = jnp.where((lane >= RECORD) & (lane < COUNT_AT), pltpu.roll(data, RECORD - RIM_AT, 1), 0.0)
    found = placed(chosen_ref[...], jnp.concatenate([data, late, rim], axis=0))
    row = lax.rem(lax.broadcasted_iota(jnp.int32, found.shape, 0), PACK)
    counts = jnp.where(lax.rem(row, 2) == 0, count_ref[0:1, :], count_ref[1:2, :])
    out_ref[...] = found + jnp.where(row >= LATE, counts, 0.0)


def plan(counts):
    rows = jnp.maximum(jnp.ceil(counts / ROWS), 1.0) * ROWS
    tiles = jnp.maximum(jnp.ceil(counts / COLS), 1.0)
    fixed, per_row, extra, least = 11.0, 0.139, 22.0, 28.0
    alone = tiles * fixed + per_row * (
        jnp.minimum(rows, COLS)
        + jnp.where(tiles > 1.5, jnp.minimum(rows, 2 * COLS), 0.0)
        + jnp.where(tiles > 2.5, rows, 0.0)
    )
    after = lambda value: pltpu.roll(value, LANES - 1, 1)
    ahead = lambda value: pltpu.roll(value, 1, 1)
    here = after(tiles) * (fixed + per_row * rows) + extra
    there = tiles * (fixed + per_row * after(rows)) + extra
    lent = 1.15 * alone
    cross_step, self_step = 0.5 / (here + there), 0.15 / alone
    share, before, behind = jnp.full_like(counts, 0.5), jnp.zeros_like(counts), jnp.zeros_like(counts)
    for _ in range(16):
        load = (
            alone * (1.0 - before - behind)
            + share * here
            + ahead((1.0 - share) * there + behind * lent)
            + after(before * lent)
        )
        up, down = after(load) - load, load - ahead(load)
        share = jnp.clip(share + cross_step * up, 0.0, 1.0)
        before = jnp.clip(before + self_step * (down - least), 0.0, 0.45)
        behind = jnp.clip(behind - self_step * (up + least), 0.0, 0.45)
    return [jnp.floor(value * UNITS + 0.5) for value in (share, before, behind)]


def records(packed):
    tiles = packed.reshape(packed.shape[0] // PACK, 2, LATE, LANES)
    blocks = tiles.shape[0]
    flat = (blocks * LATE, LANES)
    low, high = tiles[:, 0].reshape(flat), tiles[:, 1].reshape(flat)
    lane = lax.broadcasted_iota(jnp.int32, flat, 1)
    late = jnp.where(
        lane < RIM_AT,
        pltpu.roll(low, LANES - RECORD, 1),
        jnp.where(lane < RECORD, pltpu.roll(high, LANES - (RECORD - RIM_AT), 1), 0.0),
    )
    each = [v.reshape(blocks, 1, LATE, LANES) for v in (low, high, late)]
    return jnp.concatenate(each, axis=1).reshape(blocks * CAP, LANES), high


def cell_counts(high):
    row = lax.rem(lax.broadcasted_iota(jnp.int32, high.shape, 0), 2)
    lane = lax.broadcasted_iota(jnp.int32, high.shape, 1)
    held = jnp.where((lane >= COUNT_AT) & (lane < COUNT_AT + HALF), high, 0.0)
    total = None
    for n in range(2):
        part = jnp.sum(jnp.where(row == n, held, 0.0), axis=0, keepdims=True) * (2.0 / LATE)
        part = pltpu.roll(part, (n * HALF - COUNT_AT) % LANES, 1)
        total = part if total is None else total + part
    total = total + pltpu.roll(total, 2 * HALF, 1)
    return total + pltpu.roll(total, 4 * HALF, 1)


def compact_kernel(packed_ref, live_ref, chosen_ref, count_ref):
    data, high = records(packed_ref[...])
    slots = data.shape[0]
    flag = jnp.transpose(data)[FLAG_AT : FLAG_AT + 1, :]
    first = lax.broadcasted_iota(jnp.int32, (slots, slots), 0)
    second = lax.broadcasted_iota(jnp.int32, (slots, slots), 1)
    before = jnp.where(first < second, 1.0, 0.0).astype(BF16)
    flags = jnp.broadcast_to(flag, (16, slots)).astype(BF16)
    place = jnp.dot(flags, before, preferred_element_type=jnp.float32)[0:1]
    place = jnp.where(flag > 0.5, place, -1.0).astype(jnp.int32)
    chosen = one_hot(first, place)
    chosen_ref[...] = chosen
    live_ref[...] = placed(chosen, data)
    count_ref[...] = cell_counts(high)


def fetched(sources, targets, sem):
    copies = [pltpu.make_async_copy(s, t, sem.at[i]) for i, (s, t) in enumerate(zip(sources, targets))]
    for copy in copies:
        copy.start()
    return copies


def tracks(live_ref, synth_ref, track_ref, flag_ref, copies):
    live = jnp.transpose(live_ref[...])
    flag_ref[...] = jnp.broadcast_to(live[FLAG_AT : FLAG_AT + 1, :], flag_ref.shape)
    for copy in copies:
        copy.wait()
    track = jnp.dot(synth_ref[...], live, precision=lax.Precision.HIGHEST, preferred_element_type=jnp.float32)
    track_ref[...] = track.reshape(track_ref.shape)


def source_of(track_ref, flag_ref, unit):
    count = track_ref.shape[3]
    parts, norm = [], None
    for c in range(3):
        axis = track_ref[c, unit]
        pieces, rest = split(axis, PARTS)
        parts.append(pieces)
        held = axis - rest
        norm = held * held if norm is None else norm + held * held
    norm = jnp.where(flag_ref[...] > 0.5, 0.5 * norm, FAR)
    kinds = [parts[c][i] for i in range(PARTS) for c in range(3)] + split(norm, NORMS)[0]
    ones = jnp.ones((CHUNK, count), jnp.float32)
    zeros = jnp.zeros((SRC - (KINDS + 1) * CHUNK, count), jnp.float32)
    return jnp.concatenate(kinds + [ones, zeros], axis=0)


def put_right(source, right_sel_ref, right_ref, unit):
    right = jnp.dot(right_sel_ref[...], source.astype(BF16), preferred_element_type=jnp.float32)
    right_ref[pl.ds(unit * CHUNK, CHUNK)] = right.astype(BF16).reshape(CHUNK, PIECES, right.shape[1])


def put_left(source, left_sel_ref, left_ref, unit, offset):
    left = jnp.dot(jnp.transpose(source).astype(BF16), left_sel_ref[...], preferred_element_type=jnp.float32)
    left = left.astype(BF16)
    for g in range(CHUNK // GROUP):
        left_ref[offset + unit * (CHUNK // GROUP) + g] = left[:, g * LANES : (g + 1) * LANES]


def sweep(left_ref, offset, right_ref, acc_ref, row_tiles, col_start, first, last):
    acc_ref[...] = jnp.full_like(acc_ref, CLIP)
    for n in range(1, acc_ref.shape[0] // ROWS + 1):

        @pl.when(row_tiles == n)
        def _(rows=n * ROWS):
            def step(unit, carry):
                best = acc_ref[0:rows, :]
                for h in range(CHUNK // GROUP):
                    g = unit * (CHUNK // GROUP) + h
                    left = left_ref[offset + g, 0:rows, :]
                    for j in range(GROUP):
                        parts = [right_ref[g * GROUP + j, :, pl.ds(col_start, COLS)]]
                        if j > 0:
                            parts = [jnp.zeros((PIECES * j, COLS), BF16)] + parts
                        if j < GROUP - 1:
                            parts = parts + [jnp.zeros((PIECES * (GROUP - 1 - j), COLS), BF16)]
                        weights = jnp.concatenate(parts, axis=0)
                        best = jnp.minimum(best, jnp.dot(left, weights, preferred_element_type=jnp.float32))
                acc_ref[0:rows, :] = best
                return carry

            lax.fori_loop(first, last, step, 0)


def fold(acc_ref, row_ref, job):
    acc = acc_ref[...]
    row_ref[job] = jnp.minimum(row_ref[job], jnp.minimum(acc[:, :LANES], acc[:, LANES:]))
    return finished(jnp.min(acc, axis=0, keepdims=True))


def drop_diagonal(acc_ref, start, active):
    same = lax.broadcasted_iota(jnp.int32, (COLS, COLS), 0) == lax.broadcasted_iota(jnp.int32, (COLS, COLS), 1)
    acc_ref[pl.ds(start, COLS), :] = jnp.where(same & active, CLIP, acc_ref[pl.ds(start, COLS), :])


def by_row(row_ref, job):
    return finished(jnp.min(jnp.transpose(row_ref[job]), axis=0, keepdims=True))


def finished(half):
    return jnp.clip(2.0 * half, 0.0, CLIP)


def planned(plan_ref, row, cell, cells):
    lane = lax.broadcasted_iota(jnp.int32, (1, LANES), 1)
    value = jnp.sum(jnp.where(lane == lax.rem(cell, cells), plan_ref[row : row + 1, :], 0.0))
    return value.astype(jnp.int32)


def tiles_of(count, size):
    return jnp.maximum((count + (size - 1)) // size, 1)


def self_kernel(
    cells, cell_ref, live_ref, count_ref, synth_hbm, left_sel_hbm, right_sel_hbm, out_ref, left_ref, plan_ref,
    right_ref, acc_ref, row_ref, col_ref, synth_ref, left_sel_ref, right_sel_ref, track_ref, flag_ref, sem,
):
    copies = fetched((synth_hbm, left_sel_hbm, right_sel_hbm), (synth_ref, left_sel_ref, right_sel_ref), sem)
    tracks(live_ref, synth_ref, track_ref, flag_ref, copies)
    counts = count_ref[...]
    plan_ref[0:1, :] = counts
    for n, units in enumerate(plan(counts)):
        plan_ref[n + 1 : n + 2, :] = units
    for unit in range(UNITS):
        source = source_of(track_ref, flag_ref, unit)
        put_right(source, right_sel_ref, right_ref, unit)
        put_left(source, left_sel_ref, left_ref, unit, 0)
    cell = cell_ref[0]
    count = planned(plan_ref, 0, cell, cells)
    first, last = planned(plan_ref, 2, cell, cells), UNITS - planned(plan_ref, 3, cell, cells)
    row_tiles = tiles_of(count, ROWS)
    row_ref[...] = jnp.full_like(row_ref, CLIP)
    col_ref[...] = jnp.full_like(col_ref, CLIP)

    def column(n, carry):
        start = pl.multiple_of(n * COLS, COLS)
        limit = jnp.minimum(row_tiles, (n + 1) * (COLS // ROWS))
        sweep(left_ref, 0, right_ref, acc_ref, limit, start, first, last)
        drop_diagonal(acc_ref, start, True)
        col_ref[:, pl.ds(start, COLS)] = fold(acc_ref, row_ref, 0)
        return carry

    lax.fori_loop(0, tiles_of(count, COLS), column, 0)
    out_ref[...] = jnp.minimum(by_row(row_ref, 0), col_ref[...])


def neighbour_kernel(
    cells, cell_ref, plan_ref, next_ref, prev_ref, base_ref, left_in_ref, synth_hbm, left_sel_hbm, right_sel_hbm,
    out_ref, next_out_ref, prev_out_ref, left_ref,
    right_ref, acc_ref, row_ref, col_ref, synth_ref, left_sel_ref, right_sel_ref, track_ref, flag_ref, sem,
):
    del left_in_ref
    copies = fetched((synth_hbm, left_sel_hbm, right_sel_hbm), (synth_ref, left_sel_ref, right_sel_ref), sem)
    cell = cell_ref[0]
    after, ahead = cell + 1, cell + (cells - 1)
    own_rows = tiles_of(planned(plan_ref, 0, cell, cells), ROWS)
    own_share, their_share = planned(plan_ref, 1, cell, cells), planned(plan_ref, 1, ahead, cells)
    of_next, of_prev = planned(plan_ref, 2, after, cells), planned(plan_ref, 3, ahead, cells)
    next_count, prev_count = planned(plan_ref, 0, after, cells), planned(plan_ref, 0, ahead, cells)
    offset = left_ref.shape[0] // 2
    for copy in copies:
        copy.wait()
    row_ref[0] = jnp.full(row_ref.shape[1:], CLIP, jnp.float32)

    def phase(p, carry):
        forward = p == 0
        cross = jnp.where(forward, 0, their_share), jnp.where(forward, own_share, UNITS)
        alone = jnp.where(forward, 0, UNITS - of_prev), jnp.where(forward, of_next, UNITS)
        cross_on, alone_on = cross[0] < cross[1], alone[0] < alone[1]
        first = jnp.minimum(cross[0], alone[0])
        last = jnp.maximum(cross[1], alone[1])
        count = jnp.where(forward, next_count, prev_count)
        other_rows, other_cols = tiles_of(count, ROWS), tiles_of(count, COLS)

        @pl.when(forward & (first < last))
        def _():
            tracks(next_ref, synth_ref, track_ref, flag_ref, ())

        @pl.when((p == 1) & (first < last))
        def _():
            tracks(prev_ref, synth_ref, track_ref, flag_ref, ())

        def unit_step(unit, c):
            source = source_of(track_ref, flag_ref, unit)
            put_right(source, right_sel_ref, right_ref, unit)

            @pl.when((unit >= alone[0]) & (unit < alone[1]))
            def _():
                put_left(source, left_sel_ref, left_ref, unit, offset)

            return c

        lax.fori_loop(first, last, unit_step, 0)
        row_ref[1] = jnp.full(row_ref.shape[1:], CLIP, jnp.float32)
        col_ref[...] = jnp.full_like(col_ref, CLIP)

        def column(k, c):
            job = jnp.where(k < other_cols, 0, 1)
            n = k - job * other_cols
            start = pl.multiple_of(n * COLS, COLS)
            limit = jnp.where(job == 0, own_rows, jnp.minimum(other_rows, (n + 1) * (COLS // ROWS)))
            low, high = jnp.where(job == 0, cross[0], alone[0]), jnp.where(job == 0, cross[1], alone[1])
            sweep(left_ref, job * offset, right_ref, acc_ref, limit, start, low, high)
            drop_diagonal(acc_ref, start, job == 1)
            col_ref[:, pl.ds(start, COLS)] = jnp.minimum(col_ref[:, pl.ds(start, COLS)], fold(acc_ref, row_ref, job))
            return c

        lax.fori_loop(
            jnp.where(cross_on, 0, other_cols), jnp.where(alone_on, 2 * other_cols, other_cols), column, 0
        )
        best = jnp.minimum(col_ref[...], by_row(row_ref, 1))

        @pl.when(forward)
        def _():
            next_out_ref[...] = best

        @pl.when(p == 1)
        def _():
            prev_out_ref[...] = best

        return carry

    lax.fori_loop(0, 2, phase, 0)
    out_ref[...] = jnp.minimum(by_row(row_ref, 0), base_ref[...])


def restore_kernel(*refs):
    *minima, chosen_ref, out_ref = refs
    count = out_ref.shape[1]
    best = functools.reduce(jnp.minimum, [ref[...] for ref in minima])
    pieces = split(best, 3)[0]
    ones, zeros = jnp.ones((1, count), jnp.float32), jnp.zeros((12, count), jnp.float32)
    rows = jnp.concatenate(pieces + [ones, zeros], axis=0).astype(BF16)
    found = jnp.dot(rows, chosen_ref[...], preferred_element_type=jnp.float32)
    value = found[0:1] + found[1:2] + found[2:3]
    out_ref[...] = jnp.where(found[3:4] > 0.5, value, CLIP)


VMEM = pl.BlockSpec(memory_space=pltpu.VMEM)
SMEM = pl.BlockSpec(memory_space=pltpu.SMEM)
ANY = pl.BlockSpec(memory_space=pl.ANY)


def call(kernel, name, out_shape, in_specs, scratch, vmem, flops, aliases=None):
    return pl.pallas_call(
        kernel,
        out_shape=out_shape,
        in_specs=in_specs,
        out_specs=jax.tree.map(lambda _: VMEM, out_shape),
        scratch_shapes=scratch,
        compiler_params=pltpu.CompilerParams(vmem_limit_bytes=vmem << 20),
        cost_estimate=pl.CostEstimate(flops=flops, bytes_accessed=4_000_000, transcendentals=0),
        input_output_aliases=aliases or {},
        name=name,
    )


def body(cheb_coef, obj_cell):
    objects = cheb_coef.shape[3]
    own = cheb_coef.reshape(3 * DEG1, 1, objects)
    cells = lax.axis_size("cell")
    slots = cells * CAP
    windows = lax.axis_size("tm")
    window = lax.axis_index("tm").astype(jnp.int32).reshape(1)
    prev = lax.ppermute(own, "tm", [(i, i + 1) for i in range(windows - 1)])
    row = jax.ShapeDtypeStruct((1, slots), jnp.float32)
    cell = lax.axis_index("cell").astype(jnp.int32).reshape(1)
    wide = jax.ShapeDtypeStruct((slots, LANES), jnp.float32)
    chosen, counts = call(
        place_kernel,
        "place",
        (jax.ShapeDtypeStruct((cells * PACK, 3 * objects), BF16), jax.ShapeDtypeStruct((8, LANES), jnp.float32)),
        [VMEM],
        [],
        8,
        2_000_000_000,
    )(obj_cell.reshape(1, objects))
    send = call(
        front_kernel,
        "front",
        jax.ShapeDtypeStruct((cells * PACK, LANES), jnp.float32),
        [SMEM] + [VMEM] * 5,
        [pltpu.VMEM((LANES, objects), jnp.float32)],
        8,
        2_000_000_000,
    )(window, own, prev, chosen, counts, jnp.asarray(rim_tables()))
    packed = lax.all_to_all(send, "cell", split_axis=0, concat_axis=0, tiled=True)
    live, chosen, counts = call(
        compact_kernel,
        "compact",
        (wide, jax.ShapeDtypeStruct((slots, slots), BF16), jax.ShapeDtypeStruct((1, LANES), jnp.float32)),
        [VMEM],
        [],
        16,
        2_000_000_000,
    )(packed)
    forward = [(i, (i + 1) % cells) for i in range(cells)]
    backward = [((i + 1) % cells, i) for i in range(cells)]
    next_live = lax.ppermute(live, "cell", backward)
    prev_live = lax.ppermute(live, "cell", forward)
    synth = jnp.asarray(synth_matrix())
    left_sel = jnp.asarray(np.ascontiguousarray(selection(True).T))
    right_sel = jnp.asarray(selection(False))
    left_shape = jax.ShapeDtypeStruct((2 * (EXT // GROUP), slots, LANES), BF16)
    scratch = [
        pltpu.VMEM((EXT, PIECES, slots), BF16),
        pltpu.VMEM((slots, COLS), jnp.float32),
        pltpu.VMEM((2, slots, LANES), jnp.float32),
        pltpu.VMEM((1, slots), jnp.float32),
        pltpu.VMEM(synth.shape, jnp.float32),
        pltpu.VMEM(left_sel.shape, BF16),
        pltpu.VMEM(right_sel.shape, BF16),
        pltpu.VMEM((3, UNITS, CHUNK, slots), jnp.float32),
        pltpu.VMEM((CHUNK, slots), jnp.float32),
        pltpu.SemaphoreType.DMA((3,)),
    ]
    own_min, left, shares = call(
        functools.partial(self_kernel, cells),
        "self_screen",
        (row, left_shape, jax.ShapeDtypeStruct((8, LANES), jnp.float32)),
        [SMEM, VMEM, VMEM, ANY, ANY, ANY],
        scratch,
        40,
        15_000_000_000,
    )(cell, live, counts, synth, left_sel, right_sel)
    best, next_min, prev_min, _ = call(
        functools.partial(neighbour_kernel, cells),
        "neighbour_screen",
        (row, row, row, left_shape),
        [SMEM] + [VMEM] * 5 + [ANY] * 3,
        scratch,
        40,
        20_000_000_000,
        {5: 3},
    )(cell, shares, next_live, prev_live, own_min, left, synth, left_sel, right_sel)
    from_prev = lax.ppermute(next_min, "cell", forward)
    from_next = lax.ppermute(prev_min, "cell", backward)
    return call(restore_kernel, "restore", row, [VMEM] * 4, [], 8, 100_000_000)(best, from_prev, from_next, chosen)


def solution(mesh):
    in_specs = (P("tm", None, None, "cell"), P("tm", "cell", None))
    return jax.shard_map(body, mesh=mesh, in_specs=in_specs, out_specs=P("tm", "cell"), check_vma=False)
```

```python
import functools

import jax
import jax.numpy as jnp
import ml_dtypes
import numpy as np
from jax import lax
from jax.experimental import pallas as pl
from jax.experimental.pallas import tpu as pltpu
from jax.sharding import PartitionSpec as P

DEG1 = 17
SAMP = 64
RIM = 8
CAP = 24
EXT = SAMP + RIM
CLIP = 25.0
FAR = 1.0e9

LANES = 128
FLAG_AT = 3 * DEG1
RIM_AT = FLAG_AT + 1
RECORD = RIM_AT + 3 * RIM
PACK = 16
LATE = CAP - PACK
COUNT_AT = RECORD + 3 * RIM
HALF = 16

PIECES = 32
GROUP = LANES // PIECES
CHUNK = 8
UNITS = EXT // CHUNK
PARTS = 2
NORMS = 3
KINDS = 3 * PARTS + NORMS
SRC = 128
ROWS = 128
COLS = 256
BF16 = jnp.bfloat16


def cheb_table():
    nodes = ((2.0 * np.arange(SAMP, dtype=np.float32) + 1.0) / SAMP - 1.0).astype(np.float32)
    columns = [np.ones_like(nodes), nodes]
    for _ in range(2, DEG1):
        columns.append((2.0 * nodes * columns[-1] - columns[-2]).astype(np.float32))
    return np.stack(columns, axis=1)


def rim_tables():
    table = cheb_table()
    return np.stack([table[:RIM], table[SAMP - RIM :]])


def synth_matrix():
    table = cheb_table()
    weights = np.zeros((3 * EXT, LANES), np.float32)
    for c in range(3):
        for s in range(RIM):
            weights[c * EXT + s, RIM_AT + RIM * c + s] = 1.0
        weights[c * EXT + RIM : (c + 1) * EXT, DEG1 * c : DEG1 * (c + 1)] = table
    return weights


def selection(left):
    one = KINDS
    uses = []
    for i in range(PARTS):
        for j in range(PARTS):
            for c in range(3):
                uses.append((3 * i + c, 1.0) if left else (3 * j + c, -1.0))
    for n in range(NORMS):
        uses.append((3 * PARTS + n, 1.0) if left else (one, 1.0))
    for n in range(NORMS):
        uses.append((one, 1.0) if left else (3 * PARTS + n, 1.0))
    matrix = np.zeros((CHUNK * PIECES, SRC), np.float32)
    for t in range(CHUNK):
        for k, (kind, value) in enumerate(uses):
            matrix[t * PIECES + k, kind * CHUNK + (0 if kind == one else t)] = value
    return matrix.astype(ml_dtypes.bfloat16)


def split(value, count):
    pieces = []
    for _ in range(count):
        piece = value.astype(BF16).astype(jnp.float32)
        value = value - piece
        pieces.append(piece)
    return pieces, value


def one_hot(row_ids, names):
    return jnp.where(row_ids == jnp.broadcast_to(names, row_ids.shape), 1.0, 0.0).astype(BF16)


def place_kernel(cell_ref, out_ref, count_ref):
    rows = out_ref.shape[0]
    count = cell_ref.shape[1]
    cell = cell_ref[...].astype(jnp.float32)
    column = jnp.transpose(jnp.broadcast_to(cell, (LANES, count)))
    lane = lax.broadcasted_iota(jnp.int32, (count, LANES), 1)
    for n in range(2):
        name = jnp.where((lane >= COUNT_AT) & (lane < COUNT_AT + HALF), lane - COUNT_AT + n * HALF, -1)
        named = jnp.where(column == name.astype(jnp.float32), 1.0, 0.0)
        count_ref[n : n + 1, :] = jnp.sum(named, axis=0, keepdims=True)
    column = jnp.concatenate([column] * (count // LANES), axis=1)
    before = lax.broadcasted_iota(jnp.int32, (count, count), 0) < lax.broadcasted_iota(jnp.int32, (count, count), 1)
    same = (column == jnp.broadcast_to(cell, (count, count))) & before
    rank = jnp.sum(jnp.where(same, 1.0, 0.0), axis=0, keepdims=True)
    early = jnp.where(rank < PACK, cell * PACK + rank, -1.0).astype(jnp.int32)
    late = jnp.where(rank < PACK, -1.0, cell * PACK + rank - PACK).astype(jnp.int32)
    ids = lax.broadcasted_iota(jnp.int32, (rows, count), 0)
    out_ref[:, 0:count] = one_hot(ids, early)
    out_ref[:, count : 2 * count] = one_hot(ids, late)
    out_ref[:, 2 * count : 3 * count] = one_hot(ids, jnp.where(late < 0, -1, late + LATE))


def placed(chosen, data):
    pieces = []
    for _ in range(3):
        piece = data.astype(BF16)
        data = data - piece.astype(jnp.float32)
        pieces.append(piece)
    found = jnp.dot(chosen, jnp.concatenate(pieces, axis=1), preferred_element_type=jnp.float32)
    return found[:, :LANES] + found[:, LANES : 2 * LANES] + found[:, 2 * LANES :]


def front_kernel(first_ref, own_ref, prev_ref, chosen_ref, count_ref, table_ref, out_ref, rows_ref):
    count = own_ref.shape[2]
    first = first_ref[0] == 0
    rows_ref[...] = jnp.zeros_like(rows_ref)
    table = jnp.where(first, table_ref[0], table_ref[1])
    for c in range(3):
        rows = slice(c * DEG1, (c + 1) * DEG1)
        own = own_ref[rows, 0, :]
        rows_ref[rows, :] = own
        source = jnp.where(first, own, prev_ref[rows, 0, :])
        rows_ref[RIM_AT + RIM * c : RIM_AT + RIM * (c + 1), :] = jnp.dot(
            table, source, precision=lax.Precision.HIGHEST, preferred_element_type=jnp.float32
        )
    rows_ref[FLAG_AT : FLAG_AT + 1, :] = jnp.ones((1, count), jnp.float32)
    data = jnp.transpose(rows_ref[...])
    lane = lax.broadcasted_iota(jnp.int32, data.shape, 1)
    late = jnp.where(lane >= RECORD, pltpu.roll(data, RECORD, 1), 0.0)
    rim = jnp.where((lane >= RECORD) & (lane < COUNT_AT), pltpu.roll(data, RECORD - RIM_AT, 1), 0.0)
    found = placed(chosen_ref[...], jnp.concatenate([data, late, rim], axis=0))
    row = lax.rem(lax.broadcasted_iota(jnp.int32, found.shape, 0), PACK)
    counts = jnp.where(lax.rem(row, 2) == 0, count_ref[0:1, :], count_ref[1:2, :])
    out_ref[...] = found + jnp.where(row >= LATE, counts, 0.0)


def plan(counts):
    rows = jnp.maximum(jnp.ceil(counts / ROWS), 1.0) * ROWS
    tiles = jnp.maximum(jnp.ceil(counts / COLS), 1.0)
    fixed, per_row, extra, least = 11.0, 0.139, 22.0, 28.0
    alone = tiles * fixed + per_row * (
        jnp.minimum(rows, COLS)
        + jnp.where(tiles > 1.5, jnp.minimum(rows, 2 * COLS), 0.0)
        + jnp.where(tiles > 2.5, rows, 0.0)
    )
    after = lambda value: pltpu.roll(value, LANES - 1, 1)
    ahead = lambda value: pltpu.roll(value, 1, 1)
    here = after(tiles) * (fixed + per_row * rows) + extra
    there = tiles * (fixed + per_row * after(rows)) + extra
    lent = 1.15 * alone
    cross_step, self_step = 0.5 / (here + there), 0.15 / alone
    share, before, behind = jnp.full_like(counts, 0.5), jnp.zeros_like(counts), jnp.zeros_like(counts)
    for _ in range(16):
        load = (
            alone * (1.0 - before - behind)
            + share * here
            + ahead((1.0 - share) * there + behind * lent)
            + after(before * lent)
        )
        up, down = after(load) - load, load - ahead(load)
        share = jnp.clip(share + cross_step * up, 0.0, 1.0)
        before = jnp.clip(before + self_step * (down - least), 0.0, 0.45)
        behind = jnp.clip(behind - self_step * (up + least), 0.0, 0.45)
    return [jnp.floor(value * UNITS + 0.5) for value in (share, before, behind)]


def records(packed):
    tiles = packed.reshape(packed.shape[0] // PACK, 2, LATE, LANES)
    blocks = tiles.shape[0]
    flat = (blocks * LATE, LANES)
    low, high = tiles[:, 0].reshape(flat), tiles[:, 1].reshape(flat)
    lane = lax.broadcasted_iota(jnp.int32, flat, 1)
    late = jnp.where(
        lane < RIM_AT,
        pltpu.roll(low, LANES - RECORD, 1),
        jnp.where(lane < RECORD, pltpu.roll(high, LANES - (RECORD - RIM_AT), 1), 0.0),
    )
    each = [v.reshape(blocks, 1, LATE, LANES) for v in (low, high, late)]
    return jnp.concatenate(each, axis=1).reshape(blocks * CAP, LANES), high


def cell_counts(high):
    row = lax.rem(lax.broadcasted_iota(jnp.int32, high.shape, 0), 2)
    lane = lax.broadcasted_iota(jnp.int32, high.shape, 1)
    held = jnp.where((lane >= COUNT_AT) & (lane < COUNT_AT + HALF), high, 0.0)
    total = None
    for n in range(2):
        part = jnp.sum(jnp.where(row == n, held, 0.0), axis=0, keepdims=True) * (2.0 / LATE)
        part = pltpu.roll(part, (n * HALF - COUNT_AT) % LANES, 1)
        total = part if total is None else total + part
    total = total + pltpu.roll(total, 2 * HALF, 1)
    return total + pltpu.roll(total, 4 * HALF, 1)


def compact_kernel(packed_ref, live_ref, chosen_ref, count_ref):
    data, high = records(packed_ref[...])
    slots = data.shape[0]
    flag = jnp.transpose(data)[FLAG_AT : FLAG_AT + 1, :]
    first = lax.broadcasted_iota(jnp.int32, (slots, slots), 0)
    second = lax.broadcasted_iota(jnp.int32, (slots, slots), 1)
    before = jnp.where(first < second, 1.0, 0.0).astype(BF16)
    flags = jnp.broadcast_to(flag, (16, slots)).astype(BF16)
    place = jnp.dot(flags, before, preferred_element_type=jnp.float32)[0:1]
    place = jnp.where(flag > 0.5, place, -1.0).astype(jnp.int32)
    chosen = one_hot(first, place)
    chosen_ref[...] = chosen
    live_ref[...] = placed(chosen, data)
    count_ref[...] = cell_counts(high)


def fetched(sources, targets, sem):
    copies = [pltpu.make_async_copy(s, t, sem.at[i]) for i, (s, t) in enumerate(zip(sources, targets))]
    for copy in copies:
        copy.start()
    return copies


def tracks(live_ref, synth_ref, track_ref, flag_ref, copies):
    live = jnp.transpose(live_ref[...])
    flag_ref[...] = jnp.broadcast_to(live[FLAG_AT : FLAG_AT + 1, :], flag_ref.shape)
    for copy in copies:
        copy.wait()
    track = jnp.dot(synth_ref[...], live, precision=lax.Precision.HIGHEST, preferred_element_type=jnp.float32)
    track_ref[...] = track.reshape(track_ref.shape)


def source_of(track_ref, flag_ref, unit):
    count = track_ref.shape[3]
    parts, norm = [], None
    for c in range(3):
        axis = track_ref[c, unit]
        pieces, rest = split(axis, PARTS)
        parts.append(pieces)
        held = axis - rest
        norm = held * held if norm is None else norm + held * held
    norm = jnp.where(flag_ref[...] > 0.5, 0.5 * norm, FAR)
    kinds = [parts[c][i] for i in range(PARTS) for c in range(3)] + split(norm, NORMS)[0]
    ones = jnp.ones((CHUNK, count), jnp.float32)
    zeros = jnp.zeros((SRC - (KINDS + 1) * CHUNK, count), jnp.float32)
    return jnp.concatenate(kinds + [ones, zeros], axis=0)


def put_right(source, right_sel_ref, right_ref, unit):
    right = jnp.dot(right_sel_ref[...], source.astype(BF16), preferred_element_type=jnp.float32)
    right_ref[pl.ds(unit * CHUNK, CHUNK)] = right.astype(BF16).reshape(CHUNK, PIECES, right.shape[1])


def put_left(source, left_sel_ref, left_ref, unit, offset):
    left = jnp.dot(jnp.transpose(source).astype(BF16), left_sel_ref[...], preferred_element_type=jnp.float32)
    left = left.astype(BF16)
    for g in range(CHUNK // GROUP):
        left_ref[offset + unit * (CHUNK // GROUP) + g] = left[:, g * LANES : (g + 1) * LANES]


def sweep(left_ref, right_ref, acc_ref, row_ref, col_ref, job, row_tiles, col_start, first, last, diagonal):
    groups = CHUNK // GROUP
    offset = job * (EXT // GROUP)
    columns = pl.ds(col_start, COLS)

    def screen(rows, unit, units):
        best = acc_ref[0:rows, :]
        for h in range(units * groups):
            g = unit * groups + h
            left = left_ref[offset + g, 0:rows, :]
            for j in range(GROUP):
                parts = [right_ref[g * GROUP + j, :, columns]]
                if j > 0:
                    parts = [jnp.zeros((PIECES * j, COLS), BF16)] + parts
                if j < GROUP - 1:
                    parts = parts + [jnp.zeros((PIECES * (GROUP - 1 - j), COLS), BF16)]
                weights = jnp.concatenate(parts, axis=0)
                best = jnp.minimum(best, jnp.dot(left, weights, preferred_element_type=jnp.float32))
        acc_ref[0:rows, :] = best

    for n in range(1, acc_ref.shape[0] // ROWS + 1):

        @pl.when(row_tiles == n)
        def _(rows=n * ROWS, each=2 if n < 4 else 1):
            acc_ref[0:rows, :] = jnp.full((rows, COLS), CLIP, jnp.float32)
            steps = (last - first) // each

            def step(i, carry):
                screen(rows, first + i * each, each)
                return carry

            lax.fori_loop(0, steps, step, 0)
            if each > 1:

                @pl.when(first + steps * each < last)
                def _():
                    screen(rows, last - 1, 1)

            @pl.when(diagonal)
            def _():
                same = lax.broadcasted_iota(jnp.int32, (COLS, COLS), 0) == lax.broadcasted_iota(
                    jnp.int32, (COLS, COLS), 1
                )
                near = pl.ds(col_start, COLS)
                acc_ref[near, :] = jnp.where(same, CLIP, acc_ref[near, :])

            acc = acc_ref[0:rows, :]
            half = jnp.minimum(acc[:, :LANES], acc[:, LANES:])
            row_ref[job, 0:rows, :] = jnp.minimum(row_ref[job, 0:rows, :], half)
            best = finished(jnp.min(acc, axis=0, keepdims=True))
            col_ref[:, columns] = jnp.minimum(col_ref[:, columns], best)


def by_row(row_ref, job):
    return finished(jnp.min(jnp.transpose(row_ref[job]), axis=0, keepdims=True))


def finished(half):
    return jnp.clip(2.0 * half, 0.0, CLIP)


def planned(plan_ref, row, cell, cells):
    lane = lax.broadcasted_iota(jnp.int32, (1, LANES), 1)
    value = jnp.sum(jnp.where(lane == lax.rem(cell, cells), plan_ref[row : row + 1, :], 0.0))
    return value.astype(jnp.int32)


def tiles_of(count, size):
    return jnp.maximum((count + (size - 1)) // size, 1)


def self_kernel(
    cells, cell_ref, live_ref, count_ref, synth_hbm, left_sel_hbm, right_sel_hbm, out_ref, left_ref, plan_ref,
    right_ref, acc_ref, row_ref, col_ref, synth_ref, left_sel_ref, right_sel_ref, track_ref, flag_ref, sem,
):
    copies = fetched((synth_hbm, left_sel_hbm, right_sel_hbm), (synth_ref, left_sel_ref, right_sel_ref), sem)
    tracks(live_ref, synth_ref, track_ref, flag_ref, copies)
    counts = count_ref[...]
    plan_ref[0:1, :] = counts
    for n, units in enumerate(plan(counts)):
        plan_ref[n + 1 : n + 2, :] = units
    for unit in range(UNITS):
        source = source_of(track_ref, flag_ref, unit)
        put_right(source, right_sel_ref, right_ref, unit)
        put_left(source, left_sel_ref, left_ref, unit, 0)
    cell = cell_ref[0]
    count = planned(plan_ref, 0, cell, cells)
    first, last = planned(plan_ref, 2, cell, cells), UNITS - planned(plan_ref, 3, cell, cells)
    row_tiles = tiles_of(count, ROWS)
    row_ref[...] = jnp.full_like(row_ref, CLIP)
    col_ref[...] = jnp.full_like(col_ref, CLIP)

    def column(n, carry):
        start = pl.multiple_of(n * COLS, COLS)
        limit = jnp.minimum(row_tiles, (n + 1) * (COLS // ROWS))
        sweep(left_ref, right_ref, acc_ref, row_ref, col_ref, 0, limit, start, first, last, n >= 0)
        return carry

    lax.fori_loop(0, tiles_of(count, COLS), column, 0)
    out_ref[...] = jnp.minimum(by_row(row_ref, 0), col_ref[...])


def neighbour_kernel(
    cells, cell_ref, plan_ref, next_ref, prev_ref, base_ref, left_in_ref, synth_hbm, left_sel_hbm, right_sel_hbm,
    out_ref, next_out_ref, prev_out_ref, left_ref,
    right_ref, acc_ref, row_ref, col_ref, synth_ref, left_sel_ref, right_sel_ref, track_ref, flag_ref, sem,
):
    del left_in_ref
    copies = fetched((synth_hbm, left_sel_hbm, right_sel_hbm), (synth_ref, left_sel_ref, right_sel_ref), sem)
    cell = cell_ref[0]
    after, ahead = cell + 1, cell + (cells - 1)
    own_rows = tiles_of(planned(plan_ref, 0, cell, cells), ROWS)
    own_share, their_share = planned(plan_ref, 1, cell, cells), planned(plan_ref, 1, ahead, cells)
    of_next, of_prev = planned(plan_ref, 2, after, cells), planned(plan_ref, 3, ahead, cells)
    next_count, prev_count = planned(plan_ref, 0, after, cells), planned(plan_ref, 0, ahead, cells)
    offset = left_ref.shape[0] // 2
    for copy in copies:
        copy.wait()
    row_ref[0] = jnp.full(row_ref.shape[1:], CLIP, jnp.float32)

    def phase(p, carry):
        forward = p == 0
        cross = jnp.where(forward, 0, their_share), jnp.where(forward, own_share, UNITS)
        alone = jnp.where(forward, 0, UNITS - of_prev), jnp.where(forward, of_next, UNITS)
        cross_on, alone_on = cross[0] < cross[1], alone[0] < alone[1]
        first = jnp.minimum(cross[0], alone[0])
        last = jnp.maximum(cross[1], alone[1])
        count = jnp.where(forward, next_count, prev_count)
        other_rows, other_cols = tiles_of(count, ROWS), tiles_of(count, COLS)

        @pl.when(forward & (first < last))
        def _():
            tracks(next_ref, synth_ref, track_ref, flag_ref, ())

        @pl.when((p == 1) & (first < last))
        def _():
            tracks(prev_ref, synth_ref, track_ref, flag_ref, ())

        def unit_step(unit, c):
            source = source_of(track_ref, flag_ref, unit)
            put_right(source, right_sel_ref, right_ref, unit)

            @pl.when((unit >= alone[0]) & (unit < alone[1]))
            def _():
                put_left(source, left_sel_ref, left_ref, unit, offset)

            return c

        lax.fori_loop(first, last, unit_step, 0)
        row_ref[1] = jnp.full(row_ref.shape[1:], CLIP, jnp.float32)
        col_ref[...] = jnp.full_like(col_ref, CLIP)

        def column(k, c):
            job = jnp.where(k < other_cols, 0, 1)
            n = k - job * other_cols
            start = pl.multiple_of(n * COLS, COLS)
            limit = jnp.where(job == 0, own_rows, jnp.minimum(other_rows, (n + 1) * (COLS // ROWS)))
            low, high = jnp.where(job == 0, cross[0], alone[0]), jnp.where(job == 0, cross[1], alone[1])
            sweep(left_ref, right_ref, acc_ref, row_ref, col_ref, job, limit, start, low, high, job == 1)
            return c

        lax.fori_loop(
            jnp.where(cross_on, 0, other_cols), jnp.where(alone_on, 2 * other_cols, other_cols), column, 0
        )
        best = jnp.minimum(col_ref[...], by_row(row_ref, 1))

        @pl.when(forward)
        def _():
            next_out_ref[...] = best

        @pl.when(p == 1)
        def _():
            prev_out_ref[...] = best

        return carry

    lax.fori_loop(0, 2, phase, 0)
    out_ref[...] = jnp.minimum(by_row(row_ref, 0), base_ref[...])


def restore_kernel(*refs):
    *minima, chosen_ref, out_ref = refs
    count = out_ref.shape[1]
    best = functools.reduce(jnp.minimum, [ref[...] for ref in minima])
    pieces = split(best, 3)[0]
    ones, zeros = jnp.ones((1, count), jnp.float32), jnp.zeros((12, count), jnp.float32)
    rows = jnp.concatenate(pieces + [ones, zeros], axis=0).astype(BF16)
    found = jnp.dot(rows, chosen_ref[...], preferred_element_type=jnp.float32)
    value = found[0:1] + found[1:2] + found[2:3]
    out_ref[...] = jnp.where(found[3:4] > 0.5, value, CLIP)


VMEM = pl.BlockSpec(memory_space=pltpu.VMEM)
SMEM = pl.BlockSpec(memory_space=pltpu.SMEM)
ANY = pl.BlockSpec(memory_space=pl.ANY)


def call(kernel, name, out_shape, in_specs, scratch, vmem, flops, aliases=None):
    return pl.pallas_call(
        kernel,
        out_shape=out_shape,
        in_specs=in_specs,
        out_specs=jax.tree.map(lambda _: VMEM, out_shape),
        scratch_shapes=scratch,
        compiler_params=pltpu.CompilerParams(vmem_limit_bytes=vmem << 20),
        cost_estimate=pl.CostEstimate(flops=flops, bytes_accessed=4_000_000, transcendentals=0),
        input_output_aliases=aliases or {},
        name=name,
    )


def body(cheb_coef, obj_cell):
    objects = cheb_coef.shape[3]
    own = cheb_coef.reshape(3 * DEG1, 1, objects)
    cells = lax.axis_size("cell")
    slots = cells * CAP
    windows = lax.axis_size("tm")
    window = lax.axis_index("tm").astype(jnp.int32).reshape(1)
    prev = lax.ppermute(own, "tm", [(i, i + 1) for i in range(windows - 1)])
    row = jax.ShapeDtypeStruct((1, slots), jnp.float32)
    cell = lax.axis_index("cell").astype(jnp.int32).reshape(1)
    wide = jax.ShapeDtypeStruct((slots, LANES), jnp.float32)
    chosen, counts = call(
        place_kernel,
        "place",
        (jax.ShapeDtypeStruct((cells * PACK, 3 * objects), BF16), jax.ShapeDtypeStruct((8, LANES), jnp.float32)),
        [VMEM],
        [],
        8,
        2_000_000_000,
    )(obj_cell.reshape(1, objects))
    send = call(
        front_kernel,
        "front",
        jax.ShapeDtypeStruct((cells * PACK, LANES), jnp.float32),
        [SMEM] + [VMEM] * 5,
        [pltpu.VMEM((LANES, objects), jnp.float32)],
        8,
        2_000_000_000,
    )(window, own, prev, chosen, counts, jnp.asarray(rim_tables()))
    packed = lax.all_to_all(send, "cell", split_axis=0, concat_axis=0, tiled=True)
    live, chosen, counts = call(
        compact_kernel,
        "compact",
        (wide, jax.ShapeDtypeStruct((slots, slots), BF16), jax.ShapeDtypeStruct((1, LANES), jnp.float32)),
        [VMEM],
        [],
        16,
        2_000_000_000,
    )(packed)
    forward = [(i, (i + 1) % cells) for i in range(cells)]
    backward = [((i + 1) % cells, i) for i in range(cells)]
    next_live = lax.ppermute(live, "cell", backward)
    prev_live = lax.ppermute(live, "cell", forward)
    synth = jnp.asarray(synth_matrix())
    left_sel = jnp.asarray(np.ascontiguousarray(selection(True).T))
    right_sel = jnp.asarray(selection(False))
    left_shape = jax.ShapeDtypeStruct((2 * (EXT // GROUP), slots, LANES), BF16)
    scratch = [
        pltpu.VMEM((EXT, PIECES, slots), BF16),
        pltpu.VMEM((slots, COLS), jnp.float32),
        pltpu.VMEM((2, slots, LANES), jnp.float32),
        pltpu.VMEM((1, slots), jnp.float32),
        pltpu.VMEM(synth.shape, jnp.float32),
        pltpu.VMEM(left_sel.shape, BF16),
        pltpu.VMEM(right_sel.shape, BF16),
        pltpu.VMEM((3, UNITS, CHUNK, slots), jnp.float32),
        pltpu.VMEM((CHUNK, slots), jnp.float32),
        pltpu.SemaphoreType.DMA((3,)),
    ]
    own_min, left, shares = call(
        functools.partial(self_kernel, cells),
        "self_screen",
        (row, left_shape, jax.ShapeDtypeStruct((8, LANES), jnp.float32)),
        [SMEM, VMEM, VMEM, ANY, ANY, ANY],
        scratch,
        40,
        15_000_000_000,
    )(cell, live, counts, synth, left_sel, right_sel)
    best, next_min, prev_min, _ = call(
        functools.partial(neighbour_kernel, cells),
        "neighbour_screen",
        (row, row, row, left_shape),
        [SMEM] + [VMEM] * 5 + [ANY] * 3,
        scratch,
        40,
        20_000_000_000,
        {5: 3},
    )(cell, shares, next_live, prev_live, own_min, left, synth, left_sel, right_sel)
    from_prev = lax.ppermute(next_min, "cell", forward)
    from_next = lax.ppermute(prev_min, "cell", backward)
    return call(restore_kernel, "restore", row, [VMEM] * 4, [], 8, 100_000_000)(best, from_prev, from_next, chosen)


def solution(mesh):
    in_specs = (P("tm", None, None, "cell"), P("tm", "cell", None))
    return jax.shard_map(body, mesh=mesh, in_specs=in_specs, out_specs=P("tm", "cell"), check_vma=False)
```

```python
import functools

import jax
import jax.numpy as jnp
import ml_dtypes
import numpy as np
from jax import lax
from jax.experimental import pallas as pl
from jax.experimental.pallas import tpu as pltpu
from jax.sharding import PartitionSpec as P

DEG1 = 17
SAMP = 64
RIM = 8
CAP = 24
EXT = SAMP + RIM
CLIP = 25.0
FAR = 1.0e9

LANES = 128
FLAG_AT = 3 * DEG1
RIM_AT = FLAG_AT + 1
RECORD = RIM_AT + 3 * RIM
PACK = 16
LATE = CAP - PACK
COUNT_AT = RECORD + 3 * RIM
HALF = 16

PIECES = 32
GROUP = LANES // PIECES
CHUNK = 8
UNITS = EXT // CHUNK
PARTS = 2
NORMS = 3
KINDS = 3 * PARTS + NORMS
SRC = 80
TERMS = 80
ROWS = 128
COLS = 256
BF16 = jnp.bfloat16


def cheb_table():
    nodes = ((2.0 * np.arange(SAMP, dtype=np.float32) + 1.0) / SAMP - 1.0).astype(np.float32)
    columns = [np.ones_like(nodes), nodes]
    for _ in range(2, DEG1):
        columns.append((2.0 * nodes * columns[-1] - columns[-2]).astype(np.float32))
    return np.stack(columns, axis=1)


def rim_tables():
    table = cheb_table()
    return np.stack([table[:RIM], table[SAMP - RIM :]])


def synth_matrix():
    table = cheb_table()
    weights = np.zeros((3 * EXT, LANES), np.float32)
    for c in range(3):
        for s in range(RIM):
            weights[c * EXT + s, RIM_AT + RIM * c + s] = 1.0
        weights[c * EXT + RIM : (c + 1) * EXT, DEG1 * c : DEG1 * (c + 1)] = table
    high = weights[:, :TERMS].astype(ml_dtypes.bfloat16)
    low = (weights[:, :TERMS] - high.astype(np.float32)).astype(ml_dtypes.bfloat16)
    return np.concatenate([high, high, low, np.zeros((3 * EXT, 2 * LANES - 3 * TERMS), high.dtype)], axis=1)


def selection(left):
    one = KINDS
    uses = []
    for i in range(PARTS):
        for j in range(PARTS):
            for c in range(3):
                uses.append((3 * i + c, 1.0) if left else (3 * j + c, -1.0))
    for n in range(NORMS):
        uses.append((3 * PARTS + n, 1.0) if left else (one, 1.0))
    for n in range(NORMS):
        uses.append((one, 1.0) if left else (3 * PARTS + n, 1.0))
    matrix = np.zeros((CHUNK * PIECES, SRC), np.float32)
    for t in range(CHUNK):
        for k, (kind, value) in enumerate(uses):
            matrix[t * PIECES + k, kind * CHUNK + (0 if kind == one else t)] = value
    return matrix.astype(ml_dtypes.bfloat16)


def split(value, count):
    pieces = []
    for _ in range(count):
        piece = value.astype(BF16).astype(jnp.float32)
        value = value - piece
        pieces.append(piece)
    return pieces, value


def one_hot(row_ids, names):
    return jnp.where(row_ids == jnp.broadcast_to(names, row_ids.shape), 1.0, 0.0).astype(BF16)


def placed(chosen, data):
    pieces = []
    for _ in range(3):
        piece = data.astype(BF16)
        data = data - piece.astype(jnp.float32)
        pieces.append(piece)
    found = jnp.dot(chosen, jnp.concatenate(pieces, axis=1), preferred_element_type=jnp.float32)
    return found[:, :LANES] + found[:, LANES : 2 * LANES] + found[:, 2 * LANES :]


def place_kernel(cell_ref, own_ref, chosen_ref, base_ref, rows_ref):
    rows = chosen_ref.shape[0]
    count = cell_ref.shape[1]
    cell = cell_ref[...].astype(jnp.float32)
    column = jnp.transpose(jnp.broadcast_to(cell, (LANES, count)))
    lane = lax.broadcasted_iota(jnp.int32, (count, LANES), 1)
    counts = []
    for n in range(2):
        name = jnp.where((lane >= COUNT_AT) & (lane < COUNT_AT + HALF), lane - COUNT_AT + n * HALF, -1)
        named = jnp.where(column == name.astype(jnp.float32), 1.0, 0.0)
        counts.append(jnp.sum(named, axis=0, keepdims=True))
    column = jnp.concatenate([column] * (count // LANES), axis=1)
    before = lax.broadcasted_iota(jnp.int32, (count, count), 0) < lax.broadcasted_iota(jnp.int32, (count, count), 1)
    same = (column == jnp.broadcast_to(cell, (count, count))) & before
    rank = jnp.sum(jnp.where(same, 1.0, 0.0), axis=0, keepdims=True)
    early = jnp.where(rank < PACK, cell * PACK + rank, -1.0).astype(jnp.int32)
    late = jnp.where(rank < PACK, -1.0, cell * PACK + rank - PACK).astype(jnp.int32)
    ids = lax.broadcasted_iota(jnp.int32, (rows, count), 0)
    early = one_hot(ids, early)
    chosen_ref[:, 0:count] = early
    chosen_ref[:, count : 2 * count] = one_hot(ids, jnp.where(late < 0, -1, late + LATE))
    rows_ref[...] = jnp.zeros_like(rows_ref)
    rows_ref[0:FLAG_AT, :] = own_ref[:, 0, :]
    rows_ref[FLAG_AT : FLAG_AT + 1, :] = jnp.ones((1, count), jnp.float32)
    data = jnp.transpose(rows_ref[...])
    data = jnp.concatenate([data, jnp.where(lane >= RECORD, pltpu.roll(data, RECORD, 1), 0.0)], axis=0)
    found = placed(jnp.concatenate([early, one_hot(ids, late)], axis=1), data)
    row = lax.rem(lax.broadcasted_iota(jnp.int32, found.shape, 0), PACK)
    held = jnp.where(lax.rem(row, 2) == 0, counts[0], counts[1])
    base_ref[...] = found + jnp.where(row >= LATE, held, 0.0)


def front_kernel(first_ref, own_ref, prev_ref, chosen_ref, base_ref, table_ref, out_ref, rows_ref):
    first = first_ref[0] == 0
    rows_ref[...] = jnp.zeros_like(rows_ref)
    table = jnp.where(first, table_ref[0], table_ref[1])
    for c in range(3):
        rows = slice(c * DEG1, (c + 1) * DEG1)
        source = jnp.where(first, own_ref[rows, 0, :], prev_ref[rows, 0, :])
        rows_ref[RIM_AT + RIM * c : RIM_AT + RIM * (c + 1), :] = jnp.dot(
            table, source, precision=lax.Precision.HIGHEST, preferred_element_type=jnp.float32
        )
    data = jnp.transpose(rows_ref[...])
    data = jnp.concatenate([data, pltpu.roll(data, RECORD - RIM_AT, 1)], axis=0)
    out_ref[...] = placed(chosen_ref[...], data) + base_ref[...]


def plan(counts):
    rows = jnp.maximum(jnp.ceil(counts / ROWS), 1.0) * ROWS
    tiles = jnp.maximum(jnp.ceil(counts / COLS), 1.0)
    fixed, per_row, extra, least = 0.0278, 1.244e-3, 0.26, 0.12
    alone = 0.0005 * tiles + 1.346e-3 * (
        jnp.minimum(rows, COLS)
        + jnp.where(tiles > 1.5, jnp.minimum(rows, 2 * COLS), 0.0)
        + jnp.where(tiles > 2.5, rows, 0.0)
    )
    after = lambda value: pltpu.roll(value, LANES - 1, 1)
    ahead = lambda value: pltpu.roll(value, 1, 1)
    here = after(tiles) * (fixed + per_row * rows) + extra
    there = tiles * (fixed + per_row * after(rows)) + extra
    lent = 0.92 * alone + tiles * fixed + 0.38
    cross_step, self_step = 0.5 / (here + there), 0.1 / alone
    share, before, behind = jnp.full_like(counts, 0.5), jnp.zeros_like(counts), jnp.zeros_like(counts)
    for _ in range(20):
        load = (
            alone * (1.0 - before - behind)
            + share * here
            + ahead((1.0 - share) * there + behind * lent)
            + after(before * lent)
        )
        up, down = after(load) - load, load - ahead(load)
        share = jnp.clip(share + cross_step * up, 0.0, 1.0)
        before = jnp.clip(before + self_step * (down - least), 0.0, 0.45)
        behind = jnp.clip(behind - self_step * (up + least), 0.0, 0.45)
    return [jnp.floor(value * UNITS + 0.5) for value in (share, before, behind)]


def records(packed):
    tiles = packed.reshape(packed.shape[0] // PACK, 2, LATE, LANES)
    blocks = tiles.shape[0]
    flat = (blocks * LATE, LANES)
    low, high = tiles[:, 0].reshape(flat), tiles[:, 1].reshape(flat)
    lane = lax.broadcasted_iota(jnp.int32, flat, 1)
    late = jnp.where(
        lane < RIM_AT,
        pltpu.roll(low, LANES - RECORD, 1),
        jnp.where(lane < RECORD, pltpu.roll(high, LANES - (RECORD - RIM_AT), 1), 0.0),
    )
    each = [v.reshape(blocks, 1, LATE, LANES) for v in (low, high, late)]
    return jnp.concatenate(each, axis=1).reshape(blocks * CAP, LANES), high


def cell_counts(high):
    row = lax.rem(lax.broadcasted_iota(jnp.int32, high.shape, 0), 2)
    lane = lax.broadcasted_iota(jnp.int32, high.shape, 1)
    held = jnp.where((lane >= COUNT_AT) & (lane < COUNT_AT + HALF), high, 0.0)
    total = None
    for n in range(2):
        part = jnp.sum(jnp.where(row == n, held, 0.0), axis=0, keepdims=True) * (2.0 / LATE)
        part = pltpu.roll(part, (n * HALF - COUNT_AT) % LANES, 1)
        total = part if total is None else total + part
    total = total + pltpu.roll(total, 2 * HALF, 1)
    return total + pltpu.roll(total, 4 * HALF, 1)


def compact_kernel(packed_ref, live_ref, chosen_ref, count_ref):
    data, high = records(packed_ref[...])
    slots = data.shape[0]
    flag = jnp.transpose(data)[FLAG_AT : FLAG_AT + 1, :]
    first = lax.broadcasted_iota(jnp.int32, (slots, slots), 0)
    second = lax.broadcasted_iota(jnp.int32, (slots, slots), 1)
    before = jnp.where(first < second, 1.0, 0.0).astype(BF16)
    flags = jnp.broadcast_to(flag, (16, slots)).astype(BF16)
    place = jnp.dot(flags, before, preferred_element_type=jnp.float32)[0:1]
    place = jnp.where(flag > 0.5, place, -1.0).astype(jnp.int32)
    chosen = one_hot(first, place)
    chosen_ref[...] = chosen
    live_ref[...] = placed(chosen, data)
    count_ref[...] = cell_counts(high)


def fetched(sources, targets, sem):
    copies = [pltpu.make_async_copy(s, t, sem.at[i]) for i, (s, t) in enumerate(zip(sources, targets))]
    for copy in copies:
        copy.start()
    return copies


def tracks(live_ref, synth_ref, track_ref, flag_ref, copies):
    live = jnp.transpose(live_ref[...])
    flag_ref[...] = jnp.broadcast_to(live[FLAG_AT : FLAG_AT + 1, :], flag_ref.shape)
    for copy in copies:
        copy.wait()
    (high, low), _ = split(live[:TERMS], 2)
    rest = jnp.zeros((2 * LANES - 3 * TERMS, live.shape[1]), jnp.float32)
    terms = jnp.concatenate([high, low, high, rest], axis=0).astype(BF16)
    track = jnp.dot(synth_ref[...], terms, preferred_element_type=jnp.float32)
    track_ref[...] = track.reshape(track_ref.shape)


def source_of(track_ref, flag_ref, unit):
    count = track_ref.shape[3]
    parts, norm = [], None
    for c in range(3):
        axis = track_ref[c, unit]
        pieces, rest = split(axis, PARTS)
        parts.append(pieces)
        held = axis - rest
        norm = held * held if norm is None else norm + held * held
    norm = jnp.where(flag_ref[...] > 0.5, 0.5 * norm, FAR)
    kinds = [parts[c][i] for i in range(PARTS) for c in range(3)] + split(norm, NORMS)[0]
    ones = jnp.ones((CHUNK, count), jnp.float32)
    return jnp.concatenate(kinds + [ones], axis=0)


def put_right(source, right_sel_ref, right_ref, unit):
    right = jnp.dot(right_sel_ref[...], source.astype(BF16), preferred_element_type=jnp.float32)
    right_ref[pl.ds(unit * CHUNK, CHUNK)] = right.astype(BF16).reshape(CHUNK, PIECES, right.shape[1])


def put_left(source, left_sel_ref, left_ref, unit, offset):
    left = jnp.dot(jnp.transpose(source).astype(BF16), left_sel_ref[...], preferred_element_type=jnp.float32)
    left = left.astype(BF16)
    for g in range(CHUNK // GROUP):
        left_ref[offset + unit * (CHUNK // GROUP) + g] = left[:, g * LANES : (g + 1) * LANES]


def sweep(left_ref, right_ref, acc_ref, row_ref, col_ref, job, row_tiles, col_start, first, last, diagonal):
    groups = CHUNK // GROUP
    offset = job * (EXT // GROUP)
    columns = pl.ds(col_start, COLS)

    def screen(rows, unit, units):
        best = acc_ref[0:rows, :]
        for h in range(units * groups):
            g = unit * groups + h
            left = left_ref[offset + g, 0:rows, :]
            for j in range(GROUP):
                parts = [right_ref[g * GROUP + j, :, columns]]
                if j > 0:
                    parts = [jnp.zeros((PIECES * j, COLS), BF16)] + parts
                if j < GROUP - 1:
                    parts = parts + [jnp.zeros((PIECES * (GROUP - 1 - j), COLS), BF16)]
                weights = jnp.concatenate(parts, axis=0)
                best = jnp.minimum(best, jnp.dot(left, weights, preferred_element_type=jnp.float32))
        acc_ref[0:rows, :] = best

    for n in range(1, acc_ref.shape[0] // ROWS + 1):

        @pl.when(row_tiles == n)
        def _(rows=n * ROWS, each=2 if n < 4 or n == 6 else 1):
            acc_ref[0:rows, :] = jnp.full((rows, COLS), CLIP, jnp.float32)
            steps = (last - first) // each

            def step(i, carry):
                screen(rows, first + i * each, each)
                return carry

            lax.fori_loop(0, steps, step, 0)
            if each > 1:

                @pl.when(first + steps * each < last)
                def _():
                    screen(rows, last - 1, 1)

            @pl.when(diagonal)
            def _():
                same = lax.broadcasted_iota(jnp.int32, (COLS, COLS), 0) == lax.broadcasted_iota(
                    jnp.int32, (COLS, COLS), 1
                )
                near = pl.ds(col_start, COLS)
                acc_ref[near, :] = jnp.where(same, CLIP, acc_ref[near, :])

            acc = acc_ref[0:rows, :]
            half = jnp.minimum(acc[:, :LANES], acc[:, LANES:])
            row_ref[job, 0:rows, :] = jnp.minimum(row_ref[job, 0:rows, :], half)
            best = finished(jnp.min(acc, axis=0, keepdims=True))
            col_ref[:, columns] = jnp.minimum(col_ref[:, columns], best)


def by_row(row_ref, job):
    return finished(jnp.min(jnp.transpose(row_ref[job]), axis=0, keepdims=True))


def finished(half):
    return jnp.clip(2.0 * half, 0.0, CLIP)


def planned(plan_ref, row, cell, cells):
    lane = lax.broadcasted_iota(jnp.int32, (1, LANES), 1)
    value = jnp.sum(jnp.where(lane == lax.rem(cell, cells), plan_ref[row : row + 1, :], 0.0))
    return value.astype(jnp.int32)


def tiles_of(count, size):
    return jnp.maximum((count + (size - 1)) // size, 1)


def self_kernel(
    cells, cell_ref, live_ref, count_ref, synth_hbm, left_sel_hbm, right_sel_hbm, out_ref, left_ref, plan_ref,
    right_ref, acc_ref, row_ref, col_ref, synth_ref, left_sel_ref, right_sel_ref, track_ref, flag_ref, sem,
):
    copies = fetched((synth_hbm, left_sel_hbm, right_sel_hbm), (synth_ref, left_sel_ref, right_sel_ref), sem)
    tracks(live_ref, synth_ref, track_ref, flag_ref, copies)
    counts = count_ref[...]
    plan_ref[0:1, :] = counts
    for n, units in enumerate(plan(counts)):
        plan_ref[n + 1 : n + 2, :] = units
    for unit in range(UNITS):
        source = source_of(track_ref, flag_ref, unit)
        put_right(source, right_sel_ref, right_ref, unit)
        put_left(source, left_sel_ref, left_ref, unit, 0)
    cell = cell_ref[0]
    count = planned(plan_ref, 0, cell, cells)
    first, last = planned(plan_ref, 2, cell, cells), UNITS - planned(plan_ref, 3, cell, cells)
    row_tiles = tiles_of(count, ROWS)
    row_ref[...] = jnp.full_like(row_ref, CLIP)
    col_ref[...] = jnp.full_like(col_ref, CLIP)

    def column(n, carry):
        start = pl.multiple_of(n * COLS, COLS)
        limit = jnp.minimum(row_tiles, (n + 1) * (COLS // ROWS))
        sweep(left_ref, right_ref, acc_ref, row_ref, col_ref, 0, limit, start, first, last, n >= 0)
        return carry

    lax.fori_loop(0, tiles_of(count, COLS), column, 0)
    out_ref[...] = jnp.minimum(by_row(row_ref, 0), col_ref[...])


def neighbour_kernel(
    cells, cell_ref, plan_ref, next_ref, prev_ref, base_ref, left_in_ref, synth_hbm, left_sel_hbm, right_sel_hbm,
    out_ref, next_out_ref, prev_out_ref, left_ref,
    right_ref, acc_ref, row_ref, col_ref, synth_ref, left_sel_ref, right_sel_ref, track_ref, flag_ref, sem,
):
    del left_in_ref
    copies = fetched((synth_hbm, left_sel_hbm, right_sel_hbm), (synth_ref, left_sel_ref, right_sel_ref), sem)
    cell = cell_ref[0]
    after, ahead = cell + 1, cell + (cells - 1)
    own_rows = tiles_of(planned(plan_ref, 0, cell, cells), ROWS)
    own_share, their_share = planned(plan_ref, 1, cell, cells), planned(plan_ref, 1, ahead, cells)
    of_next, of_prev = planned(plan_ref, 2, after, cells), planned(plan_ref, 3, ahead, cells)
    next_count, prev_count = planned(plan_ref, 0, after, cells), planned(plan_ref, 0, ahead, cells)
    offset = left_ref.shape[0] // 2
    for copy in copies:
        copy.wait()
    row_ref[0] = jnp.full(row_ref.shape[1:], CLIP, jnp.float32)

    def phase(p, carry):
        forward = p == 0
        cross = jnp.where(forward, 0, their_share), jnp.where(forward, own_share, UNITS)
        alone = jnp.where(forward, 0, UNITS - of_prev), jnp.where(forward, of_next, UNITS)
        cross_on, alone_on = cross[0] < cross[1], alone[0] < alone[1]
        first = jnp.minimum(cross[0], alone[0])
        last = jnp.maximum(cross[1], alone[1])
        count = jnp.where(forward, next_count, prev_count)
        other_rows, other_cols = tiles_of(count, ROWS), tiles_of(count, COLS)

        @pl.when(forward & (first < last))
        def _():
            tracks(next_ref, synth_ref, track_ref, flag_ref, ())

        @pl.when((p == 1) & (first < last))
        def _():
            tracks(prev_ref, synth_ref, track_ref, flag_ref, ())

        def unit_step(unit, c):
            source = source_of(track_ref, flag_ref, unit)
            put_right(source, right_sel_ref, right_ref, unit)

            @pl.when((unit >= alone[0]) & (unit < alone[1]))
            def _():
                put_left(source, left_sel_ref, left_ref, unit, offset)

            return c

        lax.fori_loop(first, last, unit_step, 0)
        row_ref[1] = jnp.full(row_ref.shape[1:], CLIP, jnp.float32)
        col_ref[...] = jnp.full_like(col_ref, CLIP)

        def column(k, c):
            job = jnp.where(k < other_cols, 0, 1)
            n = k - job * other_cols
            start = pl.multiple_of(n * COLS, COLS)
            limit = jnp.where(job == 0, own_rows, jnp.minimum(other_rows, (n + 1) * (COLS // ROWS)))
            low, high = jnp.where(job == 0, cross[0], alone[0]), jnp.where(job == 0, cross[1], alone[1])
            sweep(left_ref, right_ref, acc_ref, row_ref, col_ref, job, limit, start, low, high, job == 1)
            return c

        lax.fori_loop(
            jnp.where(cross_on, 0, other_cols), jnp.where(alone_on, 2 * other_cols, other_cols), column, 0
        )
        best = jnp.minimum(col_ref[...], by_row(row_ref, 1))

        @pl.when(forward)
        def _():
            next_out_ref[...] = best

        @pl.when(p == 1)
        def _():
            prev_out_ref[...] = best

        return carry

    lax.fori_loop(0, 2, phase, 0)
    out_ref[...] = jnp.minimum(by_row(row_ref, 0), base_ref[...])


def restore_kernel(*refs):
    *minima, chosen_ref, out_ref = refs
    count = out_ref.shape[1]
    best = functools.reduce(jnp.minimum, [ref[...] for ref in minima])
    pieces = split(best, 3)[0]
    ones, zeros = jnp.ones((1, count), jnp.float32), jnp.zeros((12, count), jnp.float32)
    rows = jnp.concatenate(pieces + [ones, zeros], axis=0).astype(BF16)
    found = jnp.dot(rows, chosen_ref[...], preferred_element_type=jnp.float32)
    value = found[0:1] + found[1:2] + found[2:3]
    out_ref[...] = jnp.where(found[3:4] > 0.5, value, CLIP)


VMEM = pl.BlockSpec(memory_space=pltpu.VMEM)
SMEM = pl.BlockSpec(memory_space=pltpu.SMEM)
ANY = pl.BlockSpec(memory_space=pl.ANY)


def call(kernel, name, out_shape, in_specs, scratch, vmem, flops, aliases=None):
    return pl.pallas_call(
        kernel,
        out_shape=out_shape,
        in_specs=in_specs,
        out_specs=jax.tree.map(lambda _: VMEM, out_shape),
        scratch_shapes=scratch,
        compiler_params=pltpu.CompilerParams(vmem_limit_bytes=vmem << 20),
        cost_estimate=pl.CostEstimate(flops=flops, bytes_accessed=4_000_000, transcendentals=0),
        input_output_aliases=aliases or {},
        name=name,
    )


def body(cheb_coef, obj_cell):
    objects = cheb_coef.shape[3]
    own = cheb_coef.reshape(3 * DEG1, 1, objects)
    cells = lax.axis_size("cell")
    slots = cells * CAP
    windows = lax.axis_size("tm")
    window = lax.axis_index("tm").astype(jnp.int32).reshape(1)
    prev = lax.ppermute(own, "tm", [(i, i + 1) for i in range(windows - 1)])
    row = jax.ShapeDtypeStruct((1, slots), jnp.float32)
    cell = lax.axis_index("cell").astype(jnp.int32).reshape(1)
    wide = jax.ShapeDtypeStruct((slots, LANES), jnp.float32)
    packed_shape = jax.ShapeDtypeStruct((cells * PACK, LANES), jnp.float32)
    rows_scratch = [pltpu.VMEM((LANES, objects), jnp.float32)]
    chosen, base = call(
        place_kernel,
        "place",
        (jax.ShapeDtypeStruct((cells * PACK, 2 * objects), BF16), packed_shape),
        [VMEM, VMEM],
        rows_scratch,
        12,
        2_000_000_000,
    )(obj_cell.reshape(1, objects), own)
    send = call(
        front_kernel, "front", packed_shape, [SMEM] + [VMEM] * 5, rows_scratch, 12, 2_000_000_000
    )(window, own, prev, chosen, base, jnp.asarray(rim_tables()))
    packed = lax.all_to_all(send, "cell", split_axis=0, concat_axis=0, tiled=True)
    live, chosen, counts = call(
        compact_kernel,
        "compact",
        (wide, jax.ShapeDtypeStruct((slots, slots), BF16), jax.ShapeDtypeStruct((1, LANES), jnp.float32)),
        [VMEM],
        [],
        16,
        2_000_000_000,
    )(packed)
    forward = [(i, (i + 1) % cells) for i in range(cells)]
    backward = [((i + 1) % cells, i) for i in range(cells)]
    next_live = lax.ppermute(live, "cell", backward)
    prev_live = lax.ppermute(live, "cell", forward)
    synth = jnp.asarray(synth_matrix())
    left_sel = jnp.asarray(np.ascontiguousarray(selection(True).T))
    right_sel = jnp.asarray(selection(False))
    left_shape = jax.ShapeDtypeStruct((2 * (EXT // GROUP), slots, LANES), BF16)
    scratch = [
        pltpu.VMEM((EXT, PIECES, slots), BF16),
        pltpu.VMEM((slots, COLS), jnp.float32),
        pltpu.VMEM((2, slots, LANES), jnp.float32),
        pltpu.VMEM((1, slots), jnp.float32),
        pltpu.VMEM(synth.shape, BF16),
        pltpu.VMEM(left_sel.shape, BF16),
        pltpu.VMEM(right_sel.shape, BF16),
        pltpu.VMEM((3, UNITS, CHUNK, slots), jnp.float32),
        pltpu.VMEM((CHUNK, slots), jnp.float32),
        pltpu.SemaphoreType.DMA((3,)),
    ]
    own_min, left, shares = call(
        functools.partial(self_kernel, cells),
        "self_screen",
        (row, left_shape, jax.ShapeDtypeStruct((8, LANES), jnp.float32)),
        [SMEM, VMEM, VMEM, ANY, ANY, ANY],
        scratch,
        40,
        15_000_000_000,
    )(cell, live, counts, synth, left_sel, right_sel)
    best, next_min, prev_min, _ = call(
        functools.partial(neighbour_kernel, cells),
        "neighbour_screen",
        (row, row, row, left_shape),
        [SMEM] + [VMEM] * 5 + [ANY] * 3,
        scratch,
        40,
        20_000_000_000,
        {5: 3},
    )(cell, shares, next_live, prev_live, own_min, left, synth, left_sel, right_sel)
    from_prev = lax.ppermute(next_min, "cell", forward)
    from_next = lax.ppermute(prev_min, "cell", backward)
    return call(restore_kernel, "restore", row, [VMEM] * 4, [], 8, 100_000_000)(best, from_prev, from_next, chosen)


def solution(mesh):
    in_specs = (P("tm", None, None, "cell"), P("tm", "cell", None))
    return jax.shard_map(body, mesh=mesh, in_specs=in_specs, out_specs=P("tm", "cell"), check_vma=False)
```

```python
import functools

import jax
import jax.numpy as jnp
import ml_dtypes
import numpy as np
from jax import lax
from jax.experimental import pallas as pl
from jax.experimental.pallas import tpu as pltpu
from jax.sharding import PartitionSpec as P

DEG1 = 17
SAMP = 64
RIM = 8
CAP = 24
EXT = SAMP + RIM
CLIP = 25.0
FAR = 1.0e9

LANES = 128
FLAG_AT = 3 * DEG1
RIM_AT = FLAG_AT + 1
RECORD = RIM_AT + 3 * RIM
PACK = 16
LATE = CAP - PACK
COUNT_AT = RECORD + 3 * RIM
HALF = 16

PIECES = 32
GROUP = LANES // PIECES
CHUNK = 8
UNITS = EXT // CHUNK
PARTS = 2
NORMS = 3
KINDS = 3 * PARTS + NORMS
SRC = 80
TERMS = 80
ROWS = 128
COLS = 256
BF16 = jnp.bfloat16


def cheb_table():
    nodes = ((2.0 * np.arange(SAMP, dtype=np.float32) + 1.0) / SAMP - 1.0).astype(np.float32)
    columns = [np.ones_like(nodes), nodes]
    for _ in range(2, DEG1):
        columns.append((2.0 * nodes * columns[-1] - columns[-2]).astype(np.float32))
    return np.stack(columns, axis=1)


def rim_tables():
    table = cheb_table()
    return np.stack([table[:RIM], table[SAMP - RIM :]])


def synth_matrix():
    table = cheb_table()
    weights = np.zeros((3 * EXT, LANES), np.float32)
    for c in range(3):
        for s in range(RIM):
            weights[c * EXT + s, RIM_AT + RIM * c + s] = 1.0
        weights[c * EXT + RIM : (c + 1) * EXT, DEG1 * c : DEG1 * (c + 1)] = table
    high = weights[:, :TERMS].astype(ml_dtypes.bfloat16)
    low = (weights[:, :TERMS] - high.astype(np.float32)).astype(ml_dtypes.bfloat16)
    return np.concatenate([high, high, low, np.zeros((3 * EXT, 2 * LANES - 3 * TERMS), high.dtype)], axis=1)


def selection(left):
    one = KINDS
    uses = []
    for i in range(PARTS):
        for j in range(PARTS):
            for c in range(3):
                uses.append((3 * i + c, 1.0) if left else (3 * j + c, -1.0))
    for n in range(NORMS):
        uses.append((3 * PARTS + n, 1.0) if left else (one, 1.0))
    for n in range(NORMS):
        uses.append((one, 1.0) if left else (3 * PARTS + n, 1.0))
    matrix = np.zeros((CHUNK * PIECES, SRC), np.float32)
    for t in range(CHUNK):
        for k, (kind, value) in enumerate(uses):
            matrix[t * PIECES + k, kind * CHUNK + (0 if kind == one else t)] = value
    return matrix.astype(ml_dtypes.bfloat16)


def split(value, count):
    pieces = []
    for _ in range(count):
        piece = value.astype(BF16).astype(jnp.float32)
        value = value - piece
        pieces.append(piece)
    return pieces, value


def one_hot(row_ids, names):
    return jnp.where(row_ids == jnp.broadcast_to(names, row_ids.shape), 1.0, 0.0).astype(BF16)


def placed(chosen, data):
    high = data.astype(BF16)
    low = (data - high.astype(jnp.float32)).astype(BF16)
    found = jnp.dot(chosen, jnp.concatenate([high, low], axis=1), preferred_element_type=jnp.float32)
    return found[:, :LANES] + found[:, LANES:]


def place_kernel(cell_ref, own_ref, chosen_ref, base_ref, rows_ref):
    rows = chosen_ref.shape[0]
    count = cell_ref.shape[1]
    cell = cell_ref[...].astype(jnp.float32)
    column = jnp.transpose(jnp.broadcast_to(cell, (LANES, count)))
    lane = lax.broadcasted_iota(jnp.int32, (count, LANES), 1)
    counts = []
    for n in range(2):
        name = jnp.where((lane >= COUNT_AT) & (lane < COUNT_AT + HALF), lane - COUNT_AT + n * HALF, -1)
        named = jnp.where(column == name.astype(jnp.float32), 1.0, 0.0)
        counts.append(jnp.sum(named, axis=0, keepdims=True))
    column = jnp.concatenate([column] * (count // LANES), axis=1)
    before = lax.broadcasted_iota(jnp.int32, (count, count), 0) < lax.broadcasted_iota(jnp.int32, (count, count), 1)
    same = (column == jnp.broadcast_to(cell, (count, count))) & before
    rank = jnp.sum(jnp.where(same, 1.0, 0.0), axis=0, keepdims=True)
    early = jnp.where(rank < PACK, cell * PACK + rank, -1.0).astype(jnp.int32)
    late = jnp.where(rank < PACK, -1.0, cell * PACK + rank - PACK).astype(jnp.int32)
    ids = lax.broadcasted_iota(jnp.int32, (rows, count), 0)
    early = one_hot(ids, early)
    chosen_ref[:, 0:count] = early
    chosen_ref[:, count : 2 * count] = one_hot(ids, jnp.where(late < 0, -1, late + LATE))
    rows_ref[...] = jnp.zeros_like(rows_ref)
    rows_ref[0:FLAG_AT, :] = own_ref[:, 0, :]
    rows_ref[FLAG_AT : FLAG_AT + 1, :] = jnp.ones((1, count), jnp.float32)
    data = jnp.transpose(rows_ref[...])
    data = jnp.concatenate([data, jnp.where(lane >= RECORD, pltpu.roll(data, RECORD, 1), 0.0)], axis=0)
    found = placed(jnp.concatenate([early, one_hot(ids, late)], axis=1), data)
    row = lax.rem(lax.broadcasted_iota(jnp.int32, found.shape, 0), PACK)
    held = jnp.where(lax.rem(row, 2) == 0, counts[0], counts[1])
    base_ref[...] = found + jnp.where(row >= LATE, held, 0.0)


def front_kernel(first_ref, own_ref, prev_ref, chosen_ref, base_ref, table_ref, out_ref, rows_ref):
    first = first_ref[0] == 0
    rows_ref[...] = jnp.zeros_like(rows_ref)
    table = jnp.where(first, table_ref[0], table_ref[1])
    for c in range(3):
        rows = slice(c * DEG1, (c + 1) * DEG1)
        source = jnp.where(first, own_ref[rows, 0, :], prev_ref[rows, 0, :])
        rows_ref[RIM_AT + RIM * c : RIM_AT + RIM * (c + 1), :] = jnp.dot(
            table, source, precision=lax.Precision.HIGHEST, preferred_element_type=jnp.float32
        )
    data = jnp.transpose(rows_ref[...])
    data = jnp.concatenate([data, pltpu.roll(data, RECORD - RIM_AT, 1)], axis=0)
    out_ref[...] = placed(chosen_ref[...], data) + base_ref[...]


def plan(counts):
    rows = jnp.maximum(jnp.ceil(counts / ROWS), 1.0) * ROWS
    tiles = jnp.maximum(jnp.ceil(counts / COLS), 1.0)
    fixed, per_row, extra, least = 0.0278, 1.244e-3, 0.26, 0.12
    alone = 0.0005 * tiles + 1.346e-3 * (
        jnp.minimum(rows, COLS)
        + jnp.where(tiles > 1.5, jnp.minimum(rows, 2 * COLS), 0.0)
        + jnp.where(tiles > 2.5, rows, 0.0)
    )
    after = lambda value: pltpu.roll(value, LANES - 1, 1)
    ahead = lambda value: pltpu.roll(value, 1, 1)
    here = after(tiles) * (fixed + per_row * rows) + extra
    there = tiles * (fixed + per_row * after(rows)) + extra
    lent = 0.92 * alone + tiles * fixed + 0.38
    cross_step, self_step = 0.5 / (here + there), 0.1 / alone
    share, before, behind = jnp.full_like(counts, 0.5), jnp.zeros_like(counts), jnp.zeros_like(counts)
    for _ in range(20):
        load = (
            alone * (1.0 - before - behind)
            + share * here
            + ahead((1.0 - share) * there + behind * lent)
            + after(before * lent)
        )
        up, down = after(load) - load, load - ahead(load)
        share = jnp.clip(share + cross_step * up, 0.0, 1.0)
        before = jnp.clip(before + self_step * (down - least), 0.0, 0.45)
        behind = jnp.clip(behind - self_step * (up + least), 0.0, 0.45)
    return [jnp.floor(value * UNITS + 0.5) for value in (share, before, behind)]


def records(packed):
    tiles = packed.reshape(packed.shape[0] // PACK, 2, LATE, LANES)
    blocks = tiles.shape[0]
    flat = (blocks * LATE, LANES)
    low, high = tiles[:, 0].reshape(flat), tiles[:, 1].reshape(flat)
    lane = lax.broadcasted_iota(jnp.int32, flat, 1)
    late = jnp.where(
        lane < RIM_AT,
        pltpu.roll(low, LANES - RECORD, 1),
        jnp.where(lane < RECORD, pltpu.roll(high, LANES - (RECORD - RIM_AT), 1), 0.0),
    )
    each = [v.reshape(blocks, 1, LATE, LANES) for v in (low, high, late)]
    return jnp.concatenate(each, axis=1).reshape(blocks * CAP, LANES), high


def cell_counts(high):
    row = lax.rem(lax.broadcasted_iota(jnp.int32, high.shape, 0), 2)
    lane = lax.broadcasted_iota(jnp.int32, high.shape, 1)
    held = jnp.where((lane >= COUNT_AT) & (lane < COUNT_AT + HALF), high, 0.0)
    total = None
    for n in range(2):
        part = jnp.sum(jnp.where(row == n, held, 0.0), axis=0, keepdims=True) * (2.0 / LATE)
        part = pltpu.roll(part, (n * HALF - COUNT_AT) % LANES, 1)
        total = part if total is None else total + part
    total = total + pltpu.roll(total, 2 * HALF, 1)
    return total + pltpu.roll(total, 4 * HALF, 1)


def compact_kernel(packed_ref, live_ref, chosen_ref, count_ref):
    data, high = records(packed_ref[...])
    slots = data.shape[0]
    flag = jnp.transpose(data)[FLAG_AT : FLAG_AT + 1, :]
    first = lax.broadcasted_iota(jnp.int32, (slots, slots), 0)
    second = lax.broadcasted_iota(jnp.int32, (slots, slots), 1)
    before = jnp.where(first < second, 1.0, 0.0).astype(BF16)
    flags = jnp.broadcast_to(flag, (16, slots)).astype(BF16)
    place = jnp.dot(flags, before, preferred_element_type=jnp.float32)[0:1]
    place = jnp.where(flag > 0.5, place, -1.0).astype(jnp.int32)
    chosen = one_hot(first, place)
    chosen_ref[...] = chosen
    live_ref[...] = placed(chosen, data)
    count_ref[...] = cell_counts(high)


def fetched(sources, targets, sem):
    copies = [pltpu.make_async_copy(s, t, sem.at[i]) for i, (s, t) in enumerate(zip(sources, targets))]
    for copy in copies:
        copy.start()
    return copies


def tracks(live_ref, synth_ref, track_ref, flag_ref, copies):
    live = jnp.transpose(live_ref[...])
    flag_ref[...] = jnp.broadcast_to(live[FLAG_AT : FLAG_AT + 1, :], flag_ref.shape)
    for copy in copies:
        copy.wait()
    (high, low), _ = split(live[:TERMS], 2)
    rest = jnp.zeros((2 * LANES - 3 * TERMS, live.shape[1]), jnp.float32)
    terms = jnp.concatenate([high, low, high, rest], axis=0).astype(BF16)
    track = jnp.dot(synth_ref[...], terms, preferred_element_type=jnp.float32)
    track_ref[...] = track.reshape(track_ref.shape)


def source_of(track_ref, flag_ref, unit):
    count = track_ref.shape[3]
    parts, norm = [], None
    for c in range(3):
        axis = track_ref[c, unit]
        pieces, rest = split(axis, PARTS)
        parts.append(pieces)
        held = axis - rest
        norm = held * held if norm is None else norm + held * held
    norm = jnp.where(flag_ref[...] > 0.5, 0.5 * norm, FAR)
    kinds = [parts[c][i] for i in range(PARTS) for c in range(3)] + split(norm, NORMS)[0]
    ones = jnp.ones((CHUNK, count), jnp.float32)
    return jnp.concatenate(kinds + [ones], axis=0)


def put_right(source, right_sel_ref, right_ref, unit):
    right = jnp.dot(right_sel_ref[...], source.astype(BF16), preferred_element_type=jnp.float32)
    right_ref[pl.ds(unit * CHUNK, CHUNK)] = right.astype(BF16).reshape(CHUNK, PIECES, right.shape[1])


def put_left(source, left_sel_ref, left_ref, unit, offset):
    left = jnp.dot(jnp.transpose(source).astype(BF16), left_sel_ref[...], preferred_element_type=jnp.float32)
    left = left.astype(BF16)
    for g in range(CHUNK // GROUP):
        left_ref[offset + unit * (CHUNK // GROUP) + g] = left[:, g * LANES : (g + 1) * LANES]


def sweep(left_ref, right_ref, acc_ref, row_ref, col_ref, job, row_tiles, col_start, first, last, diagonal):
    groups = CHUNK // GROUP
    offset = job * (EXT // GROUP)
    columns = pl.ds(col_start, COLS)

    def screen(rows, unit, units):
        best = acc_ref[0:rows, :]
        for h in range(units * groups):
            g = unit * groups + h
            left = left_ref[offset + g, 0:rows, :]
            for j in range(GROUP):
                parts = [right_ref[g * GROUP + j, :, columns]]
                if j > 0:
                    parts = [jnp.zeros((PIECES * j, COLS), BF16)] + parts
                if j < GROUP - 1:
                    parts = parts + [jnp.zeros((PIECES * (GROUP - 1 - j), COLS), BF16)]
                weights = jnp.concatenate(parts, axis=0)
                best = jnp.minimum(best, jnp.dot(left, weights, preferred_element_type=jnp.float32))
        acc_ref[0:rows, :] = best

    for n in range(1, acc_ref.shape[0] // ROWS + 1):

        @pl.when(row_tiles == n)
        def _(rows=n * ROWS, each=2 if n < 4 or n == 6 else 1):
            acc_ref[0:rows, :] = jnp.full((rows, COLS), CLIP, jnp.float32)
            steps = (last - first) // each

            def step(i, carry):
                screen(rows, first + i * each, each)
                return carry

            lax.fori_loop(0, steps, step, 0)
            if each > 1:

                @pl.when(first + steps * each < last)
                def _():
                    screen(rows, last - 1, 1)

            @pl.when(diagonal)
            def _():
                same = lax.broadcasted_iota(jnp.int32, (COLS, COLS), 0) == lax.broadcasted_iota(
                    jnp.int32, (COLS, COLS), 1
                )
                near = pl.ds(col_start, COLS)
                acc_ref[near, :] = jnp.where(same, CLIP, acc_ref[near, :])

            acc = acc_ref[0:rows, :]
            half = jnp.minimum(acc[:, :LANES], acc[:, LANES:])
            row_ref[job, 0:rows, :] = jnp.minimum(row_ref[job, 0:rows, :], half)
            best = finished(jnp.min(acc, axis=0, keepdims=True))
            col_ref[:, columns] = jnp.minimum(col_ref[:, columns], best)


def by_row(row_ref, job):
    return finished(jnp.min(jnp.transpose(row_ref[job]), axis=0, keepdims=True))


def finished(half):
    return jnp.clip(2.0 * half, 0.0, CLIP)


def planned(plan_ref, row, cell, cells):
    lane = lax.broadcasted_iota(jnp.int32, (1, LANES), 1)
    value = jnp.sum(jnp.where(lane == lax.rem(cell, cells), plan_ref[row : row + 1, :], 0.0))
    return value.astype(jnp.int32)


def tiles_of(count, size):
    return jnp.maximum((count + (size - 1)) // size, 1)


def self_kernel(
    cells, cell_ref, live_ref, count_ref, synth_hbm, left_sel_hbm, right_sel_hbm, out_ref, left_ref, plan_ref,
    right_ref, acc_ref, row_ref, col_ref, synth_ref, left_sel_ref, right_sel_ref, track_ref, flag_ref, sem,
):
    copies = fetched((synth_hbm, left_sel_hbm, right_sel_hbm), (synth_ref, left_sel_ref, right_sel_ref), sem)
    tracks(live_ref, synth_ref, track_ref, flag_ref, copies)
    counts = count_ref[...]
    plan_ref[0:1, :] = counts
    for n, units in enumerate(plan(counts)):
        plan_ref[n + 1 : n + 2, :] = units
    for unit in range(UNITS):
        source = source_of(track_ref, flag_ref, unit)
        put_right(source, right_sel_ref, right_ref, unit)
        put_left(source, left_sel_ref, left_ref, unit, 0)
    cell = cell_ref[0]
    count = planned(plan_ref, 0, cell, cells)
    first, last = planned(plan_ref, 2, cell, cells), UNITS - planned(plan_ref, 3, cell, cells)
    row_tiles = tiles_of(count, ROWS)
    row_ref[...] = jnp.full_like(row_ref, CLIP)
    col_ref[...] = jnp.full_like(col_ref, CLIP)

    def column(n, carry):
        start = pl.multiple_of(n * COLS, COLS)
        limit = jnp.minimum(row_tiles, (n + 1) * (COLS // ROWS))
        sweep(left_ref, right_ref, acc_ref, row_ref, col_ref, 0, limit, start, first, last, n >= 0)
        return carry

    lax.fori_loop(0, tiles_of(count, COLS), column, 0)
    out_ref[...] = jnp.minimum(by_row(row_ref, 0), col_ref[...])


def neighbour_kernel(
    cells, cell_ref, plan_ref, next_ref, prev_ref, base_ref, left_in_ref, synth_hbm, left_sel_hbm, right_sel_hbm,
    out_ref, next_out_ref, prev_out_ref, left_ref,
    right_ref, acc_ref, row_ref, col_ref, synth_ref, left_sel_ref, right_sel_ref, track_ref, flag_ref, sem,
):
    del left_in_ref
    copies = fetched((synth_hbm, left_sel_hbm, right_sel_hbm), (synth_ref, left_sel_ref, right_sel_ref), sem)
    cell = cell_ref[0]
    after, ahead = cell + 1, cell + (cells - 1)
    own_rows = tiles_of(planned(plan_ref, 0, cell, cells), ROWS)
    own_share, their_share = planned(plan_ref, 1, cell, cells), planned(plan_ref, 1, ahead, cells)
    of_next, of_prev = planned(plan_ref, 2, after, cells), planned(plan_ref, 3, ahead, cells)
    next_count, prev_count = planned(plan_ref, 0, after, cells), planned(plan_ref, 0, ahead, cells)
    offset = left_ref.shape[0] // 2
    for copy in copies:
        copy.wait()
    row_ref[0] = jnp.full(row_ref.shape[1:], CLIP, jnp.float32)

    def phase(p, carry):
        forward = p == 0
        cross = jnp.where(forward, 0, their_share), jnp.where(forward, own_share, UNITS)
        alone = jnp.where(forward, 0, UNITS - of_prev), jnp.where(forward, of_next, UNITS)
        cross_on, alone_on = cross[0] < cross[1], alone[0] < alone[1]
        first = jnp.minimum(cross[0], alone[0])
        last = jnp.maximum(cross[1], alone[1])
        count = jnp.where(forward, next_count, prev_count)
        other_rows, other_cols = tiles_of(count, ROWS), tiles_of(count, COLS)

        @pl.when(forward & (first < last))
        def _():
            tracks(next_ref, synth_ref, track_ref, flag_ref, ())

        @pl.when((p == 1) & (first < last))
        def _():
            tracks(prev_ref, synth_ref, track_ref, flag_ref, ())

        def right_step(i, c):
            for u in range(2):
                unit = jnp.minimum(first + 2 * i + u, UNITS - 1)
                put_right(source_of(track_ref, flag_ref, unit), right_sel_ref, right_ref, unit)
            return c

        def left_step(unit, c):
            put_left(source_of(track_ref, flag_ref, unit), left_sel_ref, left_ref, unit, offset)
            return c

        lax.fori_loop(0, (last - first + 1) // 2, right_step, 0)
        lax.fori_loop(alone[0], alone[1], left_step, 0)
        row_ref[1] = jnp.full(row_ref.shape[1:], CLIP, jnp.float32)
        col_ref[...] = jnp.full_like(col_ref, CLIP)

        def column(k, c):
            job = jnp.where(k < other_cols, 0, 1)
            n = k - job * other_cols
            start = pl.multiple_of(n * COLS, COLS)
            limit = jnp.where(job == 0, own_rows, jnp.minimum(other_rows, (n + 1) * (COLS // ROWS)))
            low, high = jnp.where(job == 0, cross[0], alone[0]), jnp.where(job == 0, cross[1], alone[1])
            sweep(left_ref, right_ref, acc_ref, row_ref, col_ref, job, limit, start, low, high, job == 1)
            return c

        lax.fori_loop(
            jnp.where(cross_on, 0, other_cols), jnp.where(alone_on, 2 * other_cols, other_cols), column, 0
        )
        best = jnp.minimum(col_ref[...], by_row(row_ref, 1))

        @pl.when(forward)
        def _():
            next_out_ref[...] = best

        @pl.when(p == 1)
        def _():
            prev_out_ref[...] = best

        return carry

    lax.fori_loop(0, 2, phase, 0)
    out_ref[...] = jnp.minimum(by_row(row_ref, 0), base_ref[...])


def restore_kernel(*refs):
    *minima, chosen_ref, out_ref = refs
    count = out_ref.shape[1]
    best = functools.reduce(jnp.minimum, [ref[...] for ref in minima])
    pieces = split(best, 3)[0]
    ones, zeros = jnp.ones((1, count), jnp.float32), jnp.zeros((12, count), jnp.float32)
    rows = jnp.concatenate(pieces + [ones, zeros], axis=0).astype(BF16)
    found = jnp.dot(rows, chosen_ref[...], preferred_element_type=jnp.float32)
    value = found[0:1] + found[1:2] + found[2:3]
    out_ref[...] = jnp.where(found[3:4] > 0.5, value, CLIP)


VMEM = pl.BlockSpec(memory_space=pltpu.VMEM)
SMEM = pl.BlockSpec(memory_space=pltpu.SMEM)
ANY = pl.BlockSpec(memory_space=pl.ANY)


def call(kernel, name, out_shape, in_specs, scratch, vmem, flops, aliases=None):
    return pl.pallas_call(
        kernel,
        out_shape=out_shape,
        in_specs=in_specs,
        out_specs=jax.tree.map(lambda _: VMEM, out_shape),
        scratch_shapes=scratch,
        compiler_params=pltpu.CompilerParams(vmem_limit_bytes=vmem << 20),
        cost_estimate=pl.CostEstimate(flops=flops, bytes_accessed=4_000_000, transcendentals=0),
        input_output_aliases=aliases or {},
        name=name,
    )


def body(cheb_coef, obj_cell):
    objects = cheb_coef.shape[3]
    own = cheb_coef.reshape(3 * DEG1, 1, objects)
    cells = lax.axis_size("cell")
    slots = cells * CAP
    windows = lax.axis_size("tm")
    window = lax.axis_index("tm").astype(jnp.int32).reshape(1)
    prev = lax.ppermute(own, "tm", [(i, i + 1) for i in range(windows - 1)])
    row = jax.ShapeDtypeStruct((1, slots), jnp.float32)
    cell = lax.axis_index("cell").astype(jnp.int32).reshape(1)
    wide = jax.ShapeDtypeStruct((slots, LANES), jnp.float32)
    packed_shape = jax.ShapeDtypeStruct((cells * PACK, LANES), jnp.float32)
    rows_scratch = [pltpu.VMEM((LANES, objects), jnp.float32)]
    chosen, base = call(
        place_kernel,
        "place",
        (jax.ShapeDtypeStruct((cells * PACK, 2 * objects), BF16), packed_shape),
        [VMEM, VMEM],
        rows_scratch,
        12,
        2_000_000_000,
    )(obj_cell.reshape(1, objects), own)
    send = call(
        front_kernel, "front", packed_shape, [SMEM] + [VMEM] * 5, rows_scratch, 12, 2_000_000_000
    )(window, own, prev, chosen, base, jnp.asarray(rim_tables()))
    packed = lax.all_to_all(send, "cell", split_axis=0, concat_axis=0, tiled=True)
    live, chosen, counts = call(
        compact_kernel,
        "compact",
        (wide, jax.ShapeDtypeStruct((slots, slots), BF16), jax.ShapeDtypeStruct((1, LANES), jnp.float32)),
        [VMEM],
        [],
        16,
        2_000_000_000,
    )(packed)
    forward = [(i, (i + 1) % cells) for i in range(cells)]
    backward = [((i + 1) % cells, i) for i in range(cells)]
    next_live = lax.ppermute(live, "cell", backward)
    prev_live = lax.ppermute(live, "cell", forward)
    synth = jnp.asarray(synth_matrix())
    left_sel = jnp.asarray(np.ascontiguousarray(selection(True).T))
    right_sel = jnp.asarray(selection(False))
    left_shape = jax.ShapeDtypeStruct((2 * (EXT // GROUP), slots, LANES), BF16)
    scratch = [
        pltpu.VMEM((EXT, PIECES, slots), BF16),
        pltpu.VMEM((slots, COLS), jnp.float32),
        pltpu.VMEM((2, slots, LANES), jnp.float32),
        pltpu.VMEM((1, slots), jnp.float32),
        pltpu.VMEM(synth.shape, BF16),
        pltpu.VMEM(left_sel.shape, BF16),
        pltpu.VMEM(right_sel.shape, BF16),
        pltpu.VMEM((3, UNITS, CHUNK, slots), jnp.float32),
        pltpu.VMEM((CHUNK, slots), jnp.float32),
        pltpu.SemaphoreType.DMA((3,)),
    ]
    own_min, left, shares = call(
        functools.partial(self_kernel, cells),
        "self_screen",
        (row, left_shape, jax.ShapeDtypeStruct((8, LANES), jnp.float32)),
        [SMEM, VMEM, VMEM, ANY, ANY, ANY],
        scratch,
        40,
        15_000_000_000,
    )(cell, live, counts, synth, left_sel, right_sel)
    best, next_min, prev_min, _ = call(
        functools.partial(neighbour_kernel, cells),
        "neighbour_screen",
        (row, row, row, left_shape),
        [SMEM] + [VMEM] * 5 + [ANY] * 3,
        scratch,
        40,
        20_000_000_000,
        {5: 3},
    )(cell, shares, next_live, prev_live, own_min, left, synth, left_sel, right_sel)
    from_prev = lax.ppermute(next_min, "cell", forward)
    from_next = lax.ppermute(prev_min, "cell", backward)
    return call(restore_kernel, "restore", row, [VMEM] * 4, [], 8, 100_000_000)(best, from_prev, from_next, chosen)


def solution(mesh):
    in_specs = (P("tm", None, None, "cell"), P("tm", "cell", None))
    return jax.shard_map(body, mesh=mesh, in_specs=in_specs, out_specs=P("tm", "cell"), check_vma=False)
```

```python
import functools

import jax
import jax.numpy as jnp
import ml_dtypes
import numpy as np
from jax import lax
from jax.experimental import pallas as pl
from jax.experimental.pallas import tpu as pltpu
from jax.sharding import PartitionSpec as P

DEG1 = 17
SAMP = 64
RIM = 8
CAP = 24
EXT = SAMP + RIM
CLIP = 25.0
FAR = 1.0e9

LANES = 128
FLAG_AT = 3 * DEG1
RIM_AT = FLAG_AT + 1
RECORD = RIM_AT + 3 * RIM
PACK = 16
LATE = CAP - PACK
COUNT_AT = RECORD + 3 * RIM
HALF = 16

PIECES = 32
GROUP = LANES // PIECES
CHUNK = 8
UNITS = EXT // CHUNK
PARTS = 2
NORMS = 3
KINDS = 3 * PARTS + NORMS
SRC = 80
TERMS = 80
ROWS = 128
COLS = 256
BF16 = jnp.bfloat16


def cheb_table():
    nodes = ((2.0 * np.arange(SAMP, dtype=np.float32) + 1.0) / SAMP - 1.0).astype(np.float32)
    columns = [np.ones_like(nodes), nodes]
    for _ in range(2, DEG1):
        columns.append((2.0 * nodes * columns[-1] - columns[-2]).astype(np.float32))
    return np.stack(columns, axis=1)


def rim_tables():
    table = cheb_table()
    return np.stack([table[:RIM], table[SAMP - RIM :]])


def synth_matrix():
    table = cheb_table()
    weights = np.zeros((3 * EXT, LANES), np.float32)
    for c in range(3):
        for s in range(RIM):
            weights[c * EXT + s, RIM_AT + RIM * c + s] = 1.0
        weights[c * EXT + RIM : (c + 1) * EXT, DEG1 * c : DEG1 * (c + 1)] = table
    high = weights[:, :TERMS].astype(ml_dtypes.bfloat16)
    low = (weights[:, :TERMS] - high.astype(np.float32)).astype(ml_dtypes.bfloat16)
    return np.concatenate([high, high, low, np.zeros((3 * EXT, 2 * LANES - 3 * TERMS), high.dtype)], axis=1)


def selection(left):
    one = KINDS
    uses = []
    for i in range(PARTS):
        for j in range(PARTS):
            for c in range(3):
                uses.append((3 * i + c, 1.0) if left else (3 * j + c, -1.0))
    for n in range(NORMS):
        uses.append((3 * PARTS + n, 1.0) if left else (one, 1.0))
    for n in range(NORMS):
        uses.append((one, 1.0) if left else (3 * PARTS + n, 1.0))
    matrix = np.zeros((CHUNK * PIECES, SRC), np.float32)
    for t in range(CHUNK):
        for k, (kind, value) in enumerate(uses):
            matrix[t * PIECES + k, kind * CHUNK + (0 if kind == one else t)] = value
    return matrix.astype(ml_dtypes.bfloat16)


def split(value, count):
    pieces = []
    for _ in range(count):
        piece = value.astype(BF16).astype(jnp.float32)
        value = value - piece
        pieces.append(piece)
    return pieces, value


def one_hot(row_ids, names):
    return jnp.where(row_ids == jnp.broadcast_to(names, row_ids.shape), 1.0, 0.0).astype(BF16)


def placed(chosen, data):
    high = data.astype(BF16)
    low = (data - high.astype(jnp.float32)).astype(BF16)
    found = jnp.dot(chosen, jnp.concatenate([high, low], axis=1), preferred_element_type=jnp.float32)
    return found[:, :LANES] + found[:, LANES:]


def place_kernel(cell_ref, own_ref, chosen_ref, base_ref, rows_ref):
    rows = chosen_ref.shape[0]
    count = cell_ref.shape[1]
    cell = cell_ref[...].astype(jnp.float32)
    column = jnp.transpose(jnp.broadcast_to(cell, (LANES, count)))
    lane = lax.broadcasted_iota(jnp.int32, (count, LANES), 1)
    counts = []
    for n in range(2):
        name = jnp.where((lane >= COUNT_AT) & (lane < COUNT_AT + HALF), lane - COUNT_AT + n * HALF, -1)
        named = jnp.where(column == name.astype(jnp.float32), 1.0, 0.0)
        counts.append(jnp.sum(named, axis=0, keepdims=True))
    column = jnp.concatenate([column] * (count // LANES), axis=1)
    before = lax.broadcasted_iota(jnp.int32, (count, count), 0) < lax.broadcasted_iota(jnp.int32, (count, count), 1)
    same = (column == jnp.broadcast_to(cell, (count, count))) & before
    rank = jnp.sum(jnp.where(same, 1.0, 0.0), axis=0, keepdims=True)
    early = jnp.where(rank < PACK, cell * PACK + rank, -1.0).astype(jnp.int32)
    late = jnp.where(rank < PACK, -1.0, cell * PACK + rank - PACK).astype(jnp.int32)
    ids = lax.broadcasted_iota(jnp.int32, (rows, count), 0)
    early = one_hot(ids, early)
    chosen_ref[:, 0:count] = early
    chosen_ref[:, count : 2 * count] = one_hot(ids, jnp.where(late < 0, -1, late + LATE))
    rows_ref[...] = jnp.zeros_like(rows_ref)
    rows_ref[0:FLAG_AT, :] = own_ref[:, 0, :]
    rows_ref[FLAG_AT : FLAG_AT + 1, :] = jnp.ones((1, count), jnp.float32)
    data = jnp.transpose(rows_ref[...])
    data = jnp.concatenate([data, jnp.where(lane >= RECORD, pltpu.roll(data, RECORD, 1), 0.0)], axis=0)
    found = placed(jnp.concatenate([early, one_hot(ids, late)], axis=1), data)
    row = lax.rem(lax.broadcasted_iota(jnp.int32, found.shape, 0), PACK)
    held = jnp.where(lax.rem(row, 2) == 0, counts[0], counts[1])
    base_ref[...] = found + jnp.where(row >= LATE, held, 0.0)


def front_kernel(first_ref, own_ref, prev_ref, chosen_ref, base_ref, table_ref, out_ref, rows_ref):
    first = first_ref[0] == 0
    rows_ref[...] = jnp.zeros_like(rows_ref)
    table = jnp.where(first, table_ref[0], table_ref[1])
    for c in range(3):
        rows = slice(c * DEG1, (c + 1) * DEG1)
        source = jnp.where(first, own_ref[rows, 0, :], prev_ref[rows, 0, :])
        rows_ref[RIM_AT + RIM * c : RIM_AT + RIM * (c + 1), :] = jnp.dot(
            table, source, precision=lax.Precision.HIGHEST, preferred_element_type=jnp.float32
        )
    data = jnp.transpose(rows_ref[...])
    data = jnp.concatenate([data, pltpu.roll(data, RECORD - RIM_AT, 1)], axis=0)
    out_ref[...] = placed(chosen_ref[...], data) + base_ref[...]


def plan(counts):
    rows = jnp.maximum(jnp.ceil(counts / ROWS), 1.0) * ROWS
    tiles = jnp.maximum(jnp.ceil(counts / COLS), 1.0)
    fixed, per_row, extra, least = 0.0278, 1.244e-3, 0.26, 0.12
    alone = 0.0005 * tiles + 1.346e-3 * (
        jnp.minimum(rows, COLS)
        + jnp.where(tiles > 1.5, jnp.minimum(rows, 2 * COLS), 0.0)
        + jnp.where(tiles > 2.5, rows, 0.0)
    )
    after = lambda value: pltpu.roll(value, LANES - 1, 1)
    ahead = lambda value: pltpu.roll(value, 1, 1)
    here = after(tiles) * (fixed + per_row * rows) + extra
    there = tiles * (fixed + per_row * after(rows)) + extra
    lent = 0.92 * alone + tiles * fixed + 0.38
    cross_step, self_step = 0.5 / (here + there), 0.1 / alone
    share, before, behind = jnp.full_like(counts, 0.5), jnp.zeros_like(counts), jnp.zeros_like(counts)
    for _ in range(8):
        load = (
            alone * (1.0 - before - behind)
            + share * here
            + ahead((1.0 - share) * there + behind * lent)
            + after(before * lent)
        )
        up, down = after(load) - load, load - ahead(load)
        share = jnp.clip(share + cross_step * up, 0.0, 1.0)
        before = jnp.clip(before + self_step * (down - least), 0.0, 0.45)
        behind = jnp.clip(behind - self_step * (up + least), 0.0, 0.45)
    return [jnp.floor(value * UNITS + 0.5) for value in (share, before, behind)]


def records(packed):
    tiles = packed.reshape(packed.shape[0] // PACK, 2, LATE, LANES)
    blocks = tiles.shape[0]
    flat = (blocks * LATE, LANES)
    low, high = tiles[:, 0].reshape(flat), tiles[:, 1].reshape(flat)
    lane = lax.broadcasted_iota(jnp.int32, flat, 1)
    late = jnp.where(
        lane < RIM_AT,
        pltpu.roll(low, LANES - RECORD, 1),
        jnp.where(lane < RECORD, pltpu.roll(high, LANES - (RECORD - RIM_AT), 1), 0.0),
    )
    each = [v.reshape(blocks, 1, LATE, LANES) for v in (low, high, late)]
    return jnp.concatenate(each, axis=1).reshape(blocks * CAP, LANES), high


def cell_counts(high):
    row = lax.rem(lax.broadcasted_iota(jnp.int32, high.shape, 0), 2)
    lane = lax.broadcasted_iota(jnp.int32, high.shape, 1)
    held = jnp.where((lane >= COUNT_AT) & (lane < COUNT_AT + HALF), high, 0.0)
    total = None
    for n in range(2):
        part = jnp.sum(jnp.where(row == n, held, 0.0), axis=0, keepdims=True) * (2.0 / LATE)
        part = pltpu.roll(part, (n * HALF - COUNT_AT) % LANES, 1)
        total = part if total is None else total + part
    total = total + pltpu.roll(total, 2 * HALF, 1)
    return total + pltpu.roll(total, 4 * HALF, 1)


def compact_kernel(packed_ref, live_ref, chosen_ref, count_ref):
    data, high = records(packed_ref[...])
    slots = data.shape[0]
    flag = jnp.transpose(data)[FLAG_AT : FLAG_AT + 1, :]
    first = lax.broadcasted_iota(jnp.int32, (slots, slots), 0)
    second = lax.broadcasted_iota(jnp.int32, (slots, slots), 1)
    before = jnp.where(first < second, 1.0, 0.0).astype(BF16)
    flags = jnp.broadcast_to(flag, (16, slots)).astype(BF16)
    place = jnp.dot(flags, before, preferred_element_type=jnp.float32)[0:1]
    place = jnp.where(flag > 0.5, place, -1.0).astype(jnp.int32)
    chosen = one_hot(first, place)
    chosen_ref[...] = chosen
    live_ref[...] = placed(chosen, data)
    count_ref[...] = cell_counts(high)


def fetched(sources, targets, sem):
    copies = [pltpu.make_async_copy(s, t, sem.at[i]) for i, (s, t) in enumerate(zip(sources, targets))]
    for copy in copies:
        copy.start()
    return copies


def tracks(live_ref, synth_ref, track_ref, flag_ref, copies):
    live = jnp.transpose(live_ref[...])
    flag_ref[...] = jnp.broadcast_to(live[FLAG_AT : FLAG_AT + 1, :], flag_ref.shape)
    for copy in copies:
        copy.wait()
    (high, low), _ = split(live[:TERMS], 2)
    rest = jnp.zeros((2 * LANES - 3 * TERMS, live.shape[1]), jnp.float32)
    terms = jnp.concatenate([high, low, high, rest], axis=0).astype(BF16)
    track = jnp.dot(synth_ref[...], terms, preferred_element_type=jnp.float32)
    track_ref[...] = track.reshape(track_ref.shape)


def source_of(track_ref, flag_ref, unit):
    count = track_ref.shape[3]
    parts, norm = [], None
    for c in range(3):
        axis = track_ref[c, unit]
        pieces, rest = split(axis, PARTS)
        parts.append(pieces)
        held = axis - rest
        norm = held * held if norm is None else norm + held * held
    norm = jnp.where(flag_ref[...] > 0.5, 0.5 * norm, FAR)
    kinds = [parts[c][i] for i in range(PARTS) for c in range(3)] + split(norm, NORMS)[0]
    ones = jnp.ones((CHUNK, count), jnp.float32)
    return jnp.concatenate(kinds + [ones], axis=0)


def put_right(source, right_sel_ref, right_ref, unit):
    right = jnp.dot(right_sel_ref[...], source.astype(BF16), preferred_element_type=jnp.float32)
    right_ref[pl.ds(unit * CHUNK, CHUNK)] = right.astype(BF16).reshape(CHUNK, PIECES, right.shape[1])


def put_left(source, left_sel_ref, left_ref, unit, offset):
    left = jnp.dot(jnp.transpose(source).astype(BF16), left_sel_ref[...], preferred_element_type=jnp.float32)
    left = left.astype(BF16)
    for g in range(CHUNK // GROUP):
        left_ref[offset + unit * (CHUNK // GROUP) + g] = left[:, g * LANES : (g + 1) * LANES]


def sweep(left_ref, right_ref, acc_ref, row_ref, col_ref, job, row_tiles, col_start, first, last, diagonal):
    groups = CHUNK // GROUP
    offset = job * (EXT // GROUP)
    columns = pl.ds(col_start, COLS)

    def screen(rows, unit, units):
        best = acc_ref[0:rows, :]
        for h in range(units * groups):
            g = unit * groups + h
            left = left_ref[offset + g, 0:rows, :]
            for j in range(GROUP):
                parts = [right_ref[g * GROUP + j, :, columns]]
                if j > 0:
                    parts = [jnp.zeros((PIECES * j, COLS), BF16)] + parts
                if j < GROUP - 1:
                    parts = parts + [jnp.zeros((PIECES * (GROUP - 1 - j), COLS), BF16)]
                weights = jnp.concatenate(parts, axis=0)
                best = jnp.minimum(best, jnp.dot(left, weights, preferred_element_type=jnp.float32))
        acc_ref[0:rows, :] = best

    for n in range(1, acc_ref.shape[0] // ROWS + 1):

        @pl.when(row_tiles == n)
        def _(rows=n * ROWS, each=2):
            acc_ref[0:rows, :] = jnp.full((rows, COLS), CLIP, jnp.float32)
            steps = (last - first) // each

            def step(i, carry):
                screen(rows, first + i * each, each)
                return carry

            lax.fori_loop(0, steps, step, 0)
            if each > 1:

                @pl.when(first + steps * each < last)
                def _():
                    screen(rows, last - 1, 1)

            @pl.when(diagonal)
            def _():
                same = lax.broadcasted_iota(jnp.int32, (COLS, COLS), 0) == lax.broadcasted_iota(
                    jnp.int32, (COLS, COLS), 1
                )
                near = pl.ds(col_start, COLS)
                acc_ref[near, :] = jnp.where(same, CLIP, acc_ref[near, :])

            acc = acc_ref[0:rows, :]
            half = jnp.minimum(acc[:, :LANES], acc[:, LANES:])
            row_ref[job, 0:rows, :] = jnp.minimum(row_ref[job, 0:rows, :], half)
            best = finished(jnp.min(acc, axis=0, keepdims=True))
            col_ref[:, columns] = jnp.minimum(col_ref[:, columns], best)


def by_row(row_ref, job):
    return finished(jnp.min(jnp.transpose(row_ref[job]), axis=0, keepdims=True))


def finished(half):
    return jnp.clip(2.0 * half, 0.0, CLIP)


def planned(plan_ref, row, cell, cells):
    lane = lax.broadcasted_iota(jnp.int32, (1, LANES), 1)
    value = jnp.sum(jnp.where(lane == lax.rem(cell, cells), plan_ref[row : row + 1, :], 0.0))
    return value.astype(jnp.int32)


def tiles_of(count, size):
    return jnp.maximum((count + (size - 1)) // size, 1)


def self_kernel(
    cells, cell_ref, live_ref, count_ref, synth_hbm, left_sel_hbm, right_sel_hbm, out_ref, left_ref, plan_ref,
    right_ref, acc_ref, row_ref, col_ref, synth_ref, left_sel_ref, right_sel_ref, track_ref, flag_ref, sem,
):
    copies = fetched((synth_hbm, left_sel_hbm, right_sel_hbm), (synth_ref, left_sel_ref, right_sel_ref), sem)
    tracks(live_ref, synth_ref, track_ref, flag_ref, copies)
    counts = count_ref[...]
    plan_ref[0:1, :] = counts
    for n, units in enumerate(plan(counts)):
        plan_ref[n + 1 : n + 2, :] = units
    for unit in range(UNITS):
        source = source_of(track_ref, flag_ref, unit)
        put_right(source, right_sel_ref, right_ref, unit)
        put_left(source, left_sel_ref, left_ref, unit, 0)
    cell = cell_ref[0]
    count = planned(plan_ref, 0, cell, cells)
    first, last = planned(plan_ref, 2, cell, cells), UNITS - planned(plan_ref, 3, cell, cells)
    row_tiles = tiles_of(count, ROWS)
    row_ref[...] = jnp.full_like(row_ref, CLIP)
    col_ref[...] = jnp.full_like(col_ref, CLIP)

    def column(n, carry):
        start = pl.multiple_of(n * COLS, COLS)
        limit = jnp.minimum(row_tiles, (n + 1) * (COLS // ROWS))
        sweep(left_ref, right_ref, acc_ref, row_ref, col_ref, 0, limit, start, first, last, n >= 0)
        return carry

    lax.fori_loop(0, tiles_of(count, COLS), column, 0)
    out_ref[...] = jnp.minimum(by_row(row_ref, 0), col_ref[...])


def neighbour_kernel(
    cells, cell_ref, plan_ref, next_ref, prev_ref, base_ref, left_in_ref, synth_hbm, left_sel_hbm, right_sel_hbm,
    out_ref, next_out_ref, prev_out_ref, left_ref,
    right_ref, acc_ref, row_ref, col_ref, synth_ref, left_sel_ref, right_sel_ref, track_ref, flag_ref, sem,
):
    del left_in_ref
    copies = fetched((synth_hbm, left_sel_hbm, right_sel_hbm), (synth_ref, left_sel_ref, right_sel_ref), sem)
    cell = cell_ref[0]
    after, ahead = cell + 1, cell + (cells - 1)
    own_rows = tiles_of(planned(plan_ref, 0, cell, cells), ROWS)
    own_share, their_share = planned(plan_ref, 1, cell, cells), planned(plan_ref, 1, ahead, cells)
    of_next, of_prev = planned(plan_ref, 2, after, cells), planned(plan_ref, 3, ahead, cells)
    next_count, prev_count = planned(plan_ref, 0, after, cells), planned(plan_ref, 0, ahead, cells)
    offset = left_ref.shape[0] // 2
    for copy in copies:
        copy.wait()
    row_ref[0] = jnp.full(row_ref.shape[1:], CLIP, jnp.float32)

    def phase(p, carry):
        forward = p == 0
        cross = jnp.where(forward, 0, their_share), jnp.where(forward, own_share, UNITS)
        alone = jnp.where(forward, 0, UNITS - of_prev), jnp.where(forward, of_next, UNITS)
        cross_on, alone_on = cross[0] < cross[1], alone[0] < alone[1]
        first = jnp.minimum(cross[0], alone[0])
        last = jnp.maximum(cross[1], alone[1])
        count = jnp.where(forward, next_count, prev_count)
        other_rows, other_cols = tiles_of(count, ROWS), tiles_of(count, COLS)

        @pl.when(forward & (first < last))
        def _():
            tracks(next_ref, synth_ref, track_ref, flag_ref, ())

        @pl.when((p == 1) & (first < last))
        def _():
            tracks(prev_ref, synth_ref, track_ref, flag_ref, ())

        def right_step(i, c):
            for u in range(2):
                unit = jnp.minimum(first + 2 * i + u, UNITS - 1)
                put_right(source_of(track_ref, flag_ref, unit), right_sel_ref, right_ref, unit)
            return c

        def left_step(unit, c):
            put_left(source_of(track_ref, flag_ref, unit), left_sel_ref, left_ref, unit, offset)
            return c

        lax.fori_loop(0, (last - first + 1) // 2, right_step, 0)
        lax.fori_loop(alone[0], alone[1], left_step, 0)
        row_ref[1] = jnp.full(row_ref.shape[1:], CLIP, jnp.float32)
        col_ref[...] = jnp.full_like(col_ref, CLIP)

        def column(k, c):
            job = jnp.where(k < other_cols, 0, 1)
            n = k - job * other_cols
            start = pl.multiple_of(n * COLS, COLS)
            limit = jnp.where(job == 0, own_rows, jnp.minimum(other_rows, (n + 1) * (COLS // ROWS)))
            low, high = jnp.where(job == 0, cross[0], alone[0]), jnp.where(job == 0, cross[1], alone[1])
            sweep(left_ref, right_ref, acc_ref, row_ref, col_ref, job, limit, start, low, high, job == 1)
            return c

        lax.fori_loop(
            jnp.where(cross_on, 0, other_cols), jnp.where(alone_on, 2 * other_cols, other_cols), column, 0
        )
        best = jnp.minimum(col_ref[...], by_row(row_ref, 1))

        @pl.when(forward)
        def _():
            next_out_ref[...] = best

        @pl.when(p == 1)
        def _():
            prev_out_ref[...] = best

        return carry

    lax.fori_loop(0, 2, phase, 0)
    out_ref[...] = jnp.minimum(by_row(row_ref, 0), base_ref[...])


def restore_kernel(*refs):
    *minima, chosen_ref, out_ref = refs
    count = out_ref.shape[1]
    best = functools.reduce(jnp.minimum, [ref[...] for ref in minima])
    pieces = split(best, 3)[0]
    ones, zeros = jnp.ones((1, count), jnp.float32), jnp.zeros((12, count), jnp.float32)
    rows = jnp.concatenate(pieces + [ones, zeros], axis=0).astype(BF16)
    found = jnp.dot(rows, chosen_ref[...], preferred_element_type=jnp.float32)
    value = found[0:1] + found[1:2] + found[2:3]
    out_ref[...] = jnp.where(found[3:4] > 0.5, value, CLIP)


VMEM = pl.BlockSpec(memory_space=pltpu.VMEM)
SMEM = pl.BlockSpec(memory_space=pltpu.SMEM)
ANY = pl.BlockSpec(memory_space=pl.ANY)


def call(kernel, name, out_shape, in_specs, scratch, vmem, flops, aliases=None):
    return pl.pallas_call(
        kernel,
        out_shape=out_shape,
        in_specs=in_specs,
        out_specs=jax.tree.map(lambda _: VMEM, out_shape),
        scratch_shapes=scratch,
        compiler_params=pltpu.CompilerParams(vmem_limit_bytes=vmem << 20),
        cost_estimate=pl.CostEstimate(flops=flops, bytes_accessed=4_000_000, transcendentals=0),
        input_output_aliases=aliases or {},
        name=name,
    )


def body(cheb_coef, obj_cell):
    objects = cheb_coef.shape[3]
    own = cheb_coef.reshape(3 * DEG1, 1, objects)
    cells = lax.axis_size("cell")
    slots = cells * CAP
    windows = lax.axis_size("tm")
    window = lax.axis_index("tm").astype(jnp.int32).reshape(1)
    prev = lax.ppermute(own, "tm", [(i, i + 1) for i in range(windows - 1)])
    row = jax.ShapeDtypeStruct((1, slots), jnp.float32)
    cell = lax.axis_index("cell").astype(jnp.int32).reshape(1)
    wide = jax.ShapeDtypeStruct((slots, LANES), jnp.float32)
    packed_shape = jax.ShapeDtypeStruct((cells * PACK, LANES), jnp.float32)
    rows_scratch = [pltpu.VMEM((LANES, objects), jnp.float32)]
    chosen, base = call(
        place_kernel,
        "place",
        (jax.ShapeDtypeStruct((cells * PACK, 2 * objects), BF16), packed_shape),
        [VMEM, VMEM],
        rows_scratch,
        12,
        2_000_000_000,
    )(obj_cell.reshape(1, objects), own)
    send = call(
        front_kernel, "front", packed_shape, [SMEM] + [VMEM] * 5, rows_scratch, 12, 2_000_000_000
    )(window, own, prev, chosen, base, jnp.asarray(rim_tables()))
    packed = lax.all_to_all(send, "cell", split_axis=0, concat_axis=0, tiled=True)
    live, chosen, counts = call(
        compact_kernel,
        "compact",
        (wide, jax.ShapeDtypeStruct((slots, slots), BF16), jax.ShapeDtypeStruct((1, LANES), jnp.float32)),
        [VMEM],
        [],
        16,
        2_000_000_000,
    )(packed)
    forward = [(i, (i + 1) % cells) for i in range(cells)]
    backward = [((i + 1) % cells, i) for i in range(cells)]
    next_live = lax.ppermute(live, "cell", backward)
    prev_live = lax.ppermute(live, "cell", forward)
    synth = jnp.asarray(synth_matrix())
    left_sel = jnp.asarray(np.ascontiguousarray(selection(True).T))
    right_sel = jnp.asarray(selection(False))
    left_shape = jax.ShapeDtypeStruct((2 * (EXT // GROUP), slots, LANES), BF16)
    scratch = [
        pltpu.VMEM((EXT, PIECES, slots), BF16),
        pltpu.VMEM((slots, COLS), jnp.float32),
        pltpu.VMEM((2, slots, LANES), jnp.float32),
        pltpu.VMEM((1, slots), jnp.float32),
        pltpu.VMEM(synth.shape, BF16),
        pltpu.VMEM(left_sel.shape, BF16),
        pltpu.VMEM(right_sel.shape, BF16),
        pltpu.VMEM((3, UNITS, CHUNK, slots), jnp.float32),
        pltpu.VMEM((CHUNK, slots), jnp.float32),
        pltpu.SemaphoreType.DMA((3,)),
    ]
    own_min, left, shares = call(
        functools.partial(self_kernel, cells),
        "self_screen",
        (row, left_shape, jax.ShapeDtypeStruct((8, LANES), jnp.float32)),
        [SMEM, VMEM, VMEM, ANY, ANY, ANY],
        scratch,
        40,
        15_000_000_000,
    )(cell, live, counts, synth, left_sel, right_sel)
    best, next_min, prev_min, _ = call(
        functools.partial(neighbour_kernel, cells),
        "neighbour_screen",
        (row, row, row, left_shape),
        [SMEM] + [VMEM] * 5 + [ANY] * 3,
        scratch,
        40,
        20_000_000_000,
        {5: 3},
    )(cell, shares, next_live, prev_live, own_min, left, synth, left_sel, right_sel)
    from_prev = lax.ppermute(next_min, "cell", forward)
    from_next = lax.ppermute(prev_min, "cell", backward)
    return call(restore_kernel, "restore", row, [VMEM] * 4, [], 8, 100_000_000)(best, from_prev, from_next, chosen)


def solution(mesh):
    in_specs = (P("tm", None, None, "cell"), P("tm", "cell", None))
    return jax.shard_map(body, mesh=mesh, in_specs=in_specs, out_specs=P("tm", "cell"), check_vma=False)
```

```python
import functools

import jax
import jax.numpy as jnp
import ml_dtypes
import numpy as np
from jax import lax
from jax.experimental import pallas as pl
from jax.experimental.pallas import tpu as pltpu
from jax.sharding import PartitionSpec as P

DEG1 = 17
SAMP = 64
RIM = 8
CAP = 24
EXT = SAMP + RIM
CLIP = 25.0
FAR = 1.0e9

LANES = 128
FLAG_AT = 3 * DEG1
RIM_AT = FLAG_AT + 1
RECORD = RIM_AT + 3 * RIM
PACK = 16
LATE = CAP - PACK
COUNT_AT = RECORD + 3 * RIM
HALF = 16

PIECES = 32
GROUP = LANES // PIECES
CHUNK = 8
UNITS = EXT // CHUNK
PARTS = 2
NORMS = 3
KINDS = 3 * PARTS + NORMS
SRC = 80
TERMS = 80
ROWS = 128
COLS = 256
BF16 = jnp.bfloat16


def cheb_table():
    nodes = ((2.0 * np.arange(SAMP, dtype=np.float32) + 1.0) / SAMP - 1.0).astype(np.float32)
    columns = [np.ones_like(nodes), nodes]
    for _ in range(2, DEG1):
        columns.append((2.0 * nodes * columns[-1] - columns[-2]).astype(np.float32))
    return np.stack(columns, axis=1)


def rim_tables():
    table = cheb_table()
    return np.stack([table[:RIM], table[SAMP - RIM :]])


def synth_matrix():
    table = cheb_table()
    weights = np.zeros((3 * EXT, LANES), np.float32)
    for c in range(3):
        for s in range(RIM):
            weights[c * EXT + s, RIM_AT + RIM * c + s] = 1.0
        weights[c * EXT + RIM : (c + 1) * EXT, DEG1 * c : DEG1 * (c + 1)] = table
    high = weights[:, :TERMS].astype(ml_dtypes.bfloat16)
    low = (weights[:, :TERMS] - high.astype(np.float32)).astype(ml_dtypes.bfloat16)
    return np.concatenate([high, high, low, np.zeros((3 * EXT, 2 * LANES - 3 * TERMS), high.dtype)], axis=1)


def selection(left):
    one = KINDS
    uses = []
    for i in range(PARTS):
        for j in range(PARTS):
            for c in range(3):
                uses.append((3 * i + c, 1.0) if left else (3 * j + c, -1.0))
    for n in range(NORMS):
        uses.append((3 * PARTS + n, 1.0) if left else (one, 1.0))
    for n in range(NORMS):
        uses.append((one, 1.0) if left else (3 * PARTS + n, 1.0))
    matrix = np.zeros((CHUNK * PIECES, SRC), np.float32)
    for t in range(CHUNK):
        for k, (kind, value) in enumerate(uses):
            matrix[t * PIECES + k, kind * CHUNK + (0 if kind == one else t)] = value
    return matrix.astype(ml_dtypes.bfloat16)


def split(value, count):
    pieces = []
    for _ in range(count):
        piece = value.astype(BF16).astype(jnp.float32)
        value = value - piece
        pieces.append(piece)
    return pieces, value


def one_hot(row_ids, names):
    return jnp.where(row_ids == jnp.broadcast_to(names, row_ids.shape), 1.0, 0.0).astype(BF16)


def placed(chosen, data):
    high = data.astype(BF16)
    low = (data - high.astype(jnp.float32)).astype(BF16)
    found = jnp.dot(chosen, jnp.concatenate([high, low], axis=1), preferred_element_type=jnp.float32)
    return found[:, :LANES] + found[:, LANES:]


def place_kernel(cell_ref, own_ref, chosen_ref, base_ref, rows_ref):
    rows = chosen_ref.shape[0]
    count = cell_ref.shape[1]
    cell = cell_ref[...].astype(jnp.float32)
    column = jnp.transpose(jnp.broadcast_to(cell, (LANES, count)))
    lane = lax.broadcasted_iota(jnp.int32, (count, LANES), 1)
    counts = []
    for n in range(2):
        name = jnp.where((lane >= COUNT_AT) & (lane < COUNT_AT + HALF), lane - COUNT_AT + n * HALF, -1)
        named = jnp.where(column == name.astype(jnp.float32), 1.0, 0.0)
        counts.append(jnp.sum(named, axis=0, keepdims=True))
    column = jnp.concatenate([column] * (count // LANES), axis=1)
    before = lax.broadcasted_iota(jnp.int32, (count, count), 0) < lax.broadcasted_iota(jnp.int32, (count, count), 1)
    same = (column == jnp.broadcast_to(cell, (count, count))) & before
    rank = jnp.sum(jnp.where(same, 1.0, 0.0), axis=0, keepdims=True)
    early = jnp.where(rank < PACK, cell * PACK + rank, -1.0).astype(jnp.int32)
    late = jnp.where(rank < PACK, -1.0, cell * PACK + rank - PACK).astype(jnp.int32)
    ids = lax.broadcasted_iota(jnp.int32, (rows, count), 0)
    early = one_hot(ids, early)
    chosen_ref[:, 0:count] = early
    chosen_ref[:, count : 2 * count] = one_hot(ids, jnp.where(late < 0, -1, late + LATE))
    rows_ref[...] = jnp.zeros_like(rows_ref)
    rows_ref[0:FLAG_AT, :] = own_ref[:, 0, :]
    rows_ref[FLAG_AT : FLAG_AT + 1, :] = jnp.ones((1, count), jnp.float32)
    data = jnp.transpose(rows_ref[...])
    data = jnp.concatenate([data, jnp.where(lane >= RECORD, pltpu.roll(data, RECORD, 1), 0.0)], axis=0)
    found = placed(jnp.concatenate([early, one_hot(ids, late)], axis=1), data)
    row = lax.rem(lax.broadcasted_iota(jnp.int32, found.shape, 0), PACK)
    held = jnp.where(lax.rem(row, 2) == 0, counts[0], counts[1])
    base_ref[...] = found + jnp.where(row >= LATE, held, 0.0)


def front_kernel(first_ref, own_ref, prev_ref, chosen_ref, base_ref, table_ref, out_ref, rows_ref):
    first = first_ref[0] == 0
    rows_ref[...] = jnp.zeros_like(rows_ref)
    table = jnp.where(first, table_ref[0], table_ref[1])
    for c in range(3):
        rows = slice(c * DEG1, (c + 1) * DEG1)
        source = jnp.where(first, own_ref[rows, 0, :], prev_ref[rows, 0, :])
        rows_ref[RIM_AT + RIM * c : RIM_AT + RIM * (c + 1), :] = jnp.dot(
            table, source, precision=lax.Precision.HIGHEST, preferred_element_type=jnp.float32
        )
    data = jnp.transpose(rows_ref[...])
    data = jnp.concatenate([data, pltpu.roll(data, RECORD - RIM_AT, 1)], axis=0)
    out_ref[...] = placed(chosen_ref[...], data) + base_ref[...]


def plan(counts):
    rows = jnp.maximum(jnp.ceil(counts / ROWS), 1.0) * ROWS
    tiles = jnp.maximum(jnp.ceil(counts / COLS), 1.0)
    fixed, per_row, extra, least = 0.0278, 1.244e-3, 0.26, 0.12
    alone = 0.0005 * tiles + 1.346e-3 * (
        jnp.minimum(rows, COLS)
        + jnp.where(tiles > 1.5, jnp.minimum(rows, 2 * COLS), 0.0)
        + jnp.where(tiles > 2.5, rows, 0.0)
    )
    after = lambda value: pltpu.roll(value, LANES - 1, 1)
    ahead = lambda value: pltpu.roll(value, 1, 1)
    here = after(tiles) * (fixed + per_row * rows) + extra
    there = tiles * (fixed + per_row * after(rows)) + extra
    lent = 0.92 * alone + tiles * fixed + 0.38
    cross_step, self_step = 0.5 / (here + there), 0.1 / alone
    share, before, behind = jnp.full_like(counts, 0.5), jnp.zeros_like(counts), jnp.zeros_like(counts)
    for _ in range(8):
        load = (
            alone * (1.0 - before - behind)
            + share * here
            + ahead((1.0 - share) * there + behind * lent)
            + after(before * lent)
        )
        up, down = after(load) - load, load - ahead(load)
        share = jnp.clip(share + cross_step * up, 0.0, 1.0)
        before = jnp.clip(before + self_step * (down - least), 0.0, 0.45)
        behind = jnp.clip(behind - self_step * (up + least), 0.0, 0.45)
    return [jnp.floor(value * UNITS + 0.5) for value in (share, before, behind)]


def records(packed):
    tiles = packed.reshape(packed.shape[0] // PACK, 2, LATE, LANES)
    blocks = tiles.shape[0]
    flat = (blocks * LATE, LANES)
    low, high = tiles[:, 0].reshape(flat), tiles[:, 1].reshape(flat)
    lane = lax.broadcasted_iota(jnp.int32, flat, 1)
    late = jnp.where(
        lane < RIM_AT,
        pltpu.roll(low, LANES - RECORD, 1),
        jnp.where(lane < RECORD, pltpu.roll(high, LANES - (RECORD - RIM_AT), 1), 0.0),
    )
    each = [v.reshape(blocks, 1, LATE, LANES) for v in (low, high, late)]
    return jnp.concatenate(each, axis=1).reshape(blocks * CAP, LANES), high


def cell_counts(high):
    row = lax.rem(lax.broadcasted_iota(jnp.int32, high.shape, 0), 2)
    lane = lax.broadcasted_iota(jnp.int32, high.shape, 1)
    held = jnp.where((lane >= COUNT_AT) & (lane < COUNT_AT + HALF), high, 0.0)
    total = None
    for n in range(2):
        part = jnp.sum(jnp.where(row == n, held, 0.0), axis=0, keepdims=True) * (2.0 / LATE)
        part = pltpu.roll(part, (n * HALF - COUNT_AT) % LANES, 1)
        total = part if total is None else total + part
    total = total + pltpu.roll(total, 2 * HALF, 1)
    return total + pltpu.roll(total, 4 * HALF, 1)


def compact_kernel(packed_ref, live_ref, chosen_ref, count_ref):
    data, high = records(packed_ref[...])
    slots = data.shape[0]
    flag = jnp.transpose(data)[FLAG_AT : FLAG_AT + 1, :]
    first = lax.broadcasted_iota(jnp.int32, (slots, slots), 0)
    second = lax.broadcasted_iota(jnp.int32, (slots, slots), 1)
    before = jnp.where(first < second, 1.0, 0.0).astype(BF16)
    flags = jnp.broadcast_to(flag, (16, slots)).astype(BF16)
    place = jnp.dot(flags, before, preferred_element_type=jnp.float32)[0:1]
    place = jnp.where(flag > 0.5, place, -1.0).astype(jnp.int32)
    chosen = one_hot(first, place)
    chosen_ref[...] = chosen
    live_ref[...] = placed(chosen, data)
    count_ref[...] = cell_counts(high)


def fetched(sources, targets, sem):
    copies = [pltpu.make_async_copy(s, t, sem.at[i]) for i, (s, t) in enumerate(zip(sources, targets))]
    for copy in copies:
        copy.start()
    return copies


def tracks(live_ref, synth_ref, track_ref, flag_ref, copies):
    live = jnp.transpose(live_ref[...])
    flag_ref[...] = jnp.broadcast_to(live[FLAG_AT : FLAG_AT + 1, :], flag_ref.shape)
    for copy in copies:
        copy.wait()
    (high, low), _ = split(live[:TERMS], 2)
    rest = jnp.zeros((2 * LANES - 3 * TERMS, live.shape[1]), jnp.float32)
    terms = jnp.concatenate([high, low, high, rest], axis=0).astype(BF16)
    track = jnp.dot(synth_ref[...], terms, preferred_element_type=jnp.float32)
    track_ref[...] = track.reshape(track_ref.shape)


def source_of(track_ref, flag_ref, unit):
    count = track_ref.shape[3]
    parts, norm = [], None
    for c in range(3):
        axis = track_ref[c, unit]
        pieces, rest = split(axis, PARTS)
        parts.append(pieces)
        held = axis - rest
        norm = held * held if norm is None else norm + held * held
    norm = jnp.where(flag_ref[...] > 0.5, 0.5 * norm, FAR)
    kinds = [parts[c][i] for i in range(PARTS) for c in range(3)] + split(norm, NORMS)[0]
    ones = jnp.ones((CHUNK, count), jnp.float32)
    return jnp.concatenate(kinds + [ones], axis=0)


def put_right(source, right_sel_ref, right_ref, unit):
    right = jnp.dot(right_sel_ref[...], source.astype(BF16), preferred_element_type=jnp.float32)
    right_ref[pl.ds(unit * CHUNK, CHUNK)] = right.astype(BF16).reshape(CHUNK, PIECES, right.shape[1])


def put_left(source, left_sel_ref, left_ref, unit, offset):
    left = jnp.dot(jnp.transpose(source).astype(BF16), left_sel_ref[...], preferred_element_type=jnp.float32)
    left = left.astype(BF16)
    for g in range(CHUNK // GROUP):
        left_ref[offset + unit * (CHUNK // GROUP) + g] = left[:, g * LANES : (g + 1) * LANES]


def sweep(left_ref, right_ref, acc_ref, row_ref, col_ref, job, row_tiles, col_start, first, last, diagonal):
    groups = CHUNK // GROUP
    offset = job * (EXT // GROUP)
    columns = pl.ds(col_start, COLS)

    def screen(rows, unit, units):
        best = acc_ref[0:rows, :]
        for h in range(units * groups):
            g = unit * groups + h
            left = left_ref[offset + g, 0:rows, :]
            for j in range(GROUP):
                parts = [right_ref[g * GROUP + j, :, columns]]
                if j > 0:
                    parts = [jnp.zeros((PIECES * j, COLS), BF16)] + parts
                if j < GROUP - 1:
                    parts = parts + [jnp.zeros((PIECES * (GROUP - 1 - j), COLS), BF16)]
                weights = jnp.concatenate(parts, axis=0)
                best = jnp.minimum(best, jnp.dot(left, weights, preferred_element_type=jnp.float32))
        acc_ref[0:rows, :] = best

    for n in range(1, acc_ref.shape[0] // ROWS + 1):

        @pl.when(row_tiles == n)
        def _(rows=n * ROWS, each=2):
            acc_ref[0:rows, :] = jnp.full((rows, COLS), CLIP, jnp.float32)
            steps = (last - first) // each

            def step(i, carry):
                screen(rows, first + i * each, each)
                return carry

            lax.fori_loop(0, steps, step, 0)
            if each > 1:

                @pl.when(first + steps * each < last)
                def _():
                    screen(rows, last - 1, 1)

            @pl.when(diagonal)
            def _():
                same = lax.broadcasted_iota(jnp.int32, (COLS, COLS), 0) == lax.broadcasted_iota(
                    jnp.int32, (COLS, COLS), 1
                )
                near = pl.ds(col_start, COLS)
                acc_ref[near, :] = jnp.where(same, CLIP, acc_ref[near, :])

            acc = acc_ref[0:rows, :]
            half = jnp.minimum(acc[:, :LANES], acc[:, LANES:])
            row_ref[job, 0:rows, :] = jnp.minimum(row_ref[job, 0:rows, :], half)
            best = finished(jnp.min(acc, axis=0, keepdims=True))
            col_ref[:, columns] = jnp.minimum(col_ref[:, columns], best)


def by_row(row_ref, job):
    return finished(jnp.min(jnp.transpose(row_ref[job]), axis=0, keepdims=True))


def finished(half):
    return jnp.clip(2.0 * half, 0.0, CLIP)


def planned(plan_ref, row, cell, cells):
    lane = lax.broadcasted_iota(jnp.int32, (1, LANES), 1)
    value = jnp.sum(jnp.where(lane == lax.rem(cell, cells), plan_ref[row : row + 1, :], 0.0))
    return value.astype(jnp.int32)


def tiles_of(count, size):
    return jnp.maximum((count + (size - 1)) // size, 1)


def self_kernel(
    cells, cell_ref, live_ref, count_ref, synth_hbm, left_sel_hbm, right_sel_hbm, out_ref, left_ref, plan_ref,
    right_ref, acc_ref, row_ref, col_ref, synth_ref, left_sel_ref, right_sel_ref, track_ref, flag_ref, sem,
):
    copies = fetched((synth_hbm, left_sel_hbm, right_sel_hbm), (synth_ref, left_sel_ref, right_sel_ref), sem)
    tracks(live_ref, synth_ref, track_ref, flag_ref, copies)
    counts = count_ref[...]
    plan_ref[0:1, :] = counts
    for n, units in enumerate(plan(counts)):
        plan_ref[n + 1 : n + 2, :] = units
    for unit in range(UNITS):
        source = source_of(track_ref, flag_ref, unit)
        put_right(source, right_sel_ref, right_ref, unit)
        put_left(source, left_sel_ref, left_ref, unit, 0)
    cell = cell_ref[0]
    count = planned(plan_ref, 0, cell, cells)
    first, last = planned(plan_ref, 2, cell, cells), UNITS - planned(plan_ref, 3, cell, cells)
    row_tiles = tiles_of(count, ROWS)
    row_ref[...] = jnp.full_like(row_ref, CLIP)
    col_ref[...] = jnp.full_like(col_ref, CLIP)

    def column(n, carry):
        start = pl.multiple_of(n * COLS, COLS)
        limit = jnp.minimum(row_tiles, (n + 1) * (COLS // ROWS))
        sweep(left_ref, right_ref, acc_ref, row_ref, col_ref, 0, limit, start, first, last, n >= 0)
        return carry

    lax.fori_loop(0, tiles_of(count, COLS), column, 0)
    out_ref[...] = jnp.minimum(by_row(row_ref, 0), col_ref[...])


def neighbour_kernel(
    cells, cell_ref, plan_ref, next_ref, prev_ref, base_ref, left_in_ref, synth_hbm, left_sel_hbm, right_sel_hbm,
    out_ref, next_out_ref, prev_out_ref, left_ref,
    right_ref, acc_ref, row_ref, col_ref, synth_ref, left_sel_ref, right_sel_ref, track_ref, flag_ref, sem,
):
    del left_in_ref
    copies = fetched((synth_hbm, left_sel_hbm, right_sel_hbm), (synth_ref, left_sel_ref, right_sel_ref), sem)
    cell = cell_ref[0]
    after, ahead = cell + 1, cell + (cells - 1)
    own_rows = tiles_of(planned(plan_ref, 0, cell, cells), ROWS)
    own_share, their_share = planned(plan_ref, 1, cell, cells), planned(plan_ref, 1, ahead, cells)
    of_next, of_prev = planned(plan_ref, 2, after, cells), planned(plan_ref, 3, ahead, cells)
    next_count, prev_count = planned(plan_ref, 0, after, cells), planned(plan_ref, 0, ahead, cells)
    offset = left_ref.shape[0] // 2
    for copy in copies:
        copy.wait()
    row_ref[0] = jnp.full(row_ref.shape[1:], CLIP, jnp.float32)

    def phase(p, carry):
        forward = p == 0
        cross = jnp.where(forward, 0, their_share), jnp.where(forward, own_share, UNITS)
        alone = jnp.where(forward, 0, UNITS - of_prev), jnp.where(forward, of_next, UNITS)
        cross_on, alone_on = cross[0] < cross[1], alone[0] < alone[1]
        first = jnp.minimum(cross[0], alone[0])
        last = jnp.maximum(cross[1], alone[1])
        count = jnp.where(forward, next_count, prev_count)
        other_rows, other_cols = tiles_of(count, ROWS), tiles_of(count, COLS)

        @pl.when(forward & (first < last))
        def _():
            tracks(next_ref, synth_ref, track_ref, flag_ref, ())

        @pl.when((p == 1) & (first < last))
        def _():
            tracks(prev_ref, synth_ref, track_ref, flag_ref, ())

        def right_step(i, c):
            for u in range(2):
                unit = jnp.minimum(first + 2 * i + u, UNITS - 1)
                put_right(source_of(track_ref, flag_ref, unit), right_sel_ref, right_ref, unit)
            return c

        def left_step(i, c):
            for u in range(2):
                unit = jnp.minimum(alone[0] + 2 * i + u, UNITS - 1)
                put_left(source_of(track_ref, flag_ref, unit), left_sel_ref, left_ref, unit, offset)
            return c

        lax.fori_loop(0, (last - first + 1) // 2, right_step, 0)
        lax.fori_loop(0, (alone[1] - alone[0] + 1) // 2, left_step, 0)
        row_ref[1] = jnp.full(row_ref.shape[1:], CLIP, jnp.float32)
        col_ref[...] = jnp.full_like(col_ref, CLIP)

        def column(k, c):
            job = jnp.where(k < other_cols, 0, 1)
            n = k - job * other_cols
            start = pl.multiple_of(n * COLS, COLS)
            limit = jnp.where(job == 0, own_rows, jnp.minimum(other_rows, (n + 1) * (COLS // ROWS)))
            low, high = jnp.where(job == 0, cross[0], alone[0]), jnp.where(job == 0, cross[1], alone[1])
            sweep(left_ref, right_ref, acc_ref, row_ref, col_ref, job, limit, start, low, high, job == 1)
            return c

        lax.fori_loop(
            jnp.where(cross_on, 0, other_cols), jnp.where(alone_on, 2 * other_cols, other_cols), column, 0
        )
        best = jnp.minimum(col_ref[...], by_row(row_ref, 1))

        @pl.when(forward)
        def _():
            next_out_ref[...] = best

        @pl.when(p == 1)
        def _():
            prev_out_ref[...] = best

        return carry

    lax.fori_loop(0, 2, phase, 0)
    out_ref[...] = jnp.minimum(by_row(row_ref, 0), base_ref[...])


def restore_kernel(*refs):
    *minima, chosen_ref, out_ref = refs
    count = out_ref.shape[1]
    best = functools.reduce(jnp.minimum, [ref[...] for ref in minima])
    pieces = split(best, 3)[0]
    ones, zeros = jnp.ones((1, count), jnp.float32), jnp.zeros((12, count), jnp.float32)
    rows = jnp.concatenate(pieces + [ones, zeros], axis=0).astype(BF16)
    found = jnp.dot(rows, chosen_ref[...], preferred_element_type=jnp.float32)
    value = found[0:1] + found[1:2] + found[2:3]
    out_ref[...] = jnp.where(found[3:4] > 0.5, value, CLIP)


VMEM = pl.BlockSpec(memory_space=pltpu.VMEM)
SMEM = pl.BlockSpec(memory_space=pltpu.SMEM)
ANY = pl.BlockSpec(memory_space=pl.ANY)


def call(kernel, name, out_shape, in_specs, scratch, vmem, flops, aliases=None):
    return pl.pallas_call(
        kernel,
        out_shape=out_shape,
        in_specs=in_specs,
        out_specs=jax.tree.map(lambda _: VMEM, out_shape),
        scratch_shapes=scratch,
        compiler_params=pltpu.CompilerParams(vmem_limit_bytes=vmem << 20),
        cost_estimate=pl.CostEstimate(flops=flops, bytes_accessed=4_000_000, transcendentals=0),
        input_output_aliases=aliases or {},
        name=name,
    )


def body(cheb_coef, obj_cell):
    objects = cheb_coef.shape[3]
    own = cheb_coef.reshape(3 * DEG1, 1, objects)
    cells = lax.axis_size("cell")
    slots = cells * CAP
    windows = lax.axis_size("tm")
    window = lax.axis_index("tm").astype(jnp.int32).reshape(1)
    prev = lax.ppermute(own, "tm", [(i, i + 1) for i in range(windows - 1)])
    row = jax.ShapeDtypeStruct((1, slots), jnp.float32)
    cell = lax.axis_index("cell").astype(jnp.int32).reshape(1)
    wide = jax.ShapeDtypeStruct((slots, LANES), jnp.float32)
    packed_shape = jax.ShapeDtypeStruct((cells * PACK, LANES), jnp.float32)
    rows_scratch = [pltpu.VMEM((LANES, objects), jnp.float32)]
    chosen, base = call(
        place_kernel,
        "place",
        (jax.ShapeDtypeStruct((cells * PACK, 2 * objects), BF16), packed_shape),
        [VMEM, VMEM],
        rows_scratch,
        12,
        2_000_000_000,
    )(obj_cell.reshape(1, objects), own)
    send = call(
        front_kernel, "front", packed_shape, [SMEM] + [VMEM] * 5, rows_scratch, 12, 2_000_000_000
    )(window, own, prev, chosen, base, jnp.asarray(rim_tables()))
    packed = lax.all_to_all(send, "cell", split_axis=0, concat_axis=0, tiled=True)
    live, chosen, counts = call(
        compact_kernel,
        "compact",
        (wide, jax.ShapeDtypeStruct((slots, slots), BF16), jax.ShapeDtypeStruct((1, LANES), jnp.float32)),
        [VMEM],
        [],
        16,
        2_000_000_000,
    )(packed)
    forward = [(i, (i + 1) % cells) for i in range(cells)]
    backward = [((i + 1) % cells, i) for i in range(cells)]
    next_live = lax.ppermute(live, "cell", backward)
    prev_live = lax.ppermute(live, "cell", forward)
    synth = jnp.asarray(synth_matrix())
    left_sel = jnp.asarray(np.ascontiguousarray(selection(True).T))
    right_sel = jnp.asarray(selection(False))
    left_shape = jax.ShapeDtypeStruct((2 * (EXT // GROUP), slots, LANES), BF16)
    scratch = [
        pltpu.VMEM((EXT, PIECES, slots), BF16),
        pltpu.VMEM((slots, COLS), jnp.float32),
        pltpu.VMEM((2, slots, LANES), jnp.float32),
        pltpu.VMEM((1, slots), jnp.float32),
        pltpu.VMEM(synth.shape, BF16),
        pltpu.VMEM(left_sel.shape, BF16),
        pltpu.VMEM(right_sel.shape, BF16),
        pltpu.VMEM((3, UNITS, CHUNK, slots), jnp.float32),
        pltpu.VMEM((CHUNK, slots), jnp.float32),
        pltpu.SemaphoreType.DMA((3,)),
    ]
    own_min, left, shares = call(
        functools.partial(self_kernel, cells),
        "self_screen",
        (row, left_shape, jax.ShapeDtypeStruct((8, LANES), jnp.float32)),
        [SMEM, VMEM, VMEM, ANY, ANY, ANY],
        scratch,
        40,
        15_000_000_000,
    )(cell, live, counts, synth, left_sel, right_sel)
    best, next_min, prev_min, _ = call(
        functools.partial(neighbour_kernel, cells),
        "neighbour_screen",
        (row, row, row, left_shape),
        [SMEM] + [VMEM] * 5 + [ANY] * 3,
        scratch,
        40,
        20_000_000_000,
        {5: 3},
    )(cell, shares, next_live, prev_live, own_min, left, synth, left_sel, right_sel)
    from_prev = lax.ppermute(next_min, "cell", forward)
    from_next = lax.ppermute(prev_min, "cell", backward)
    return call(restore_kernel, "restore", row, [VMEM] * 4, [], 8, 100_000_000)(best, from_prev, from_next, chosen)


def solution(mesh):
    in_specs = (P("tm", None, None, "cell"), P("tm", "cell", None))
    return jax.shard_map(body, mesh=mesh, in_specs=in_specs, out_specs=P("tm", "cell"), check_vma=False)
```
